32 devices in a mesh: seq: 8 (over y, x, core), expert: 4 (over z).
Axes of the slice: x: 2, y: 2, z: 4, core: 2. Of those that a mesh axis runs over, the one named last changes fastest.
Arguments:
- x_in: bfloat16 [1024, 4096], P('seq', 'expert'), may hold values from -6 to 6
- z_in: bfloat16 [1024, 4096], P('seq', 'expert'), may hold values from -6 to 6
- dt_raw: float32 [1024, 4096], P('seq', 'expert'), may hold values from -4 to 4
- bc_in: float32 [2, 16, 1024], P(None, None, 'seq'), may hold values from -6 to 6
- a_log: float32 [16, 4096], P(None, 'expert'), may hold values from -2 to 1.5
- conv_weight: float32 [4, 4096], P(None, 'expert'), may hold values from -3 to 3
- conv_bias: float32 [4096], P('expert'), may hold values from -3 to 3
- skip_gain: float32 [4096], P('expert'), may hold values from 0.25 to 1.75
- dt_bias: float32 [4096], P('expert'), may hold values from -6 to -1
- out_weight: bfloat16 [4096, 2048], P('expert'), may hold values from -0.09375 to 0.09375
- resid: bfloat16 [1024, 2048], P(('seq', 'expert')), may hold values from -6 to 6
- w_gate: bfloat16 [4, 2048, 7168], P('expert', None, 'seq'), may hold values from -0.125 to 0.125
- w_up: bfloat16 [4, 2048, 7168], P('expert', None, 'seq'), may hold values from -0.125 to 0.125
- w_down: bfloat16 [4, 7168, 2048], P('expert', 'seq'), may hold values from -0.0625 to 0.0625
- route_ids: int32 [1024, 2], P(('seq', 'expert')), may hold values from 0 to 3, all different within a row; in each aligned block of 32 rows (0 to 31, 32 to 63, ...) at most 32 rows name the same one
- route_weight: float32 [1024, 2], P(('seq', 'expert')), may hold values from 0.2 to 0.8
- grad_mix: bfloat16 [1024, 2048], P('seq'), may hold values from -6 to 6
Outputs:
- layer_out: bfloat16 [1024, 2048], P(('seq', 'expert'))
- grad_x: float32 [1024, 4096], P('seq', 'expert')
- grad_z: float32 [1024, 4096], P('seq', 'expert')
- grad_dt: float32 [1024, 4096], P('seq', 'expert')
- grad_bc: float32 [2, 16, 1024], P(None, None, 'seq')
- grad_alog: float32 [16, 4096], P(None, 'expert')
- grad_conv: float32 [4, 4096], P(None, 'expert')
- grad_chan: float32 [3, 4096], P(None, 'expert')
The draws below stay inside these ranges and needn't reach their ends.
Inputs may be any that keep to these rules, and one draw needn't show every extreme that they name: `route_ids`: within the 32 rows of one device no expert is named by more than 32 rows; some expert is named by exactly 32. The two experts of a token differ.
All inputs are finite; a program needn't handle non-finite values.
Results may differ from the reference program's by a relative error of at most 0.028.
Values may be sent and summed in bfloat16 or wider, within the bound.
A program may use at most 128 MiB of HBM per device.

```python
import math
import jax
import jax.numpy as jnp
import numpy as np
from jax import lax

DM = 2048
CH = 4096
NS = 16
KW = 4
HID = 7168
EXPERTS = 4
TOKENS = 1024
ROWS = 32
CAP = 32
N_SEQ = 8


def shard_levels(key, dims, shards, low, largest):
    def one(dim, shards_of):
        heights = jax.random.uniform(jax.random.fold_in(jax.random.fold_in(key, 6), dim), (shards_of,), jnp.float32, low / len(shards), largest / len(shards))
        return jnp.repeat(jnp.exp(heights), dims[dim] // shards_of).reshape((-1,) + (1,) * (len(dims) - dim - 1))

    level = one(*shards[0])
    for cut in shards[1:]:
        level = level * one(*cut)
    return level


def deal_out(own_key, own, number, rows, count, top, bound, lean):
    order = jax.random.permutation(own_key, count)
    heavy_load, common = portions_of(count, rows * top, bound, lean, True), portions_of(count, rows * top, bound, lean, False)
    places = jnp.arange(count)

    def named(sizes, turn):
        used = int((sizes > 0).sum())
        fixed = max(1, used // 4)
        passed = fixed + (places - fixed + turn * (used - fixed)) % max(1, count - fixed)
        return jnp.zeros((count,), jnp.int32).at[order[jnp.where(places < fixed, places, passed)]].set(jnp.asarray(sizes, jnp.int32))

    sizes = jnp.where(number % 4 == 0, named(heavy_load, number // 4), named(common, number - number // 4 - 1))
    mixed = jax.random.permutation(jax.random.fold_in(own, 3), count)
    source_of, taker = mixed[0:count // 2 * 2:2], mixed[1:count // 2 * 2:2]
    room = jnp.minimum(sizes[source_of] - 1, bound - sizes[taker]) // 2
    room = jnp.where((source_of == order[0]) | (taker == order[0]) | (sizes[taker] == 0), 0, jnp.maximum(room, 0))
    passed = jax.random.randint(jax.random.fold_in(own, 4), (count // 2,), 0, 1 << 20) % (room + 1)
    sizes = sizes.at[source_of].add(-passed).at[taker].add(passed)
    members = jnp.searchsorted(jnp.cumsum(sizes), jnp.arange(rows * top), side="right").astype(jnp.int32)
    listing = members.reshape(top, rows).T
    listing = listing[jax.random.permutation(jax.random.fold_in(own, 1), rows)]
    turn = jax.random.randint(jax.random.fold_in(own, 2), (rows, 1), 0, top)
    return jnp.take_along_axis(listing, (jnp.arange(top)[None, :] + turn) % top, axis=1)


def portions_of(number_of, total, reach, lean, full):
    portions = [(1 << 20) // math.isqrt(grade ** lean) + 1 for grade in range(1, number_of + 1)]
    largest = reach if full else min(reach, max(-(-total // number_of), total * portions[0] // sum(portions)))
    least = 1 if total - largest >= number_of - 1 else 0
    holding, rest = [largest] + [least] * (number_of - 1), total - largest - least * (number_of - 1)
    while rest > 0:
        movable = [i for i in range(1, number_of) if holding[i] < largest] or [i for i in range(1, number_of) if holding[i] < reach]
        pool, left = sum([portions[i] for i in movable]), rest
        for i in movable:
            addition = min(reach - holding[i], max(1, left * portions[i] // pool), rest)
            holding[i] = holding[i] + addition
            rest = rest - addition
    return np.array(holding)


def centred(own_key, shape, spread, reach, split=(), kind=jnp.bfloat16):
    factor_of = shard_levels(own_key, shape, split, -0.22, 0.18) if split else 1.0
    drawn = jax.random.normal(own_key, shape, jnp.float32) * spread * factor_of
    return jnp.minimum(jnp.maximum(drawn, -reach), reach).astype(kind)


def setup_inputs(seed: int = 0) -> dict:
    keys = jax.random.split(jax.random.key(seed), 18)
    x_in = centred(keys[0], (TOKENS, CH), 1.0, 6.0, ((0, 8), (1, 4)))
    z_in = centred(keys[1], (TOKENS, CH), 1.0, 6.0, ((0, 8), (1, 4)))
    dt_raw = centred(keys[2], (TOKENS, CH), 1.0, 4.0, ((0, 8), (1, 4)), jnp.float32)
    bc_in = centred(keys[3], (2, NS, TOKENS), 1.0, 6.0, ((2, 8),), jnp.float32)
    a_log = jnp.clip(-2.0 + 3.5 * jax.random.uniform(keys[4], (NS, CH), jnp.float32) ** shard_levels(keys[4], (NS, CH), ((1, 4),), -0.2, 0.2), -2.0, 1.5)
    conv_weight = centred(keys[5], (KW, CH), KW ** -0.5, 3.0, ((1, 4),), jnp.float32)
    conv_bias = centred(keys[6], (CH,), 0.5, 3.0, ((0, 4),), jnp.float32)
    skip_gain = jnp.clip(1.0 + 0.15 * jax.random.normal(keys[7], (CH,), jnp.float32), 0.25, 1.75)
    dt_bias = jnp.clip(-6.0 + 5.0 * jax.random.uniform(keys[8], (CH,), jnp.float32) ** shard_levels(keys[8], (CH,), ((0, 4),), -0.2, 0.2), -6.0, -1.0)
    out_weight = centred(keys[9], (CH, DM), CH ** -0.5, 0.09375, ((0, 4),))
    resid = centred(keys[10], (TOKENS, DM), 1.0, 6.0, ((0, 32),))
    w_gate = centred(keys[11], (EXPERTS, DM, HID), DM ** -0.5, 0.125, ((0, 4), (2, 8)))
    w_up = centred(keys[12], (EXPERTS, DM, HID), DM ** -0.5, 0.125, ((0, 4), (2, 8)))
    w_down = centred(keys[13], (EXPERTS, HID, DM), HID ** -0.5, 0.0625, ((0, 4), (1, 8)))
    route_ids_keys = jax.random.split(jax.random.fold_in(keys[14], 1), TOKENS // ROWS)
    route_ids_turns = jax.random.permutation(jax.random.fold_in(keys[14], 3), TOKENS // ROWS)
    route_ids = jax.vmap(lambda own, number: deal_out(jax.random.fold_in(keys[14], 2), own, number, ROWS, EXPERTS, 2, CAP, 2))(route_ids_keys, route_ids_turns).reshape((TOKENS, 2))
    route_weight = jnp.clip(0.2 + 0.6 * jax.random.uniform(keys[15], (TOKENS, 2), jnp.float32) ** shard_levels(keys[15], (TOKENS, 2), ((0, 32),), -0.2, 0.2), 0.2, 0.8)
    grad_mix = centred(keys[16], (TOKENS, DM), 1.0, 6.0, ((0, 8),))
    return dict(x_in=x_in, z_in=z_in, dt_raw=dt_raw, bc_in=bc_in, a_log=a_log, conv_weight=conv_weight, conv_bias=conv_bias, skip_gain=skip_gain, dt_bias=dt_bias, out_weight=out_weight, resid=resid, w_gate=w_gate, w_up=w_up, w_down=w_down, route_ids=route_ids, route_weight=route_weight, grad_mix=grad_mix)


def pair_combine(earlier, later):
    return (earlier[0] * later[0], later[0] * earlier[1] + later[1])

def mixer_core(x_val, dt_val, bc_val, a_val, conv_val, bias_val, skip_val, dtb_val):
    length = x_val.shape[0]
    padded = jnp.concatenate([jnp.zeros((KW - 1, x_val.shape[1]), jnp.float32), x_val], axis=0)
    pre = bias_val[None, :] + conv_val[0][None, :] * padded[0:length]
    for tap in range(1, KW):
        pre = pre + conv_val[tap][None, :] * padded[tap:tap + length]
    conv_out = jax.nn.silu(pre)
    step = jax.nn.softplus(dt_val + dtb_val[None, :])
    rate = -jnp.exp(a_val)
    decay = jnp.exp(step[:, None, :] * rate[None])
    drive = step[:, None, :] * bc_val[0].T[:, :, None] * conv_out[:, None, :]
    states = lax.associative_scan(pair_combine, (decay, drive), axis=0)[1]
    return lax.optimization_barrier(jnp.sum(bc_val[1].T[:, :, None] * states, axis=1)) + skip_val[None, :] * conv_out

def reference(x_in, z_in, dt_raw, bc_in, a_log, conv_weight, conv_bias, skip_gain, dt_bias, out_weight, resid, w_gate, w_up, w_down, route_ids, route_weight, grad_mix):
    width = math.gcd(CH, 256)
    nblk = CH // width

    def split_cols(arr):
        lead = arr.shape[:-1]
        return jnp.moveaxis(arr.reshape(lead + (nblk, width)), -2, 0)

    def join_cols(arr):
        moved = jnp.moveaxis(arr, 0, -2)
        return moved.reshape(moved.shape[:-2] + (CH,))
    back_mix = lax.dot_general(grad_mix, out_weight, (((1,), (1,)), ((), ())), preferred_element_type=jnp.float32)

    def block_work(pieces):
        xb, zb, db, ab, cwb, cbb, sgb, dbb, gb = pieces
        yb, pull = jax.vjp(mixer_core, xb, db, bc_in, ab, cwb, cbb, sgb, dbb)
        sig = jax.nn.sigmoid(zb)
        gated = yb * zb * sig
        grad_y = gb * zb * sig
        grad_zb = gb * yb * sig * (1.0 + zb * (1.0 - sig))
        return (gated, grad_zb) + tuple(pull(grad_y))
    results = lax.map(block_work, (split_cols(x_in.astype(jnp.float32)), split_cols(z_in.astype(jnp.float32)), split_cols(dt_raw), split_cols(a_log), split_cols(conv_weight), split_cols(conv_bias), split_cols(skip_gain), split_cols(dt_bias), split_cols(back_mix)))
    gated = join_cols(results[0]).astype(jnp.bfloat16)
    grad_z = join_cols(results[1])
    grad_x = join_cols(results[2])
    grad_dt = join_cols(results[3])
    grad_bc = lax.optimization_barrier(jnp.sum(results[4], axis=0))
    grad_alog = join_cols(results[5])
    grad_conv = join_cols(results[6])
    grad_chan = jnp.stack([join_cols(results[7]), join_cols(results[8]), join_cols(results[9])])
    mixed = jnp.dot(gated, out_weight, preferred_element_type=jnp.float32)
    hidden_in = (resid.astype(jnp.float32) + mixed).astype(jnp.bfloat16)
    nblocks = TOKENS // ROWS
    slot_count = nblocks * CAP
    flat_ids = route_ids.reshape(nblocks, ROWS * 2)
    onehot = (flat_ids[:, :, None] == jnp.arange(EXPERTS, dtype=jnp.int32)[None, None, :]).astype(jnp.int32)
    rank = lax.optimization_barrier(jnp.sum(jnp.cumsum(onehot, axis=1) * onehot, axis=2)) - 1
    target = flat_ids * slot_count + jnp.arange(nblocks, dtype=jnp.int32)[:, None] * CAP + rank
    target = target.reshape(-1).astype(jnp.int32)
    doubled = jnp.repeat(hidden_in, 2, axis=0)
    buffer = jnp.zeros((EXPERTS * slot_count, DM), jnp.bfloat16).at[target].set(doubled)
    buffer = buffer.reshape(EXPERTS, slot_count, DM)
    hid_dev = HID // N_SEQ

    def expert_work(pieces):
        rows_e, gate_w, up_w, down_w = pieces
        rows_f = rows_e.astype(jnp.float32)
        gate = jnp.dot(rows_f, gate_w.astype(jnp.float32), precision=lax.Precision.HIGHEST)
        upper = jnp.dot(rows_f, up_w.astype(jnp.float32), precision=lax.Precision.HIGHEST)
        hidden = (jax.nn.silu(gate) * upper).astype(jnp.bfloat16)
        hid_blocks = jnp.transpose(hidden.reshape(slot_count, N_SEQ, hid_dev), (1, 0, 2))
        down_blocks = down_w.reshape(N_SEQ, hid_dev, DM)

        def add_block(total, pair):
            part = jnp.dot(pair[0], pair[1], preferred_element_type=jnp.float32).astype(jnp.bfloat16)
            part = lax.optimization_barrier(part)
            return (total + part.astype(jnp.float32), None)
        total, _ = lax.scan(add_block, jnp.zeros((slot_count, DM), jnp.float32), (hid_blocks, down_blocks))
        return total.astype(jnp.bfloat16)
    outs = lax.map(expert_work, (buffer, w_gate, w_up, w_down))
    picked = outs.reshape(-1, DM)[target].astype(jnp.float32).reshape(TOKENS, 2, DM)
    moe = picked[:, 0] * route_weight[:, 0:1] + picked[:, 1] * route_weight[:, 1:2]
    layer_out = (hidden_in.astype(jnp.float32) + moe).astype(jnp.bfloat16)
    return (layer_out, grad_x, grad_z, grad_dt, grad_bc, grad_alog, grad_conv, grad_chan)
```

```python
import jax
import jax.numpy as jnp
from jax import lax
from jax.experimental import pallas as pl
from jax.experimental.pallas import tpu as pltpu
from jax.sharding import PartitionSpec as P

KW = 4
SUB = 8
LANES = 128


def shifted(x, axis, by):
    peers = lax.axis_size(axis)
    pairs = [(i, i + by) for i in range(peers) if 0 <= i + by < peers]
    return lax.ppermute(x, axis, pairs)


def wide(tile, width):
    return jnp.concatenate([tile] * (width // tile.shape[1]), axis=1)


def folded(value):
    total = value[:, :LANES]
    for at in range(LANES, value.shape[1], LANES):
        total = total + value[:, at : at + LANES]
    return total


def totals_kernel(step_ref, drive_ref, grad_ref, b_ref, c_ref, rate_ref, out_ref):
    rate = rate_ref[...]
    width = rate.shape[1]

    def advance(i, carry):
        state, passed, leaving = carry
        for j in range(SUB):
            decay = jnp.exp(step_ref[i, j : j + 1, :] * rate)
            state = decay * state + drive_ref[i, j : j + 1, :] * wide(b_ref[i, j], width)
            passed = passed * decay
            leaving = leaving + passed * (grad_ref[i, j : j + 1, :] * wide(c_ref[i, j], width))
        return (state, passed, leaving)

    zero = jnp.zeros_like(rate)
    state, passed, leaving = lax.fori_loop(
        0, step_ref.shape[0], advance, (zero, jnp.ones_like(rate), zero)
    )
    out_ref[0] = passed.astype(out_ref.dtype)
    out_ref[1] = state.astype(out_ref.dtype)
    out_ref[2] = leaving.astype(out_ref.dtype)


def forward_kernel(step_ref, drive_ref, b_ref, c_ref, rate_ref, start_ref, y_ref):
    rate = rate_ref[...]
    width = rate.shape[1]

    def advance(i, state):
        for j in range(SUB):
            decay = jnp.exp(step_ref[i, j : j + 1, :] * rate)
            state = decay * state + drive_ref[i, j : j + 1, :] * wide(b_ref[i, j], width)
            y_ref[i, j : j + 1, :] = jnp.sum(
                wide(c_ref[i, j], width) * state, axis=0, keepdims=True
            )
        return state

    lax.fori_loop(0, step_ref.shape[0], advance, start_ref[...])


def backward_kernel(
    step_ref,
    drive_ref,
    conv_ref,
    grad_ref,
    b_ref,
    c_ref,
    rate_ref,
    start_ref,
    arriving_ref,
    step_out_ref,
    conv_out_ref,
    b_out_ref,
    c_out_ref,
    alog_ref,
    states,
):
    rate = rate_ref[...]
    width = rate.shape[1]
    groups = step_ref.shape[0]

    @pl.when(pl.program_id(0) == 0)
    def _():
        b_out_ref[...] = jnp.zeros_like(b_out_ref)
        c_out_ref[...] = jnp.zeros_like(c_out_ref)

    states[0] = start_ref[...]

    def advance(i, state):
        for j in range(SUB):
            decay = jnp.exp(step_ref[i, j : j + 1, :] * rate)
            state = decay * state + drive_ref[i, j : j + 1, :] * wide(b_ref[i, j], width)
            states[i * SUB + j + 1] = state
        return state

    lax.fori_loop(0, groups, advance, start_ref[...])

    def retreat(k, carry):
        flow, alog_sum = carry
        i = groups - 1 - k
        for j in reversed(range(SUB)):
            at = i * SUB + j
            step_now = step_ref[i, j : j + 1, :]
            grad_now = grad_ref[i, j : j + 1, :]
            decay = jnp.exp(step_now * rate)
            adjoint = wide(c_ref[i, j], width) * grad_now + flow
            flow = decay * adjoint
            held = flow * states[at]
            alog_sum = alog_sum + step_now * held
            into_drive = jnp.sum(adjoint * wide(b_ref[i, j], width), axis=0, keepdims=True)
            step_out_ref[i, j : j + 1, :] = (
                jnp.sum(rate * held, axis=0, keepdims=True)
                + conv_ref[i, j : j + 1, :] * into_drive
            )
            conv_out_ref[i, j : j + 1, :] = step_now * into_drive
            b_out_ref[i, j] += folded(adjoint * drive_ref[i, j : j + 1, :])
            c_out_ref[i, j] += folded(grad_now * states[at + 1])
        return (flow, alog_sum)

    _, alog_sum = lax.fori_loop(0, groups, retreat, (arriving_ref[...], jnp.zeros_like(rate)))
    alog_ref[...] = alog_sum * rate


def sweeps(length, channels, states):
    block = min(512, channels)
    groups = length // SUB
    rows = pl.BlockSpec((groups, SUB, block), lambda k: (0, 0, k))
    spread = pl.BlockSpec((groups, SUB, states, LANES), lambda k: (0, 0, 0, 0))
    column = pl.BlockSpec((states, block), lambda k: (0, k))
    grid = (channels // block,)
    f32 = jnp.float32
    row_shape = jax.ShapeDtypeStruct((groups, SUB, channels), f32)
    spread_shape = jax.ShapeDtypeStruct((groups, SUB, states, LANES), f32)
    column_shape = jax.ShapeDtypeStruct((states, channels), f32)
    totals = pl.pallas_call(
        totals_kernel,
        grid=grid,
        in_specs=[rows, rows, rows, spread, spread, column],
        out_specs=pl.BlockSpec((3, states, block), lambda k: (0, 0, k)),
        out_shape=jax.ShapeDtypeStruct((3, states, channels), jnp.bfloat16),
        name="totals",
    )
    forward = pl.pallas_call(
        forward_kernel,
        grid=grid,
        in_specs=[rows, rows, spread, spread, column, column],
        out_specs=rows,
        out_shape=row_shape,
        name="forward",
    )
    backward = pl.pallas_call(
        backward_kernel,
        grid=grid,
        in_specs=[rows, rows, rows, rows, spread, spread, column, column, column],
        out_specs=[rows, rows, spread, spread, column],
        out_shape=[row_shape, row_shape, spread_shape, spread_shape, column_shape],
        scratch_shapes=[pltpu.VMEM((length + 1, states, block), f32)],
        name="backward",
    )
    return totals, forward, backward


MESH = pl.DeviceIdType.MESH


def places():
    s, z = lax.axis_index("seq"), lax.axis_index("expert")
    core = lax.rem(s, 2)
    sib = s + 1 - 2 * core
    across_x = s + 2 - 4 * lax.rem(lax.div(s, 2), 2)
    across_y = s + 4 - 8 * lax.div(s, 4)
    return s, z, core, sib, across_x, across_y


def moe_kernel(
    p_ref,
    resid_ref,
    share_ref,
    sums_ref,
    bc_ref,
    wg_hbm,
    wu_hbm,
    wd_hbm,
    out_ref,
    sums_out,
    bc_out,
    rows_all,
    wgu,
    wd,
    hidden,
    own_h,
    zrecv,
    zfin,
    part,
    psib,
    acc,
    rx,
    ry,
    rdx,
    rdy,
    fin,
    sums_recv,
    sums_acc,
    bc_recv,
    w_sem,
    z_sem,
    g_sem,
    x_sem,
    y_sem,
    b_sem,
    f_sem,
    sb_sem,
    ps_sem,
    rs_sem,
    zf_sem,
    sm_sem,
    bc_sem,
):
    s, z, core, sib, ax, ay = places()
    f32, bf16 = jnp.float32, jnp.bfloat16
    ways = 4
    rows = resid_ref.shape[0]
    length, width = p_ref.shape
    half = width // 2
    tiles = wgu.shape[1] // 256

    def to(sem, index, src, dst, seq, exp):
        return pltpu.make_async_remote_copy(
            src_ref=src,
            dst_ref=dst,
            send_sem=sem.at[0, index],
            recv_sem=sem.at[1, index],
            device_id=(seq, exp),
            device_id_type=MESH,
        )

    loads = []
    for t in range(tiles):
        for k, w_hbm in enumerate((wg_hbm, wu_hbm)):
            loads.append(
                pltpu.make_async_copy(
                    w_hbm.at[0, :, pl.ds(t * 128, 128)],
                    wgu.at[:, pl.ds(t * 256 + k * 128, 128)],
                    w_sem.at[2 * t + k],
                )
            )
    loads.append(pltpu.make_async_copy(wd_hbm.at[0], wd, w_sem.at[2 * tiles]))
    for load in loads:
        load.start()

    zs = [lax.rem(z + d, ways) for d in range(ways)]
    zb = [lax.rem(z + ways - d, ways) for d in range(ways)]

    barrier = pltpu.get_barrier_semaphore()
    for seq, exp in ((sib, z), (ax, z), (ay, z), (s, zs[1]), (s, zs[2]), (s, zs[3])):
        pl.semaphore_signal(barrier, inc=1, device_id=(seq, exp), device_id_type=MESH)
    pl.semaphore_wait(barrier, 6)

    def block(seq, exp):
        return pl.ds(pl.multiple_of(seq * length + exp * rows, rows), rows)

    def within(exp):
        return pl.ds(pl.multiple_of(exp * rows, rows), rows)

    z_out = [to(z_sem, d - 1, p_ref.at[within(zs[d])], zrecv.at[d - 1], s, zs[d]) for d in (1, 2, 3)]
    for copy in z_out:
        copy.start()
    sums_copies = [
        to(sm_sem, 0, sums_ref, sums_recv.at[0], sib, z),
        to(sm_sem, 1, sums_acc.at[0], sums_recv.at[1], ax, z),
        to(sm_sem, 2, sums_acc.at[1], sums_recv.at[2], ay, z),
    ]
    sums_copies[0].start()
    bc_copies = [to(bc_sem, d - 1, bc_ref, bc_recv.at[d - 1], s, zs[d]) for d in (1, 2, 3)]
    for copy in bc_copies:
        copy.start()

    for copy in z_out:
        copy.wait_recv()
    total = resid_ref[...].astype(f32) + p_ref[within(z), :].astype(f32)
    for d in range(3):
        total = total + zrecv[d].astype(f32)
    own_h[...] = total.astype(bf16)
    here = block(s, z)
    rows_all[here, :] = total.astype(bf16)

    gather = [to(g_sem, d - 1, rows_all.at[here], rows_all.at[here], s, zs[d]) for d in (1, 2, 3)]
    to_x, to_y, to_b = [], [], []
    for d in range(ways):
        at = rows_all.at[block(s, zb[d])]
        to_x.append(to(x_sem, d, at, at, ax, z))
        to_y.append(to(y_sem, d, at, at, ay, z))
        to_b.append(to(b_sem, d, at, at, sib, z))
    for copy in gather + [to_x[0], to_y[0], to_b[0]]:
        copy.start()

    sums_copies[0].wait_recv()
    sums_acc[0] = sums_ref[...] + sums_recv[0]
    sums_copies[1].start()

    for d in (1, 2, 3):
        gather[d - 1].wait_recv()
        to_x[d].start()
        to_y[d].start()
        to_b[d].start()

    sums_copies[1].wait_recv()
    sums_acc[1] = sums_acc[0] + sums_recv[1]
    sums_copies[2].start()

    for copy in bc_copies:
        copy.wait_recv()
    bc_out[...] = (bc_ref[...] + bc_recv[0]) + (bc_recv[1] + bc_recv[2])

    def chip_rows(seq):
        return pl.ds(pl.multiple_of(lax.div(seq, 2) * (2 * length), 2 * length), 2 * length)

    def up(seq):
        at = chip_rows(seq)

        def tile(t, _):
            both = jnp.dot(
                rows_all[at, :],
                wgu[:, pl.ds(pl.multiple_of(t * 256, 256), 256)],
                preferred_element_type=f32,
            )
            gate, upper = both[:, :128], both[:, 128:]
            value = gate * jax.nn.sigmoid(gate) * upper
            hidden[:, pl.ds(pl.multiple_of(t * 128, 128), 128)] = value.astype(bf16)
            return 0

        lax.fori_loop(0, tiles, tile, 0)

    other = pl.ds(pl.multiple_of((1 - core) * length, length), length)
    mine = pl.ds(pl.multiple_of(core * length, length), length)

    def cols(h):
        return pl.ds(h * half, half)

    pair = {}

    def down(r, h):
        def tile(t, _):
            at = pl.ds(pl.multiple_of(h * half + t * 256, 256), 256)
            part[r, :, at] = jnp.dot(
                hidden[...], wd[:, at], preferred_element_type=f32
            ).astype(bf16)
            return 0

        lax.fori_loop(0, half // 256, tile, 0)
        copy = to(ps_sem, 2 * r + h, part.at[r, other, cols(h)], psib.at[r, :, cols(h)], sib, z)
        copy.start()
        pair[r, h] = copy

    def paired(r, h):
        pair[r, h].wait_recv()
        acc[r, :, cols(h)] = (
            part[r, mine, cols(h)].astype(f32) + psib[r, :, cols(h)].astype(f32)
        ).astype(bf16)

    for copy in to_b:
        copy.wait_recv()
    for load in loads:
        load.wait()
    up(s)

    for copy in to_x + to_y:
        copy.wait_recv()
    forward = []
    for d in range(ways):
        origin, target = (ay, ax) if d < 2 else (ax, ay)
        at = rows_all.at[block(origin, zb[d])]
        forward.append(to(f_sem, d, at, at, target, z))
    for d in (0, 2, 1, 3):
        forward[d].start()

    def all_of(seq):
        return rows_all.at[pl.ds(pl.multiple_of(seq * length, length), length)]

    diag = ax + ay - s
    share_out = [to(sb_sem, k, all_of(o), all_of(o), sib, z) for k, o in enumerate((ax, ay, diag))]
    share_out[0].start()
    share_out[1].start()

    down(0, 0)
    down(0, 1)
    share_out[0].wait_recv()
    up(ax)
    down(1, 0)
    down(1, 1)
    for copy in forward:
        copy.wait_recv()
    share_out[2].start()
    paired(0, 0)
    paired(0, 1)
    paired(1, 0)
    paired(1, 1)
    send = {}

    def reduce_out(name, index, src, dst, seq):
        copy = to(rs_sem, index, src, dst, seq, z)
        copy.start()
        send[name] = copy

    reduce_out("x0", 0, acc.at[1, :, cols(0)], rx.at[:, cols(0)], ax)
    share_out[1].wait_recv()
    up(ay)
    down(2, 0)
    down(2, 1)
    paired(2, 0)
    paired(2, 1)
    reduce_out("y1", 1, acc.at[2, :, cols(1)], ry.at[:, cols(1)], ay)
    share_out[2].wait_recv()
    up(diag)
    down(3, 0)
    down(3, 1)
    paired(3, 0)
    reduce_out("d0", 2, acc.at[3, :, cols(0)], rdx, ax)
    paired(3, 1)
    reduce_out("d1", 3, acc.at[3, :, cols(1)], rdy, ay)

    sums_copies[2].wait_recv()
    sums_out[...] = sums_acc[1] + sums_recv[2]

    send["d0"].wait_recv()
    acc[2, :, cols(0)] = (acc[2, :, cols(0)].astype(f32) + rdx[...].astype(f32)).astype(bf16)
    reduce_out("y0", 4, acc.at[2, :, cols(0)], ry.at[:, cols(0)], ay)
    send["d1"].wait_recv()
    acc[1, :, cols(1)] = (acc[1, :, cols(1)].astype(f32) + rdy[...].astype(f32)).astype(bf16)
    reduce_out("x1", 5, acc.at[1, :, cols(1)], rx.at[:, cols(1)], ax)

    back = []
    for h in range(2):
        send["x%d" % h].wait_recv()
        send["y%d" % h].wait_recv()
        fin[:, cols(h)] = (
            acc[0, :, cols(h)].astype(f32)
            + rx[:, cols(h)].astype(f32)
            + ry[:, cols(h)].astype(f32)
        ).astype(bf16)
        for d in (1, 2, 3):
            copy = to(
                zf_sem,
                3 * h + d - 1,
                fin.at[within(zs[d]), cols(h)],
                zfin.at[d - 1, :, cols(h)],
                s,
                zs[d],
            )
            copy.start()
            back.append(copy)
    for h in range(2):
        for copy in back[3 * h : 3 * h + 3]:
            copy.wait_recv()
        total = own_h[:, cols(h)].astype(f32)
        total = total + share_ref[z][:, :1] * fin[within(z), cols(h)].astype(f32)
        for d in (1, 2, 3):
            total = total + share_ref[zb[d]][:, :1] * zfin[d - 1, :, cols(h)].astype(f32)
        out_ref[:, cols(h)] = total.astype(bf16)

    for copy in (
        z_out + sums_copies + bc_copies + gather + to_x + to_y + to_b + forward + share_out + back
    ):
        copy.wait_send()
    for copy in list(pair.values()) + list(send.values()):
        copy.wait_send()


def moe_exchange(partial_value, resid, share, own_sums, own_bc, w_gate, w_up, w_down):
    rows, width = resid.shape
    length = partial_value.shape[0]
    units = w_gate.shape[2]
    tiles = units // 128
    seqs = lax.axis_size("seq")
    half = width // 2
    bf16, f32 = jnp.bfloat16, jnp.float32
    vmem = pl.BlockSpec(memory_space=pltpu.VMEM)
    hbm = pl.BlockSpec(memory_space=pl.ANY)
    sem = pltpu.SemaphoreType.DMA
    return pl.pallas_call(
        moe_kernel,
        out_shape=[
            jax.ShapeDtypeStruct((rows, width), bf16),
            jax.ShapeDtypeStruct(own_sums.shape, f32),
            jax.ShapeDtypeStruct(own_bc.shape, f32),
        ],
        in_specs=[vmem] * 5 + [hbm] * 3,
        out_specs=[vmem] * 3,
        scratch_shapes=[
            pltpu.VMEM((seqs * length, width), bf16),
            pltpu.VMEM((width, 2 * units), bf16),
            pltpu.VMEM((units, width), bf16),
            pltpu.VMEM((2 * length, units), bf16),
            pltpu.VMEM((rows, width), bf16),
            pltpu.VMEM((3, rows, width), bf16),
            pltpu.VMEM((3, rows, width), bf16),
            pltpu.VMEM((4, 2 * length, width), bf16),
            pltpu.VMEM((4, length, width), bf16),
            pltpu.VMEM((4, length, width), bf16),
            pltpu.VMEM((length, width), bf16),
            pltpu.VMEM((length, width), bf16),
            pltpu.VMEM((length, half), bf16),
            pltpu.VMEM((length, half), bf16),
            pltpu.VMEM((length, width), bf16),
            pltpu.VMEM((3,) + own_sums.shape, f32),
            pltpu.VMEM((2,) + own_sums.shape, f32),
            pltpu.VMEM((3,) + own_bc.shape, f32),
            sem((2 * tiles + 1,)),
            sem((2, 3)),
            sem((2, 3)),
            sem((2, 4)),
            sem((2, 4)),
            sem((2, 4)),
            sem((2, 4)),
            sem((2, 3)),
            sem((2, 8)),
            sem((2, 6)),
            sem((2, 6)),
            sem((2, 3)),
            sem((2, 3)),
        ],
        compiler_params=pltpu.CompilerParams(
            collective_id=0, has_side_effects=True, vmem_limit_bytes=52 << 20
        ),
        cost_estimate=pl.CostEstimate(
            flops=6 * seqs * length * width * units,
            bytes_accessed=6 * width * units,
            transcendentals=seqs * length * units,
        ),
        name="experts",
    )(partial_value, resid, share, own_sums, own_bc, w_gate, w_up, w_down)


def entering(everything):
    peers, here = everything.shape[0], lax.axis_index("seq")
    values = everything.astype(jnp.float32)
    start = jnp.zeros_like(values[0, 0])
    arriving = jnp.zeros_like(start)
    for k in range(peers):
        start = jnp.where(k < here, values[k, 0] * start + values[k, 1], start)
        back = peers - 1 - k
        arriving = jnp.where(back > here, values[back, 0] * arriving + values[back, 2], arriving)
    return start, arriving


def routed_experts(partial_value, resid, w_gate, w_up, w_down, route_ids, route_weight):
    rows = resid.shape[0]
    mixed = lax.psum(partial_value, "expert").astype(jnp.float32)
    own = lax.dynamic_slice_in_dim(mixed, lax.axis_index("expert") * rows, rows, 0)
    hidden_in = (resid.astype(jnp.float32) + own).astype(jnp.bfloat16)
    experts = lax.axis_size("expert")
    capacity = 4 * rows // experts
    flat_ids = route_ids.reshape(-1)
    order = jnp.arange(flat_ids.shape[0], dtype=jnp.int32)
    earlier = (flat_ids[:, None] == flat_ids[None, :]) & (order[None, :] < order[:, None])
    rank = jnp.sum(earlier.astype(jnp.int32), axis=1)
    slot = flat_ids * capacity + rank
    placing = (jnp.arange(experts * capacity, dtype=jnp.int32)[:, None] == slot[None, :]).astype(
        jnp.bfloat16
    )
    doubled = jnp.repeat(hidden_in, 2, axis=0)
    outgoing = jnp.dot(placing, doubled, preferred_element_type=jnp.float32).astype(jnp.bfloat16)
    incoming = lax.all_to_all(outgoing, "expert", split_axis=0, concat_axis=0, tiled=True)
    piece = lax.all_gather(incoming, "seq", axis=0, tiled=True)
    gate = jnp.dot(piece, w_gate[0], preferred_element_type=jnp.float32)
    upper = jnp.dot(piece, w_up[0], preferred_element_type=jnp.float32)
    hidden = (jax.nn.silu(gate) * upper).astype(jnp.bfloat16)
    expert_sum = lax.psum_scatter(
        jnp.dot(hidden, w_down[0], preferred_element_type=jnp.float32).astype(jnp.bfloat16),
        "seq",
        scatter_dimension=0,
        tiled=True,
    )
    returned = lax.all_to_all(expert_sum, "expert", split_axis=0, concat_axis=0, tiled=True)
    picked = lax.dot_general(
        placing, returned, (((0,), (0,)), ((), ())), preferred_element_type=jnp.float32
    )
    picked = picked.reshape(rows, 2, -1)
    moe = picked[:, 0] * route_weight[:, 0:1] + picked[:, 1] * route_weight[:, 1:2]
    return (hidden_in.astype(jnp.float32) + moe).astype(jnp.bfloat16)


def local(
    x_in,
    z_in,
    dt_raw,
    bc_in,
    a_log,
    conv_weight,
    conv_bias,
    skip_gain,
    dt_bias,
    out_weight,
    resid,
    w_gate,
    w_up,
    w_down,
    route_ids,
    route_weight,
    grad_mix,
):
    length, channels = x_in.shape
    states = a_log.shape[0]
    rim = KW - 1
    x_val = x_in.astype(jnp.float32)
    z_val = z_in.astype(jnp.float32)
    before = shifted(x_in[length - rim :], "seq", 1)
    padded = jnp.concatenate([before.astype(jnp.float32), x_val], axis=0)
    pre = conv_bias[None, :] + conv_weight[0][None, :] * padded[0:length]
    for tap in range(1, KW):
        pre = pre + conv_weight[tap][None, :] * padded[tap : tap + length]
    conv_sig = jax.nn.sigmoid(pre)
    conv_out = pre * conv_sig
    step = jax.nn.softplus(dt_raw + dt_bias[None, :])
    rate = -jnp.exp(a_log)
    drive = step * conv_out
    z_sig = jax.nn.sigmoid(z_val)
    back_mix = lax.dot_general(
        grad_mix, out_weight, (((1,), (1,)), ((), ())), preferred_element_type=jnp.float32
    )
    grad_y = back_mix * z_val * z_sig

    def grouped(array):
        return array.reshape(length // SUB, SUB, channels)

    def flat(array):
        return array.reshape(length, channels)

    spread = jnp.broadcast_to(
        bc_in.transpose(0, 2, 1)[:, :, :, None], (2, length, states, LANES)
    ).reshape(2, length // SUB, SUB, states, LANES)
    b_wide, c_wide = spread[0], spread[1]
    totals, forward, backward = sweeps(length, channels, states)
    step_g, drive_g, grad_g, conv_g = (grouped(a) for a in (step, drive, grad_y, conv_out))
    own_totals = totals(step_g, drive_g, grad_g, b_wide, c_wide, rate)
    start, arriving = entering(lax.all_gather(own_totals, "seq"))
    y_val = flat(forward(step_g, drive_g, b_wide, c_wide, rate, start))
    y_val = y_val + skip_gain[None, :] * conv_out
    gated = (y_val * z_val * z_sig).astype(jnp.bfloat16)
    partial_value = jnp.dot(gated, out_weight, preferred_element_type=jnp.float32)
    rows = resid.shape[0]
    experts = lax.axis_size("expert")
    dense = experts == 4 and lax.axis_size("seq") == 8
    grad_z = back_mix * y_val * z_sig * (1.0 + z_val * (1.0 - z_sig))
    grad_step, conv_part_grad, grad_b, grad_c, grad_alog_local = backward(
        step_g, drive_g, conv_g, grad_g, b_wide, c_wide, rate, start, arriving
    )
    grad_step, conv_part_grad = flat(grad_step), flat(conv_part_grad)
    grad_conv_out = skip_gain[None, :] * grad_y + conv_part_grad
    grad_skip = jnp.sum(grad_y * conv_out, axis=0)
    grad_dt = grad_step * jax.nn.sigmoid(dt_raw + dt_bias[None, :])
    grad_pre = grad_conv_out * (conv_sig * (1.0 + pre * (1.0 - conv_sig)))
    after = shifted(grad_pre[:rim], "seq", -1)
    grad_pad = jnp.concatenate([grad_pre, after], axis=0)
    grad_x = conv_weight[rim][None, :] * grad_pad[0:length]
    for tap in range(rim):
        grad_x = grad_x + conv_weight[tap][None, :] * grad_pad[rim - tap : rim - tap + length]
    grad_taps = jnp.stack(
        [jnp.sum(grad_pre * padded[tap : tap + length], axis=0) for tap in range(KW)]
    )
    channel_grads = jnp.stack([jnp.sum(grad_pre, axis=0), grad_skip, jnp.sum(grad_dt, axis=0)])
    own_sums = jnp.concatenate([grad_alog_local, grad_taps, channel_grads], axis=0)
    own_bc = jnp.stack([jnp.sum(grad_b, axis=-1), jnp.sum(grad_c, axis=-1)])
    own_bc = own_bc.reshape(2, length, states).transpose(0, 2, 1).reshape(2 * states, length)
    if dense:
        chosen = jnp.arange(experts, dtype=jnp.int32)[:, None, None] == route_ids[None]
        share = jnp.sum(jnp.where(chosen, route_weight[None], 0.0), axis=2, keepdims=True)
        share = jnp.broadcast_to(share, (experts, rows, LANES))
        padded_sums = jnp.concatenate([own_sums, jnp.zeros((1, channels), jnp.float32)], axis=0)
        layer_out, sums, grad_bc = moe_exchange(
            partial_value.astype(jnp.bfloat16), resid, share, padded_sums, own_bc, w_gate, w_up, w_down
        )
        grad_bc = grad_bc.reshape(2, states, length)
    else:
        layer_out = routed_experts(
            partial_value.astype(jnp.bfloat16),
            resid,
            w_gate,
            w_up,
            w_down,
            route_ids,
            route_weight,
        )
        sums = lax.psum(own_sums, "seq")
        grad_bc = lax.psum(own_bc, "expert").reshape(2, states, length)
    grad_alog = sums[:states]
    grad_conv = sums[states : states + KW]
    grad_chan = sums[states + KW : states + KW + 3]
    return (layer_out, grad_x, grad_z, grad_dt, grad_bc, grad_alog, grad_conv, grad_chan)


def solution(mesh):
    in_specs = (
        P("seq", "expert"),
        P("seq", "expert"),
        P("seq", "expert"),
        P(None, None, "seq"),
        P(None, "expert"),
        P(None, "expert"),
        P("expert"),
        P("expert"),
        P("expert"),
        P("expert", None),
        P(("seq", "expert"), None),
        P("expert", None, "seq"),
        P("expert", None, "seq"),
        P("expert", "seq", None),
        P(("seq", "expert"), None),
        P(("seq", "expert"), None),
        P("seq", None),
    )
    out_specs = (
        P(("seq", "expert"), None),
        P("seq", "expert"),
        P("seq", "expert"),
        P("seq", "expert"),
        P(None, None, "seq"),
        P(None, "expert"),
        P(None, "expert"),
        P(None, "expert"),
    )
    return jax.shard_map(local, mesh=mesh, in_specs=in_specs, out_specs=out_specs, check_vma=False)
```

```python
import jax
import jax.numpy as jnp
from jax import lax
from jax.experimental import pallas as pl
from jax.experimental.pallas import tpu as pltpu
from jax.sharding import PartitionSpec as P

KW = 4
SUB = 8
LANES = 128


def shifted(x, axis, by):
    peers = lax.axis_size(axis)
    pairs = [(i, i + by) for i in range(peers) if 0 <= i + by < peers]
    return lax.ppermute(x, axis, pairs)


def wide(tile, width):
    return jnp.concatenate([tile] * (width // tile.shape[1]), axis=1)


def folded(value):
    total = value[:, :LANES]
    for at in range(LANES, value.shape[1], LANES):
        total = total + value[:, at : at + LANES]
    return total


def totals_kernel(step_ref, drive_ref, grad_ref, b_ref, c_ref, rate_ref, out_ref):
    rate = rate_ref[...]
    width = rate.shape[1]

    def advance(i, carry):
        state, passed, leaving = carry
        for j in range(SUB):
            decay = jnp.exp(step_ref[i, j : j + 1, :] * rate)
            state = decay * state + drive_ref[i, j : j + 1, :] * wide(b_ref[i, j], width)
            passed = passed * decay
            leaving = leaving + passed * (grad_ref[i, j : j + 1, :] * wide(c_ref[i, j], width))
        return (state, passed, leaving)

    zero = jnp.zeros_like(rate)
    state, passed, leaving = lax.fori_loop(
        0, step_ref.shape[0], advance, (zero, jnp.ones_like(rate), zero)
    )
    out_ref[0] = passed.astype(out_ref.dtype)
    out_ref[1] = state.astype(out_ref.dtype)
    out_ref[2] = leaving.astype(out_ref.dtype)


def forward_kernel(step_ref, drive_ref, b_ref, c_ref, rate_ref, start_ref, y_ref):
    rate = rate_ref[...]
    width = rate.shape[1]

    def advance(i, state):
        for j in range(SUB):
            decay = jnp.exp(step_ref[i, j : j + 1, :] * rate)
            state = decay * state + drive_ref[i, j : j + 1, :] * wide(b_ref[i, j], width)
            y_ref[i, j : j + 1, :] = jnp.sum(
                wide(c_ref[i, j], width) * state, axis=0, keepdims=True
            )
        return state

    lax.fori_loop(0, step_ref.shape[0], advance, start_ref[...])


def backward_kernel(
    step_ref,
    drive_ref,
    conv_ref,
    grad_ref,
    b_ref,
    c_ref,
    rate_ref,
    start_ref,
    arriving_ref,
    step_out_ref,
    conv_out_ref,
    b_out_ref,
    c_out_ref,
    alog_ref,
    states,
):
    rate = rate_ref[...]
    width = rate.shape[1]
    groups = step_ref.shape[0]

    @pl.when(pl.program_id(0) == 0)
    def _():
        b_out_ref[...] = jnp.zeros_like(b_out_ref)
        c_out_ref[...] = jnp.zeros_like(c_out_ref)

    states[0] = start_ref[...]

    def advance(i, state):
        for j in range(SUB):
            decay = jnp.exp(step_ref[i, j : j + 1, :] * rate)
            state = decay * state + drive_ref[i, j : j + 1, :] * wide(b_ref[i, j], width)
            states[i * SUB + j + 1] = state
        return state

    lax.fori_loop(0, groups, advance, start_ref[...])

    def retreat(k, carry):
        flow, alog_sum = carry
        i = groups - 1 - k
        for j in reversed(range(SUB)):
            at = i * SUB + j
            step_now = step_ref[i, j : j + 1, :]
            grad_now = grad_ref[i, j : j + 1, :]
            decay = jnp.exp(step_now * rate)
            adjoint = wide(c_ref[i, j], width) * grad_now + flow
            flow = decay * adjoint
            held = flow * states[at]
            alog_sum = alog_sum + step_now * held
            into_drive = jnp.sum(adjoint * wide(b_ref[i, j], width), axis=0, keepdims=True)
            step_out_ref[i, j : j + 1, :] = (
                jnp.sum(rate * held, axis=0, keepdims=True)
                + conv_ref[i, j : j + 1, :] * into_drive
            )
            conv_out_ref[i, j : j + 1, :] = step_now * into_drive
            b_out_ref[i, j] += folded(adjoint * drive_ref[i, j : j + 1, :])
            c_out_ref[i, j] += folded(grad_now * states[at + 1])
        return (flow, alog_sum)

    _, alog_sum = lax.fori_loop(0, groups, retreat, (arriving_ref[...], jnp.zeros_like(rate)))
    alog_ref[...] = alog_sum * rate


def sweeps(length, channels, states):
    block = min(512, channels)
    groups = length // SUB
    rows = pl.BlockSpec((groups, SUB, block), lambda k: (0, 0, k))
    spread = pl.BlockSpec((groups, SUB, states, LANES), lambda k: (0, 0, 0, 0))
    column = pl.BlockSpec((states, block), lambda k: (0, k))
    grid = (channels // block,)
    f32 = jnp.float32
    row_shape = jax.ShapeDtypeStruct((groups, SUB, channels), f32)
    spread_shape = jax.ShapeDtypeStruct((groups, SUB, states, LANES), f32)
    column_shape = jax.ShapeDtypeStruct((states, channels), f32)
    totals = pl.pallas_call(
        totals_kernel,
        grid=grid,
        in_specs=[rows, rows, rows, spread, spread, column],
        out_specs=pl.BlockSpec((3, states, block), lambda k: (0, 0, k)),
        out_shape=jax.ShapeDtypeStruct((3, states, channels), jnp.bfloat16),
        name="totals",
    )
    forward = pl.pallas_call(
        forward_kernel,
        grid=grid,
        in_specs=[rows, rows, spread, spread, column, column],
        out_specs=rows,
        out_shape=row_shape,
        name="forward",
    )
    backward = pl.pallas_call(
        backward_kernel,
        grid=grid,
        in_specs=[rows, rows, rows, rows, spread, spread, column, column, column],
        out_specs=[rows, rows, spread, spread, column],
        out_shape=[row_shape, row_shape, spread_shape, spread_shape, column_shape],
        scratch_shapes=[pltpu.VMEM((length + 1, states, block), f32)],
        name="backward",
    )
    return totals, forward, backward


MESH = pl.DeviceIdType.MESH
GROUP = 16


def places():
    s, z = lax.axis_index("seq"), lax.axis_index("expert")
    core = lax.rem(s, 2)
    sib = s + 1 - 2 * core
    across_x = s + 2 - 4 * lax.rem(lax.div(s, 2), 2)
    across_y = s + 4 - 8 * lax.div(s, 4)
    return s, z, core, sib, across_x, across_y


def transposed(a, b):
    return lax.dot_general(a, b, (((1,), (1,)), ((), ())), preferred_element_type=jnp.float32)


def layer_kernel(
    x_ref,
    z_ref,
    dt_ref,
    bc_ref,
    alog_ref,
    conv_ref,
    gain_ref,
    resid_ref,
    share_ref,
    ow_hbm,
    gm_hbm,
    wg_hbm,
    wu_hbm,
    wd_hbm,
    out_ref,
    gx_ref,
    gz_ref,
    gdt_ref,
    sums_out,
    bc_out,
    rows_all,
    wgu,
    wd,
    ow,
    gm,
    hidden,
    own_h,
    zrecv,
    zfin,
    part,
    psib,
    acc,
    rx,
    ry,
    rdx,
    rdy,
    fin,
    p_buf,
    sums_own,
    sums_recv,
    sums_acc,
    bc_own,
    bc_recv,
    decays,
    states,
    b_wide,
    c_wide,
    b_block,
    c_block,
    step_buf,
    drive_buf,
    conv_buf,
    grad_buf,
    dsilu_buf,
    dtsig_buf,
    zgate_buf,
    zfac_buf,
    into_buf,
    qsum_buf,
    xpad,
    gpad,
    xhalo,
    ghalo,
    gated,
    adj,
    quo,
    gb_acc,
    gc_acc,
    tot,
    tsib,
    tpair,
    trecv,
    rate_buf,
    start_buf,
    arrive_buf,
    w_sem,
    sems,
):
    s, z, core, sib, ax, ay = places()
    diag = ax + ay - s
    f32, bf16 = jnp.float32, jnp.bfloat16
    ways, seqs = 4, 8
    rows = resid_ref.shape[0]
    length, channels = x_ref.shape
    width = resid_ref.shape[1]
    half = width // 2
    scan = channels // 2
    groups = length // GROUP
    nst = alog_ref.shape[0]
    flat = GROUP * nst
    tiles = wgu.shape[1] // 256
    after = lax.rem(s + 1, seqs)
    ahead = lax.rem(s + seqs - 1, seqs)
    count = [0]
    everything = []

    def to(src, dst, seq, exp):
        index = count[0]
        count[0] += 1
        copy = pltpu.make_async_remote_copy(
            src_ref=src,
            dst_ref=dst,
            send_sem=sems.at[0, index],
            recv_sem=sems.at[1, index],
            device_id=(seq, exp),
            device_id_type=MESH,
        )
        everything.append(copy)
        return copy

    first = [
        pltpu.make_async_copy(ow_hbm, ow, w_sem.at[0]),
        pltpu.make_async_copy(gm_hbm, gm, w_sem.at[1]),
    ]
    for load in first:
        load.start()
    loads = []
    for t in range(tiles):
        for k, w_hbm in enumerate((wg_hbm, wu_hbm)):
            loads.append(
                pltpu.make_async_copy(
                    w_hbm.at[0, :, pl.ds(t * 128, 128)],
                    wgu.at[:, pl.ds(t * 256 + k * 128, 128)],
                    w_sem.at[2 + 2 * t + k],
                )
            )
    loads.append(pltpu.make_async_copy(wd_hbm.at[0], wd, w_sem.at[2 + 2 * tiles]))

    zs = [lax.rem(z + d, ways) for d in range(ways)]
    zb = [lax.rem(z + ways - d, ways) for d in range(ways)]

    barrier = pltpu.get_barrier_semaphore()
    partners = [(sib, z), (ax, z), (ay, z), (diag, z), (after, z), (ahead, z)]
    partners += [(s, zs[1]), (s, zs[2]), (s, zs[3])]
    for seq, exp in partners:
        pl.semaphore_signal(barrier, inc=1, device_id=(seq, exp), device_id_type=MESH)
    pl.semaphore_wait(barrier, len(partners))

    halo = to(x_ref.at[pl.ds(length - GROUP, GROUP), :], xhalo, after, z)
    halo.start()

    for k, spread in enumerate((b_wide, c_wide)):
        value = bc_ref[k]
        for t in range(length):
            spread[t] = jnp.broadcast_to(value[:, t : t + 1], (nst, LANES))
    lane = lax.broadcasted_iota(jnp.int32, (length, flat), 1)
    row = lax.broadcasted_iota(jnp.int32, (length, flat), 0)
    same_token = lax.div(lane, nst) == lax.rem(row, GROUP)
    lane_r = lax.broadcasted_iota(jnp.int32, (nst, flat), 1)
    row_r = lax.broadcasted_iota(jnp.int32, (nst, flat), 0)
    repeat = (lax.rem(lane_r, nst) == row_r).astype(f32).astype(bf16)
    for k, block_ref in enumerate((b_block, c_block)):
        by_token = jnp.transpose(bc_ref[k]).astype(bf16)
        laid = jnp.dot(by_token, repeat, preferred_element_type=f32)
        block_ref[...] = jnp.where(same_token, laid, 0.0).astype(bf16)
    diagonal = same_token[:GROUP].astype(f32)
    ones_block = diagonal.astype(bf16)
    rate_buf[...] = -jnp.exp(alog_ref[...])

    for load in first:
        load.wait()

    def mix_tile(t, _):
        at = pl.ds(pl.multiple_of(t * 256, 256), 256)
        zfac_buf[:, :, at] = transposed(gm[...], ow[at, :]).reshape(groups, GROUP, 256)
        return 0

    lax.fori_loop(0, channels // 256, mix_tile, 0)
    for load in loads:
        load.start()
    xpad[8 : 8 + length, :] = x_ref[...].astype(f32)
    halo.wait_recv()
    xpad[0:8, :] = jnp.where(s > 0, xhalo[...].astype(f32)[GROUP - 8 :], 0.0)

    def prepare(t, _):
        at = pl.ds(pl.multiple_of(t * LANES, LANES), LANES)

        def put(ref, value):
            ref[:, :, at] = value.reshape(groups, GROUP, LANES)

        pre = gain_ref[0:1, at] + conv_ref[0:1, at] * xpad[5 : 5 + length, at]
        for tap in range(1, KW):
            pre = pre + conv_ref[tap : tap + 1, at] * xpad[5 + tap : 5 + tap + length, at]
        conv_sig = jax.nn.sigmoid(pre)
        conv_out = pre * conv_sig
        put(conv_buf, conv_out)
        put(dsilu_buf, conv_sig * (1.0 + pre * (1.0 - conv_sig)))
        raw = dt_ref[:, at] + gain_ref[2:3, at]
        step = jnp.maximum(raw, 0.0) + jnp.log1p(jnp.exp(-jnp.abs(raw)))
        put(step_buf, step)
        put(drive_buf, step * conv_out)
        put(dtsig_buf, jax.nn.sigmoid(raw))
        z_val = z_ref[:, at].astype(f32)
        z_sig = jax.nn.sigmoid(z_val)
        mixed = zfac_buf[:, :, at].reshape(length, LANES)
        gate = z_val * z_sig
        put(zgate_buf, gate)
        put(grad_buf, mixed * gate)
        put(zfac_buf, mixed * z_sig * (1.0 + z_val * (1.0 - z_sig)))
        return 0

    lax.fori_loop(0, channels // LANES, prepare, 0)

    def lanes(k):
        return pl.ds(k * scan, scan)

    def totals(k, low, high, carry):
        at = lanes(k)
        rate = rate_buf[:, at]

        def advance(i, carry):
            state, passed, leaving = carry
            for j in range(GROUP):
                decay = jnp.exp(step_buf[i, j : j + 1, at] * rate)
                decays[i * GROUP + j, :, at] = decay
                state = decay * state + drive_buf[i, j : j + 1, at] * wide(
                    b_wide[i * GROUP + j], scan
                )
                passed = passed * decay
                leaving = leaving + passed * (
                    grad_buf[i, j : j + 1, at] * wide(c_wide[i * GROUP + j], scan)
                )
            return (state, passed, leaving)

        return lax.fori_loop(low, high, advance, carry)

    zero = jnp.zeros((nst, scan), f32)
    nothing = (zero, jnp.ones_like(zero), zero)

    def keep(k, carry):
        for m in range(3):
            tot[k, m] = carry[m].astype(bf16)

    beside = [to(tot.at[k], tsib.at[k], sib, z) for k in range(2)]
    xbit, ybit = lax.rem(lax.div(s, 2), 2), lax.div(s, 4)
    beyond = []
    for k in range(2):
        for m, (seq, bit) in enumerate(((ax, xbit), (ay, ybit), (diag, ybit))):
            at = pl.ds(bit, 2)
            beyond.append(to(tpair.at[k, at], trecv.at[k, m, at], seq, z))

    def join(k):
        beside[k].wait_recv()
        own = [tot[k, m].astype(f32) for m in range(3)]
        their = [tsib[k, m].astype(f32) for m in range(3)]
        one = [jnp.where(core == 0, a, b) for a, b in zip(own, their)]
        two = [jnp.where(core == 0, b, a) for a, b in zip(own, their)]
        tpair[k, 0] = (two[1] * one[0] + two[0]).astype(bf16)
        tpair[k, 1] = (one[1] * two[1]).astype(bf16)
        tpair[k, 2] = (one[2] + one[1] * two[2]).astype(bf16)
        for copy in beyond[3 * k : 3 * k + 3]:
            copy.start()

    def enter(k):
        for copy in beyond[3 * k : 3 * k + 3]:
            copy.wait_recv()
        chip = lax.div(s, 2)
        start, arriving = zero, zero

        def other_chip(c):
            relation = (c % 2 + xbit - 2 * (c % 2) * xbit) + 2 * (c // 2 + ybit - 2 * (c // 2) * ybit)
            return trecv.at[k, jnp.maximum(relation - 1, 0)]

        for c in range(4):
            at = other_chip(c)
            start = jnp.where(c < chip, at[1].astype(f32) * start + at[0].astype(f32), start)
            at = other_chip(3 - c)
            arriving = jnp.where(
                3 - c > chip, at[1].astype(f32) * arriving + at[2].astype(f32), arriving
            )
        passed = tsib[k, 1].astype(f32)
        start = jnp.where(core == 1, passed * start + tsib[k, 0].astype(f32), start)
        arriving = jnp.where(core == 0, passed * arriving + tsib[k, 2].astype(f32), arriving)
        start_buf[:, lanes(k)] = start
        arrive_buf[:, lanes(k)] = arriving

    keep(0, totals(0, 0, groups, nothing))
    beside[0].start()
    middle = totals(1, 0, groups // 2, nothing)
    join(0)
    keep(1, totals(1, groups // 2, groups, middle))
    beside[1].start()
    join(1)

    def state_rows(at, number):
        return pl.ds(pl.multiple_of(at * nst, nst), number * nst)

    def forward(k):
        at = lanes(k)
        states[0:nst, at] = start_buf[:, at].astype(bf16)

        def advance(i, state):
            for j in range(GROUP):
                t = i * GROUP + j
                state = decays[t, :, at] * state + drive_buf[i, j : j + 1, at] * wide(
                    b_wide[t], scan
                )
                states[state_rows(t + 1, 1), at] = state.astype(bf16)
            here = pl.ds(pl.multiple_of(i * GROUP, GROUP), GROUP)
            y_val = jnp.dot(
                c_block[here, :],
                states[state_rows(i * GROUP + 1, GROUP), at],
                preferred_element_type=f32,
            )
            y_val = y_val + gain_ref[1:2, at] * conv_buf[i, :, at]
            gz_ref[here, at] = zfac_buf[i, :, at] * y_val
            gated[here, at] = (zgate_buf[i, :, at] * y_val).astype(bf16)
            return state

        lax.fori_loop(0, groups, advance, start_buf[:, at])

    for k in range(2):
        enter(k)
        forward(k)

    def block(seq, exp):
        return pl.ds(pl.multiple_of(seq * length + exp * rows, rows), rows)

    def within(exp):
        return pl.ds(pl.multiple_of(exp * rows, rows), rows)

    def project(t, _):
        at = pl.ds(pl.multiple_of(t * 256, 256), 256)
        p_buf[:, at] = jnp.dot(gated[...], ow[:, at], preferred_element_type=f32).astype(bf16)
        return 0

    lax.fori_loop(0, width // 256, project, 0)

    z_out = [to(p_buf.at[within(zs[d])], zrecv.at[d - 1], s, zs[d]) for d in (1, 2, 3)]
    for copy in z_out:
        copy.start()

    gb_acc[...] = jnp.zeros_like(gb_acc)
    gc_acc[...] = jnp.zeros_like(gc_acc)

    def backward(k):
        at = lanes(k)

        def retreat(n, carry):
            flow, alog_sum = carry
            i = groups - 1 - n
            for j in reversed(range(GROUP)):
                t = i * GROUP + j
                adjoint = wide(c_wide[t], scan) * grad_buf[i, j : j + 1, at] + flow
                adj[j * nst : (j + 1) * nst, :] = adjoint.astype(bf16)
                flow = decays[t, :, at] * adjoint
                share = rate_buf[:, at] * (flow * states[state_rows(t, 1), at].astype(f32))
                alog_sum = alog_sum + step_buf[i, j : j + 1, at] * share
                quo[j * nst : (j + 1) * nst, :] = share.astype(bf16)
            here = pl.ds(pl.multiple_of(i * GROUP, GROUP), GROUP)
            into_buf[i, :, at] = jnp.dot(b_block[here, :], adj[...], preferred_element_type=f32)
            qsum_buf[i, :, at] = jnp.dot(ones_block, quo[...], preferred_element_type=f32)
            gb_acc[i] += transposed(drive_buf[i, :, at].astype(bf16), adj[...])
            gc_acc[i] += transposed(
                grad_buf[i, :, at].astype(bf16), states[state_rows(i * GROUP + 1, GROUP), at]
            )
            return (flow, alog_sum)

        _, alog_sum = lax.fori_loop(0, groups, retreat, (arrive_buf[:, at], zero))
        sums_own[0:nst, at] = alog_sum

    backward(0)
    backward(1)
    bc_own[0] = jnp.sum(gb_acc[...] * diagonal[None], axis=1)
    bc_own[1] = jnp.sum(gc_acc[...] * diagonal[None], axis=1)
    bc_copies = [to(bc_own, bc_recv.at[d - 1], s, zs[d]) for d in (1, 2, 3)]
    for copy in bc_copies:
        copy.start()

    def finish(t, _):
        at = pl.ds(pl.multiple_of(t * LANES, LANES), LANES)

        def get(ref):
            return ref[:, :, at].reshape(length, LANES)

        def total(value):
            return jnp.sum(value, axis=0, keepdims=True)

        into, conv_out, grad_y = get(into_buf), get(conv_buf), get(grad_buf)
        grad_dt = (get(qsum_buf) + conv_out * into) * get(dtsig_buf)
        gdt_ref[:, at] = grad_dt
        grad_pre = (gain_ref[1:2, at] * grad_y + get(step_buf) * into) * get(dsilu_buf)
        gpad[0:length, at] = grad_pre
        for tap in range(KW):
            sums_own[nst + tap : nst + tap + 1, at] = total(
                grad_pre * xpad[5 + tap : 5 + tap + length, at]
            )
        sums_own[nst + KW : nst + KW + 1, at] = total(grad_pre)
        sums_own[nst + KW + 1 : nst + KW + 2, at] = total(grad_y * conv_out)
        sums_own[nst + KW + 2 : nst + KW + 3, at] = total(grad_dt)
        return 0

    lax.fori_loop(0, channels // LANES, finish, 0)
    sums_own[nst + KW + 3 :, :] = jnp.zeros_like(sums_own[nst + KW + 3 :, :])
    rim = to(gpad.at[pl.ds(0, 8)], ghalo, ahead, z)
    rim.start()
    sums_copies = [
        to(sums_own, sums_recv.at[0], sib, z),
        to(sums_acc.at[0], sums_recv.at[1], ax, z),
        to(sums_acc.at[1], sums_recv.at[2], ay, z),
    ]
    sums_copies[0].start()

    for copy in z_out:
        copy.wait_recv()
    total = resid_ref[...].astype(f32) + p_buf[within(z), :].astype(f32)
    for d in range(3):
        total = total + zrecv[d].astype(f32)
    own_h[...] = total.astype(bf16)
    here = block(s, z)
    rows_all[here, :] = total.astype(bf16)

    gather = [to(rows_all.at[here], rows_all.at[here], s, zs[d]) for d in (1, 2, 3)]
    to_x, to_y, to_b = [], [], []
    for d in range(ways):
        at = rows_all.at[block(s, zb[d])]
        to_x.append(to(at, at, ax, z))
        to_y.append(to(at, at, ay, z))
        to_b.append(to(at, at, sib, z))
    for copy in gather + [to_x[0], to_y[0], to_b[0]]:
        copy.start()

    sums_copies[0].wait_recv()
    sums_acc[0] = sums_own[...] + sums_recv[0]
    sums_copies[1].start()
    rim.wait_recv()
    gpad[length : length + 8, :] = jnp.where(s < seqs - 1, ghalo[...], 0.0)

    def spread_back(t, _):
        at = pl.ds(pl.multiple_of(t * LANES, LANES), LANES)
        grad_x = conv_ref[KW - 1 : KW, at] * gpad[0:length, at]
        for tap in range(KW - 1):
            away = KW - 1 - tap
            grad_x = grad_x + conv_ref[tap : tap + 1, at] * gpad[away : away + length, at]
        gx_ref[:, at] = grad_x
        return 0

    lax.fori_loop(0, channels // LANES, spread_back, 0)

    for d in (1, 2, 3):
        gather[d - 1].wait_recv()
        to_x[d].start()
        to_y[d].start()
        to_b[d].start()

    sums_copies[1].wait_recv()
    sums_acc[1] = sums_acc[0] + sums_recv[1]
    sums_copies[2].start()

    for copy in bc_copies:
        copy.wait_recv()
    bc_out[...] = (bc_own[...] + bc_recv[0]) + (bc_recv[1] + bc_recv[2])

    def chip_rows(seq):
        return pl.ds(pl.multiple_of(lax.div(seq, 2) * (2 * length), 2 * length), 2 * length)

    def up(seq):
        at = chip_rows(seq)

        def tile(t, _):
            both = jnp.dot(
                rows_all[at, :],
                wgu[:, pl.ds(pl.multiple_of(t * 256, 256), 256)],
                preferred_element_type=f32,
            )
            gate, upper = both[:, :128], both[:, 128:]
            value = gate * jax.nn.sigmoid(gate) * upper
            hidden[:, pl.ds(pl.multiple_of(t * 128, 128), 128)] = value.astype(bf16)
            return 0

        lax.fori_loop(0, tiles, tile, 0)

    other = pl.ds(pl.multiple_of((1 - core) * length, length), length)
    mine = pl.ds(pl.multiple_of(core * length, length), length)

    def cols(h):
        return pl.ds(h * half, half)

    pair = {}

    def down(r, h):
        def tile(t, _):
            at = pl.ds(pl.multiple_of(h * half + t * 256, 256), 256)
            part[r, :, at] = jnp.dot(
                hidden[...], wd[:, at], preferred_element_type=f32
            ).astype(bf16)
            return 0

        lax.fori_loop(0, half // 256, tile, 0)
        copy = to(part.at[r, other, cols(h)], psib.at[r, :, cols(h)], sib, z)
        copy.start()
        pair[r, h] = copy

    def paired(r, h):
        pair[r, h].wait_recv()
        acc[r, :, cols(h)] = (
            part[r, mine, cols(h)].astype(f32) + psib[r, :, cols(h)].astype(f32)
        ).astype(bf16)

    for copy in to_b:
        copy.wait_recv()
    for load in loads:
        load.wait()
    up(s)

    for copy in to_x + to_y:
        copy.wait_recv()
    forward = []
    for d in range(ways):
        origin, target = (ay, ax) if d < 2 else (ax, ay)
        at = rows_all.at[block(origin, zb[d])]
        forward.append(to(at, at, target, z))
    for d in (0, 2, 1, 3):
        forward[d].start()

    def all_of(seq):
        return rows_all.at[pl.ds(pl.multiple_of(seq * length, length), length)]

    share_out = [to(all_of(o), all_of(o), sib, z) for k, o in enumerate((ax, ay, diag))]
    share_out[0].start()
    share_out[1].start()

    down(0, 0)
    down(0, 1)
    share_out[0].wait_recv()
    up(ax)
    down(1, 0)
    down(1, 1)
    for copy in forward:
        copy.wait_recv()
    share_out[2].start()
    paired(0, 0)
    paired(0, 1)
    paired(1, 0)
    paired(1, 1)
    send = {}

    def reduce_out(name, src, dst, seq):
        copy = to(src, dst, seq, z)
        copy.start()
        send[name] = copy

    reduce_out("x0", acc.at[1, :, cols(0)], rx.at[:, cols(0)], ax)
    share_out[1].wait_recv()
    up(ay)
    down(2, 0)
    down(2, 1)
    paired(2, 0)
    paired(2, 1)
    reduce_out("y1", acc.at[2, :, cols(1)], ry.at[:, cols(1)], ay)
    share_out[2].wait_recv()
    up(diag)
    down(3, 0)
    down(3, 1)
    paired(3, 0)
    reduce_out("d0", acc.at[3, :, cols(0)], rdx, ax)
    paired(3, 1)
    reduce_out("d1", acc.at[3, :, cols(1)], rdy, ay)

    sums_copies[2].wait_recv()
    sums_out[...] = sums_acc[1] + sums_recv[2]

    send["d0"].wait_recv()
    acc[2, :, cols(0)] = (acc[2, :, cols(0)].astype(f32) + rdx[...].astype(f32)).astype(bf16)
    reduce_out("y0", acc.at[2, :, cols(0)], ry.at[:, cols(0)], ay)
    send["d1"].wait_recv()
    acc[1, :, cols(1)] = (acc[1, :, cols(1)].astype(f32) + rdy[...].astype(f32)).astype(bf16)
    reduce_out("x1", acc.at[1, :, cols(1)], rx.at[:, cols(1)], ax)

    back = []
    for h in range(2):
        send["x%d" % h].wait_recv()
        send["y%d" % h].wait_recv()
        fin[:, cols(h)] = (
            acc[0, :, cols(h)].astype(f32)
            + rx[:, cols(h)].astype(f32)
            + ry[:, cols(h)].astype(f32)
        ).astype(bf16)
        for d in (1, 2, 3):
            copy = to(
                fin.at[within(zs[d]), cols(h)],
                zfin.at[d - 1, :, cols(h)],
                s,
                zs[d],
            )
            copy.start()
            back.append(copy)
    for h in range(2):
        for copy in back[3 * h : 3 * h + 3]:
            copy.wait_recv()
        total = own_h[:, cols(h)].astype(f32)
        total = total + share_ref[z][:, :1] * fin[within(z), cols(h)].astype(f32)
        for d in (1, 2, 3):
            total = total + share_ref[zb[d]][:, :1] * zfin[d - 1, :, cols(h)].astype(f32)
        out_ref[:, cols(h)] = total.astype(bf16)

    for copy in everything:
        copy.wait_send()


def layer(x_in, z_in, dt_raw, bc_in, a_log, taps, gains, resid, share, out_weight, grad_mix, w_gate, w_up, w_down):
    rows, width = resid.shape
    length, channels = x_in.shape
    states = a_log.shape[0]
    units = w_gate.shape[2]
    tiles = units // 128
    seqs = lax.axis_size("seq")
    half, scan, groups = width // 2, channels // 2, length // GROUP
    bf16, f32 = jnp.bfloat16, jnp.float32
    vmem = pl.BlockSpec(memory_space=pltpu.VMEM)
    hbm = pl.BlockSpec(memory_space=pl.ANY)
    sem = pltpu.SemaphoreType.DMA
    flat = GROUP * states

    def held(*shape, kind=f32):
        return pltpu.VMEM(shape, kind)

    def rows_of():
        return held(groups, GROUP, channels)

    summed = (states + 8, channels)
    grads = (2, groups, flat)
    return pl.pallas_call(
        layer_kernel,
        out_shape=[
            jax.ShapeDtypeStruct((rows, width), bf16),
            jax.ShapeDtypeStruct((length, channels), f32),
            jax.ShapeDtypeStruct((length, channels), f32),
            jax.ShapeDtypeStruct((length, channels), f32),
            jax.ShapeDtypeStruct(summed, f32),
            jax.ShapeDtypeStruct(grads, f32),
        ],
        in_specs=[vmem] * 9 + [hbm] * 5,
        out_specs=[vmem] * 6,
        scratch_shapes=[
            held(seqs * length, width, kind=bf16),
            held(width, 2 * units, kind=bf16),
            held(units, width, kind=bf16),
            held(channels, width, kind=bf16),
            held(length, width, kind=bf16),
            held(2 * length, units, kind=bf16),
            held(rows, width, kind=bf16),
            held(3, rows, width, kind=bf16),
            held(3, rows, width, kind=bf16),
            held(4, 2 * length, width, kind=bf16),
            held(4, length, width, kind=bf16),
            held(4, length, width, kind=bf16),
            held(length, width, kind=bf16),
            held(length, width, kind=bf16),
            held(length, half, kind=bf16),
            held(length, half, kind=bf16),
            held(length, width, kind=bf16),
            held(length, width, kind=bf16),
            held(*summed),
            held(3, *summed),
            held(2, *summed),
            held(*grads),
            held(3, *grads),
            held(length, states, channels),
            held((length + 1) * states, channels, kind=bf16),
            held(length, states, LANES),
            held(length, states, LANES),
            held(length, flat, kind=bf16),
            held(length, flat, kind=bf16),
        ]
        + [rows_of() for _ in range(10)]
        + [
            held(length + 8, channels),
            held(length + 8, channels),
            held(GROUP, channels, kind=bf16),
            held(8, channels),
            held(length, channels, kind=bf16),
            held(flat, scan, kind=bf16),
            held(flat, scan, kind=bf16),
            held(groups, GROUP, flat),
            held(groups, GROUP, flat),
            held(2, 3, states, scan, kind=bf16),
            held(2, 3, states, scan, kind=bf16),
            held(2, 3, states, scan, kind=bf16),
            held(2, 3, 3, states, scan, kind=bf16),
            held(states, channels),
            held(states, channels),
            held(states, channels),
            sem((2 * tiles + 3,)),
            sem((2, 80)),
        ],
        compiler_params=pltpu.CompilerParams(
            collective_id=0, has_side_effects=True, vmem_limit_bytes=60 << 20
        ),
        cost_estimate=pl.CostEstimate(
            flops=6 * seqs * length * width * units + 4 * length * width * channels,
            bytes_accessed=6 * width * units,
            transcendentals=seqs * length * units + length * channels * states,
        ),
        name="layer",
    )(x_in, z_in, dt_raw, bc_in, a_log, taps, gains, resid, share, out_weight, grad_mix, w_gate, w_up, w_down)


def entering(everything):
    peers, here = everything.shape[0], lax.axis_index("seq")
    values = everything.astype(jnp.float32)
    start = jnp.zeros_like(values[0, 0])
    arriving = jnp.zeros_like(start)
    for k in range(peers):
        start = jnp.where(k < here, values[k, 0] * start + values[k, 1], start)
        back = peers - 1 - k
        arriving = jnp.where(back > here, values[back, 0] * arriving + values[back, 2], arriving)
    return start, arriving


def routed_experts(partial_value, resid, w_gate, w_up, w_down, route_ids, route_weight):
    rows = resid.shape[0]
    mixed = lax.psum(partial_value, "expert").astype(jnp.float32)
    own = lax.dynamic_slice_in_dim(mixed, lax.axis_index("expert") * rows, rows, 0)
    hidden_in = (resid.astype(jnp.float32) + own).astype(jnp.bfloat16)
    experts = lax.axis_size("expert")
    capacity = 4 * rows // experts
    flat_ids = route_ids.reshape(-1)
    order = jnp.arange(flat_ids.shape[0], dtype=jnp.int32)
    earlier = (flat_ids[:, None] == flat_ids[None, :]) & (order[None, :] < order[:, None])
    rank = jnp.sum(earlier.astype(jnp.int32), axis=1)
    slot = flat_ids * capacity + rank
    placing = (jnp.arange(experts * capacity, dtype=jnp.int32)[:, None] == slot[None, :]).astype(
        jnp.bfloat16
    )
    doubled = jnp.repeat(hidden_in, 2, axis=0)
    outgoing = jnp.dot(placing, doubled, preferred_element_type=jnp.float32).astype(jnp.bfloat16)
    incoming = lax.all_to_all(outgoing, "expert", split_axis=0, concat_axis=0, tiled=True)
    piece = lax.all_gather(incoming, "seq", axis=0, tiled=True)
    gate = jnp.dot(piece, w_gate[0], preferred_element_type=jnp.float32)
    upper = jnp.dot(piece, w_up[0], preferred_element_type=jnp.float32)
    hidden = (jax.nn.silu(gate) * upper).astype(jnp.bfloat16)
    expert_sum = lax.psum_scatter(
        jnp.dot(hidden, w_down[0], preferred_element_type=jnp.float32).astype(jnp.bfloat16),
        "seq",
        scatter_dimension=0,
        tiled=True,
    )
    returned = lax.all_to_all(expert_sum, "expert", split_axis=0, concat_axis=0, tiled=True)
    picked = lax.dot_general(
        placing, returned, (((0,), (0,)), ((), ())), preferred_element_type=jnp.float32
    )
    picked = picked.reshape(rows, 2, -1)
    moe = picked[:, 0] * route_weight[:, 0:1] + picked[:, 1] * route_weight[:, 1:2]
    return (hidden_in.astype(jnp.float32) + moe).astype(jnp.bfloat16)


def local(
    x_in,
    z_in,
    dt_raw,
    bc_in,
    a_log,
    conv_weight,
    conv_bias,
    skip_gain,
    dt_bias,
    out_weight,
    resid,
    w_gate,
    w_up,
    w_down,
    route_ids,
    route_weight,
    grad_mix,
):
    length, channels = x_in.shape
    states = a_log.shape[0]
    rim = KW - 1
    rows = resid.shape[0]
    experts = lax.axis_size("expert")
    if experts == 4 and lax.axis_size("seq") == 8:
        chosen = jnp.arange(experts, dtype=jnp.int32)[:, None, None] == route_ids[None]
        share = jnp.sum(jnp.where(chosen, route_weight[None], 0.0), axis=2, keepdims=True)
        share = jnp.broadcast_to(share, (experts, rows, LANES))
        gains = jnp.stack([conv_bias, skip_gain, dt_bias])
        layer_out, grad_x, grad_z, grad_dt, sums, grad_bc = layer(
            x_in,
            z_in,
            dt_raw,
            bc_in,
            a_log,
            conv_weight,
            gains,
            resid,
            share,
            out_weight,
            grad_mix,
            w_gate,
            w_up,
            w_down,
        )
        grad_bc = grad_bc.reshape(2, length, states).transpose(0, 2, 1)
        return (
            layer_out,
            grad_x,
            grad_z,
            grad_dt,
            grad_bc,
            sums[:states],
            sums[states : states + KW],
            sums[states + KW : states + KW + 3],
        )
    x_val = x_in.astype(jnp.float32)
    z_val = z_in.astype(jnp.float32)
    before = shifted(x_in[length - rim :], "seq", 1)
    padded = jnp.concatenate([before.astype(jnp.float32), x_val], axis=0)
    pre = conv_bias[None, :] + conv_weight[0][None, :] * padded[0:length]
    for tap in range(1, KW):
        pre = pre + conv_weight[tap][None, :] * padded[tap : tap + length]
    conv_sig = jax.nn.sigmoid(pre)
    conv_out = pre * conv_sig
    step = jax.nn.softplus(dt_raw + dt_bias[None, :])
    rate = -jnp.exp(a_log)
    drive = step * conv_out
    z_sig = jax.nn.sigmoid(z_val)
    back_mix = lax.dot_general(
        grad_mix, out_weight, (((1,), (1,)), ((), ())), preferred_element_type=jnp.float32
    )
    grad_y = back_mix * z_val * z_sig

    def grouped(array):
        return array.reshape(length // SUB, SUB, channels)

    def flat(array):
        return array.reshape(length, channels)

    spread = jnp.broadcast_to(
        bc_in.transpose(0, 2, 1)[:, :, :, None], (2, length, states, LANES)
    ).reshape(2, length // SUB, SUB, states, LANES)
    b_wide, c_wide = spread[0], spread[1]
    totals, forward, backward = sweeps(length, channels, states)
    step_g, drive_g, grad_g, conv_g = (grouped(a) for a in (step, drive, grad_y, conv_out))
    own_totals = totals(step_g, drive_g, grad_g, b_wide, c_wide, rate)
    start, arriving = entering(lax.all_gather(own_totals, "seq"))
    y_val = flat(forward(step_g, drive_g, b_wide, c_wide, rate, start))
    y_val = y_val + skip_gain[None, :] * conv_out
    gated = (y_val * z_val * z_sig).astype(jnp.bfloat16)
    partial_value = jnp.dot(gated, out_weight, preferred_element_type=jnp.float32)
    grad_z = back_mix * y_val * z_sig * (1.0 + z_val * (1.0 - z_sig))
    grad_step, conv_part_grad, grad_b, grad_c, grad_alog_local = backward(
        step_g, drive_g, conv_g, grad_g, b_wide, c_wide, rate, start, arriving
    )
    grad_step, conv_part_grad = flat(grad_step), flat(conv_part_grad)
    grad_conv_out = skip_gain[None, :] * grad_y + conv_part_grad
    grad_skip = jnp.sum(grad_y * conv_out, axis=0)
    grad_dt = grad_step * jax.nn.sigmoid(dt_raw + dt_bias[None, :])
    grad_pre = grad_conv_out * (conv_sig * (1.0 + pre * (1.0 - conv_sig)))
    after = shifted(grad_pre[:rim], "seq", -1)
    grad_pad = jnp.concatenate([grad_pre, after], axis=0)
    grad_x = conv_weight[rim][None, :] * grad_pad[0:length]
    for tap in range(rim):
        grad_x = grad_x + conv_weight[tap][None, :] * grad_pad[rim - tap : rim - tap + length]
    grad_taps = jnp.stack(
        [jnp.sum(grad_pre * padded[tap : tap + length], axis=0) for tap in range(KW)]
    )
    channel_grads = jnp.stack([jnp.sum(grad_pre, axis=0), grad_skip, jnp.sum(grad_dt, axis=0)])
    own_sums = jnp.concatenate([grad_alog_local, grad_taps, channel_grads], axis=0)
    own_bc = jnp.stack([jnp.sum(grad_b, axis=-1), jnp.sum(grad_c, axis=-1)])
    own_bc = own_bc.reshape(2, length, states).transpose(0, 2, 1).reshape(2 * states, length)
    layer_out = routed_experts(
        partial_value.astype(jnp.bfloat16),
        resid,
        w_gate,
        w_up,
        w_down,
        route_ids,
        route_weight,
    )
    sums = lax.psum(own_sums, "seq")
    grad_bc = lax.psum(own_bc, "expert").reshape(2, states, length)
    grad_alog = sums[:states]
    grad_conv = sums[states : states + KW]
    grad_chan = sums[states + KW : states + KW + 3]
    return (layer_out, grad_x, grad_z, grad_dt, grad_bc, grad_alog, grad_conv, grad_chan)


def solution(mesh):
    in_specs = (
        P("seq", "expert"),
        P("seq", "expert"),
        P("seq", "expert"),
        P(None, None, "seq"),
        P(None, "expert"),
        P(None, "expert"),
        P("expert"),
        P("expert"),
        P("expert"),
        P("expert", None),
        P(("seq", "expert"), None),
        P("expert", None, "seq"),
        P("expert", None, "seq"),
        P("expert", "seq", None),
        P(("seq", "expert"), None),
        P(("seq", "expert"), None),
        P("seq", None),
    )
    out_specs = (
        P(("seq", "expert"), None),
        P("seq", "expert"),
        P("seq", "expert"),
        P("seq", "expert"),
        P(None, None, "seq"),
        P(None, "expert"),
        P(None, "expert"),
        P(None, "expert"),
    )
    return jax.shard_map(local, mesh=mesh, in_specs=in_specs, out_specs=out_specs, check_vma=False)
```

```python
import functools

import jax
import jax.numpy as jnp
from jax import lax
from jax.experimental import pallas as pl
from jax.experimental.pallas import tpu as pltpu
from jax.sharding import PartitionSpec as P

KW = 4
SUB = 8
LANES = 128


def shifted(x, axis, by):
    peers = lax.axis_size(axis)
    pairs = [(i, i + by) for i in range(peers) if 0 <= i + by < peers]
    return lax.ppermute(x, axis, pairs)


def wide(tile, width):
    return jnp.concatenate([tile] * (width // tile.shape[1]), axis=1)


def folded(value):
    total = value[:, :LANES]
    for at in range(LANES, value.shape[1], LANES):
        total = total + value[:, at : at + LANES]
    return total


def totals_kernel(step_ref, drive_ref, grad_ref, b_ref, c_ref, rate_ref, out_ref):
    rate = rate_ref[...]
    width = rate.shape[1]

    def advance(i, carry):
        state, passed, leaving = carry
        for j in range(SUB):
            decay = jnp.exp(step_ref[i, j : j + 1, :] * rate)
            state = decay * state + drive_ref[i, j : j + 1, :] * wide(b_ref[i, j], width)
            passed = passed * decay
            leaving = leaving + passed * (grad_ref[i, j : j + 1, :] * wide(c_ref[i, j], width))
        return (state, passed, leaving)

    zero = jnp.zeros_like(rate)
    state, passed, leaving = lax.fori_loop(
        0, step_ref.shape[0], advance, (zero, jnp.ones_like(rate), zero)
    )
    out_ref[0] = passed.astype(out_ref.dtype)
    out_ref[1] = state.astype(out_ref.dtype)
    out_ref[2] = leaving.astype(out_ref.dtype)


def forward_kernel(step_ref, drive_ref, b_ref, c_ref, rate_ref, start_ref, y_ref):
    rate = rate_ref[...]
    width = rate.shape[1]

    def advance(i, state):
        for j in range(SUB):
            decay = jnp.exp(step_ref[i, j : j + 1, :] * rate)
            state = decay * state + drive_ref[i, j : j + 1, :] * wide(b_ref[i, j], width)
            y_ref[i, j : j + 1, :] = jnp.sum(
                wide(c_ref[i, j], width) * state, axis=0, keepdims=True
            )
        return state

    lax.fori_loop(0, step_ref.shape[0], advance, start_ref[...])


def backward_kernel(
    step_ref,
    drive_ref,
    conv_ref,
    grad_ref,
    b_ref,
    c_ref,
    rate_ref,
    start_ref,
    arriving_ref,
    step_out_ref,
    conv_out_ref,
    b_out_ref,
    c_out_ref,
    alog_ref,
    states,
):
    rate = rate_ref[...]
    width = rate.shape[1]
    groups = step_ref.shape[0]

    @pl.when(pl.program_id(0) == 0)
    def _():
        b_out_ref[...] = jnp.zeros_like(b_out_ref)
        c_out_ref[...] = jnp.zeros_like(c_out_ref)

    states[0] = start_ref[...]

    def advance(i, state):
        for j in range(SUB):
            decay = jnp.exp(step_ref[i, j : j + 1, :] * rate)
            state = decay * state + drive_ref[i, j : j + 1, :] * wide(b_ref[i, j], width)
            states[i * SUB + j + 1] = state
        return state

    lax.fori_loop(0, groups, advance, start_ref[...])

    def retreat(k, carry):
        flow, alog_sum = carry
        i = groups - 1 - k
        for j in reversed(range(SUB)):
            at = i * SUB + j
            step_now = step_ref[i, j : j + 1, :]
            grad_now = grad_ref[i, j : j + 1, :]
            decay = jnp.exp(step_now * rate)
            adjoint = wide(c_ref[i, j], width) * grad_now + flow
            flow = decay * adjoint
            held = flow * states[at]
            alog_sum = alog_sum + step_now * held
            into_drive = jnp.sum(adjoint * wide(b_ref[i, j], width), axis=0, keepdims=True)
            step_out_ref[i, j : j + 1, :] = (
                jnp.sum(rate * held, axis=0, keepdims=True)
                + conv_ref[i, j : j + 1, :] * into_drive
            )
            conv_out_ref[i, j : j + 1, :] = step_now * into_drive
            b_out_ref[i, j] += folded(adjoint * drive_ref[i, j : j + 1, :])
            c_out_ref[i, j] += folded(grad_now * states[at + 1])
        return (flow, alog_sum)

    _, alog_sum = lax.fori_loop(0, groups, retreat, (arriving_ref[...], jnp.zeros_like(rate)))
    alog_ref[...] = alog_sum * rate


def sweeps(length, channels, states):
    block = min(512, channels)
    groups = length // SUB
    rows = pl.BlockSpec((groups, SUB, block), lambda k: (0, 0, k))
    spread = pl.BlockSpec((groups, SUB, states, LANES), lambda k: (0, 0, 0, 0))
    column = pl.BlockSpec((states, block), lambda k: (0, k))
    grid = (channels // block,)
    f32 = jnp.float32
    row_shape = jax.ShapeDtypeStruct((groups, SUB, channels), f32)
    spread_shape = jax.ShapeDtypeStruct((groups, SUB, states, LANES), f32)
    column_shape = jax.ShapeDtypeStruct((states, channels), f32)
    totals = pl.pallas_call(
        totals_kernel,
        grid=grid,
        in_specs=[rows, rows, rows, spread, spread, column],
        out_specs=pl.BlockSpec((3, states, block), lambda k: (0, 0, k)),
        out_shape=jax.ShapeDtypeStruct((3, states, channels), jnp.bfloat16),
        name="totals",
    )
    forward = pl.pallas_call(
        forward_kernel,
        grid=grid,
        in_specs=[rows, rows, spread, spread, column, column],
        out_specs=rows,
        out_shape=row_shape,
        name="forward",
    )
    backward = pl.pallas_call(
        backward_kernel,
        grid=grid,
        in_specs=[rows, rows, rows, rows, spread, spread, column, column, column],
        out_specs=[rows, rows, spread, spread, column],
        out_shape=[row_shape, row_shape, spread_shape, spread_shape, column_shape],
        scratch_shapes=[pltpu.VMEM((length + 1, states, block), f32)],
        name="backward",
    )
    return totals, forward, backward


MESH = pl.DeviceIdType.MESH
GROUP = 16


def places():
    s, z = lax.axis_index("seq"), lax.axis_index("expert")
    core = lax.rem(s, 2)
    sib = s + 1 - 2 * core
    across_x = s + 2 - 4 * lax.rem(lax.div(s, 2), 2)
    across_y = s + 4 - 8 * lax.div(s, 4)
    return s, z, core, sib, across_x, across_y


def transposed(a, b):
    return lax.dot_general(a, b, (((1,), (1,)), ((), ())), preferred_element_type=jnp.float32)


def layer_kernel(
    x_ref,
    z_ref,
    dt_ref,
    bc_ref,
    alog_ref,
    conv_ref,
    bias_ref,
    gain_ref,
    dtb_ref,
    resid_ref,
    ids_ref,
    weight_ref,
    ow_hbm,
    gm_hbm,
    wg_hbm,
    wu_hbm,
    wd_hbm,
    out_ref,
    gx_ref,
    gz_ref,
    gdt_ref,
    alog_out,
    taps_out,
    chan_out,
    bc_out,
    gx_buf,
    gz_buf,
    gdt_buf,
    rows_all,
    wgu,
    wd,
    ow,
    gm,
    hidden,
    own_h,
    zrecv,
    zfin,
    part,
    psib,
    acc,
    rx,
    ry,
    rdx,
    rdy,
    fin,
    p_buf,
    sums_own,
    sums_recv,
    sums_acc,
    bc_own,
    bc_recv,
    decays,
    states,
    b_wide,
    c_wide,
    b_block,
    c_block,
    step_buf,
    drive_buf,
    conv_buf,
    grad_buf,
    dsilu_buf,
    dtsig_buf,
    zgate_buf,
    zfac_buf,
    into_buf,
    qsum_buf,
    xpad,
    gpad,
    xhalo,
    ghalo,
    gated,
    adj,
    quo,
    gb_acc,
    gc_acc,
    tot,
    tsib,
    tpair,
    trecv,
    rate_buf,
    start_buf,
    arrive_buf,
    w_sem,
    sems,
):
    s, z, core, sib, ax, ay = places()
    diag = ax + ay - s
    f32, bf16 = jnp.float32, jnp.bfloat16
    ways, seqs = 4, 8
    rows = resid_ref.shape[0]
    length, channels = x_ref.shape
    width = resid_ref.shape[1]
    half = width // 2
    scan = channels // 2
    groups = length // GROUP
    nst = alog_ref.shape[0]
    flat = GROUP * nst
    tiles = wgu.shape[1] // 256
    after = lax.rem(s + 1, seqs)
    ahead = lax.rem(s + seqs - 1, seqs)
    count = [0]
    everything = []

    def to(src, dst, seq, exp):
        index = count[0]
        count[0] += 1
        copy = pltpu.make_async_remote_copy(
            src_ref=src,
            dst_ref=dst,
            send_sem=sems.at[0, index],
            recv_sem=sems.at[1, index],
            device_id=(seq, exp),
            device_id_type=MESH,
        )
        everything.append(copy)
        return copy

    first = [
        pltpu.make_async_copy(ow_hbm, ow, w_sem.at[0]),
        pltpu.make_async_copy(gm_hbm, gm, w_sem.at[1]),
    ]
    for load in first:
        load.start()
    loads = []
    for t in range(tiles):
        for k, w_hbm in enumerate((wg_hbm, wu_hbm)):
            loads.append(
                pltpu.make_async_copy(
                    w_hbm.at[0, :, pl.ds(t * 128, 128)],
                    wgu.at[:, pl.ds(t * 256 + k * 128, 128)],
                    w_sem.at[2 + 2 * t + k],
                )
            )
    loads.append(pltpu.make_async_copy(wd_hbm.at[0], wd, w_sem.at[2 + 2 * tiles]))

    zs = [lax.rem(z + d, ways) for d in range(ways)]
    zb = [lax.rem(z + ways - d, ways) for d in range(ways)]

    barrier = pltpu.get_barrier_semaphore()
    partners = [(sib, z), (ax, z), (ay, z), (diag, z), (after, z), (ahead, z)]
    partners += [(s, zs[1]), (s, zs[2]), (s, zs[3])]
    for seq, exp in partners:
        pl.semaphore_signal(barrier, inc=1, device_id=(seq, exp), device_id_type=MESH)
    pl.semaphore_wait(barrier, len(partners))

    halo = to(x_ref.at[pl.ds(length - GROUP, GROUP), :], xhalo, after, z)
    halo.start()

    for k, spread in enumerate((b_wide, c_wide)):
        value = bc_ref[k]
        for t in range(length):
            spread[t] = jnp.broadcast_to(value[:, t : t + 1], (nst, LANES))
    lane = lax.broadcasted_iota(jnp.int32, (length, flat), 1)
    row = lax.broadcasted_iota(jnp.int32, (length, flat), 0)
    same_token = lax.div(lane, nst) == lax.rem(row, GROUP)
    lane_r = lax.broadcasted_iota(jnp.int32, (nst, flat), 1)
    row_r = lax.broadcasted_iota(jnp.int32, (nst, flat), 0)
    unit = (lax.rem(lane_r, nst) == row_r).astype(f32)
    repeat = unit.astype(bf16)
    for k, block_ref in enumerate((b_block, c_block)):
        by_token = jnp.transpose(bc_ref[k]).astype(bf16)
        laid = jnp.dot(by_token, repeat, preferred_element_type=f32)
        block_ref[...] = jnp.where(same_token, laid, 0.0).astype(bf16)
    diagonal = same_token[:GROUP].astype(f32)
    ones_block = diagonal.astype(bf16)
    rate_buf[...] = -jnp.exp(alog_ref[...])

    for load in first:
        load.wait()

    def mix_tile(t, _):
        at = pl.ds(pl.multiple_of(t * 256, 256), 256)
        zfac_buf[:, :, at] = transposed(gm[...], ow[at, :]).reshape(groups, GROUP, 256)
        return 0

    lax.fori_loop(0, channels // 256, mix_tile, 0, unroll=True)
    for load in loads:
        load.start()
    xpad[8 : 8 + length, :] = x_ref[...].astype(f32)
    halo.wait_recv()
    xpad[0:8, :] = jnp.where(s > 0, xhalo[...].astype(f32)[GROUP - 8 :], 0.0)

    def prepare(t, _):
        at = pl.ds(pl.multiple_of(t * LANES, LANES), LANES)

        def put(ref, value):
            ref[:, :, at] = value.reshape(groups, GROUP, LANES)

        pre = bias_ref[:, at] + conv_ref[0:1, at] * xpad[5 : 5 + length, at]
        for tap in range(1, KW):
            pre = pre + conv_ref[tap : tap + 1, at] * xpad[5 + tap : 5 + tap + length, at]
        conv_sig = jax.nn.sigmoid(pre)
        conv_out = pre * conv_sig
        put(conv_buf, conv_out)
        put(dsilu_buf, conv_sig * (1.0 + pre * (1.0 - conv_sig)))
        raw = dt_ref[:, at] + dtb_ref[:, at]
        step = jnp.maximum(raw, 0.0) + jnp.log1p(jnp.exp(-jnp.abs(raw)))
        put(step_buf, step)
        put(drive_buf, step * conv_out)
        put(dtsig_buf, jax.nn.sigmoid(raw))
        z_val = z_ref[:, at].astype(f32)
        z_sig = jax.nn.sigmoid(z_val)
        mixed = zfac_buf[:, :, at].reshape(length, LANES)
        gate = z_val * z_sig
        put(zgate_buf, gate)
        put(grad_buf, mixed * gate)
        put(zfac_buf, mixed * z_sig * (1.0 + z_val * (1.0 - z_sig)))
        return 0

    lax.fori_loop(0, channels // LANES, prepare, 0)

    def lanes(k):
        return pl.ds(k * scan, scan)

    def totals(k, low, high, carry):
        at = lanes(k)
        rate = rate_buf[:, at]

        def advance(i, carry):
            state, passed, leaving = carry
            for j in range(GROUP):
                decay = jnp.exp(step_buf[i, j : j + 1, at] * rate)
                decays[i * GROUP + j, :, at] = decay
                state = decay * state + drive_buf[i, j : j + 1, at] * wide(
                    b_wide[i * GROUP + j], scan
                )
                passed = passed * decay
                leaving = leaving + passed * (
                    grad_buf[i, j : j + 1, at] * wide(c_wide[i * GROUP + j], scan)
                )
            return (state, passed, leaving)

        return lax.fori_loop(low, high, advance, carry)

    zero = jnp.zeros((nst, scan), f32)
    nothing = (zero, jnp.ones_like(zero), zero)

    def keep(k, carry):
        for m in range(3):
            tot[k, m] = carry[m].astype(bf16)

    beside = [to(tot.at[k], tsib.at[k], sib, z) for k in range(2)]
    xbit, ybit = lax.rem(lax.div(s, 2), 2), lax.div(s, 4)
    beyond = []
    for k in range(2):
        for m, (seq, bit) in enumerate(((ax, xbit), (ay, ybit), (diag, ybit))):
            at = pl.ds(bit, 2)
            beyond.append(to(tpair.at[k, at], trecv.at[k, m, at], seq, z))

    def join(k):
        beside[k].wait_recv()
        own = [tot[k, m].astype(f32) for m in range(3)]
        their = [tsib[k, m].astype(f32) for m in range(3)]
        one = [jnp.where(core == 0, a, b) for a, b in zip(own, their)]
        two = [jnp.where(core == 0, b, a) for a, b in zip(own, their)]
        tpair[k, 0] = (two[1] * one[0] + two[0]).astype(bf16)
        tpair[k, 1] = (one[1] * two[1]).astype(bf16)
        tpair[k, 2] = (one[2] + one[1] * two[2]).astype(bf16)
        for copy in beyond[3 * k : 3 * k + 3]:
            copy.start()

    def enter(k):
        for copy in beyond[3 * k : 3 * k + 3]:
            copy.wait_recv()
        chip = lax.div(s, 2)
        start, arriving = zero, zero

        def other_chip(c):
            relation = (c % 2 + xbit - 2 * (c % 2) * xbit) + 2 * (c // 2 + ybit - 2 * (c // 2) * ybit)
            return trecv.at[k, jnp.maximum(relation - 1, 0)]

        for c in range(4):
            at = other_chip(c)
            start = jnp.where(c < chip, at[1].astype(f32) * start + at[0].astype(f32), start)
            at = other_chip(3 - c)
            arriving = jnp.where(
                3 - c > chip, at[1].astype(f32) * arriving + at[2].astype(f32), arriving
            )
        passed = tsib[k, 1].astype(f32)
        start = jnp.where(core == 1, passed * start + tsib[k, 0].astype(f32), start)
        arriving = jnp.where(core == 0, passed * arriving + tsib[k, 2].astype(f32), arriving)
        start_buf[:, lanes(k)] = start
        arrive_buf[:, lanes(k)] = arriving

    keep(0, totals(0, 0, groups, nothing))
    beside[0].start()
    middle = totals(1, 0, groups // 2, nothing)
    join(0)
    keep(1, totals(1, groups // 2, groups, middle))
    beside[1].start()
    join(1)

    def state_rows(at, number):
        return pl.ds(pl.multiple_of(at * nst, nst), number * nst)

    def forward(k):
        at = lanes(k)
        states[0:nst, at] = start_buf[:, at].astype(bf16)

        def advance(i, state):
            for j in range(GROUP):
                t = i * GROUP + j
                state = decays[t, :, at] * state + drive_buf[i, j : j + 1, at] * wide(
                    b_wide[t], scan
                )
                states[state_rows(t + 1, 1), at] = state.astype(bf16)
            here = pl.ds(pl.multiple_of(i * GROUP, GROUP), GROUP)
            y_val = jnp.dot(
                c_block[here, :],
                states[state_rows(i * GROUP + 1, GROUP), at],
                preferred_element_type=f32,
            )
            y_val = y_val + gain_ref[:, at] * conv_buf[i, :, at]
            gz_buf[here, at] = zfac_buf[i, :, at] * y_val
            gated[here, at] = (zgate_buf[i, :, at] * y_val).astype(bf16)
            return state

        lax.fori_loop(0, groups, advance, start_buf[:, at])

    for k in range(2):
        enter(k)
        forward(k)

    written = [
        pltpu.make_async_copy(gz_buf, gz_ref, w_sem.at[3 + 2 * tiles]),
        pltpu.make_async_copy(gdt_buf, gdt_ref, w_sem.at[4 + 2 * tiles]),
        pltpu.make_async_copy(gx_buf, gx_ref, w_sem.at[5 + 2 * tiles]),
    ]
    written[0].start()

    def block(seq, exp):
        return pl.ds(pl.multiple_of(seq * length + exp * rows, rows), rows)

    def within(exp):
        return pl.ds(pl.multiple_of(exp * rows, rows), rows)

    def project(t, _):
        at = pl.ds(pl.multiple_of(t * 256, 256), 256)
        p_buf[:, at] = jnp.dot(gated[...], ow[:, at], preferred_element_type=f32).astype(bf16)
        return 0

    lax.fori_loop(0, width // 256, project, 0, unroll=True)

    z_out = [to(p_buf.at[within(zs[d])], zrecv.at[d - 1], s, zs[d]) for d in (1, 2, 3)]
    for copy in z_out:
        copy.start()

    gb_acc[...] = jnp.zeros_like(gb_acc)
    gc_acc[...] = jnp.zeros_like(gc_acc)

    def backward(k):
        at = lanes(k)

        def retreat(n, carry):
            flow, alog_sum = carry
            i = groups - 1 - n
            for j in reversed(range(GROUP)):
                t = i * GROUP + j
                adjoint = wide(c_wide[t], scan) * grad_buf[i, j : j + 1, at] + flow
                adj[j * nst : (j + 1) * nst, :] = adjoint.astype(bf16)
                flow = decays[t, :, at] * adjoint
                share = rate_buf[:, at] * (flow * states[state_rows(t, 1), at].astype(f32))
                alog_sum = alog_sum + step_buf[i, j : j + 1, at] * share
                quo[j * nst : (j + 1) * nst, :] = share.astype(bf16)
            here = pl.ds(pl.multiple_of(i * GROUP, GROUP), GROUP)
            into_buf[i, :, at] = jnp.dot(b_block[here, :], adj[...], preferred_element_type=f32)
            qsum_buf[i, :, at] = jnp.dot(ones_block, quo[...], preferred_element_type=f32)
            gb_acc[i] += transposed(drive_buf[i, :, at].astype(bf16), adj[...])
            gc_acc[i] += transposed(
                grad_buf[i, :, at].astype(bf16), states[state_rows(i * GROUP + 1, GROUP), at]
            )
            return (flow, alog_sum)

        _, alog_sum = lax.fori_loop(0, groups, retreat, (arrive_buf[:, at], zero))
        sums_own[0:nst, at] = alog_sum

    backward(0)
    backward(1)
    for k, held in enumerate((gb_acc, gc_acc)):
        kept = jnp.where(same_token, held[...].reshape(length, flat), 0.0)
        bc_own[k] = lax.dot_general(
            unit,
            kept,
            (((1,), (1,)), ((), ())),
            precision=lax.Precision.HIGHEST,
            preferred_element_type=f32,
        )
    bc_copies = [to(bc_own, bc_recv.at[d - 1], s, zs[d]) for d in (1, 2, 3)]
    for copy in bc_copies:
        copy.start()

    def finish(t, _):
        at = pl.ds(pl.multiple_of(t * LANES, LANES), LANES)

        def get(ref):
            return ref[:, :, at].reshape(length, LANES)

        def total(value):
            return jnp.sum(value, axis=0, keepdims=True)

        into, conv_out, grad_y = get(into_buf), get(conv_buf), get(grad_buf)
        grad_dt = (get(qsum_buf) + conv_out * into) * get(dtsig_buf)
        gdt_buf[:, at] = grad_dt
        grad_pre = (gain_ref[:, at] * grad_y + get(step_buf) * into) * get(dsilu_buf)
        gpad[0:length, at] = grad_pre
        for tap in range(KW):
            sums_own[nst + tap : nst + tap + 1, at] = total(
                grad_pre * xpad[5 + tap : 5 + tap + length, at]
            )
        sums_own[nst + KW : nst + KW + 1, at] = total(grad_pre)
        sums_own[nst + KW + 1 : nst + KW + 2, at] = total(grad_y * conv_out)
        sums_own[nst + KW + 2 : nst + KW + 3, at] = total(grad_dt)
        return 0

    lax.fori_loop(0, channels // LANES, finish, 0)
    written[1].start()
    sums_own[nst + KW + 3 :, :] = jnp.zeros_like(sums_own[nst + KW + 3 :, :])
    rim = to(gpad.at[pl.ds(0, 8)], ghalo, ahead, z)
    rim.start()
    sums_copies = [
        to(sums_own, sums_recv.at[0], sib, z),
        to(sums_acc.at[0], sums_recv.at[1], ax, z),
        to(sums_acc.at[1], sums_recv.at[2], ay, z),
    ]
    sums_copies[0].start()

    for copy in z_out:
        copy.wait_recv()
    total = resid_ref[...].astype(f32) + p_buf[within(z), :].astype(f32)
    for d in range(3):
        total = total + zrecv[d].astype(f32)
    own_h[...] = total.astype(bf16)
    here = block(s, z)
    rows_all[here, :] = total.astype(bf16)

    gather = [to(rows_all.at[here], rows_all.at[here], s, zs[d]) for d in (1, 2, 3)]
    to_x, to_y, to_b = [], [], []
    for d in range(ways):
        at = rows_all.at[block(s, zb[d])]
        to_x.append(to(at, at, ax, z))
        to_y.append(to(at, at, ay, z))
        to_b.append(to(at, at, sib, z))
    for copy in gather + [to_x[0], to_y[0], to_b[0]]:
        copy.start()

    sums_copies[0].wait_recv()
    sums_acc[0] = sums_own[...] + sums_recv[0]
    sums_copies[1].start()
    rim.wait_recv()
    gpad[length : length + 8, :] = jnp.where(s < seqs - 1, ghalo[...], 0.0)

    def spread_back(t, _):
        at = pl.ds(pl.multiple_of(t * LANES, LANES), LANES)
        grad_x = conv_ref[KW - 1 : KW, at] * gpad[0:length, at]
        for tap in range(KW - 1):
            away = KW - 1 - tap
            grad_x = grad_x + conv_ref[tap : tap + 1, at] * gpad[away : away + length, at]
        gx_buf[:, at] = grad_x
        return 0

    lax.fori_loop(0, channels // LANES, spread_back, 0)
    written[2].start()

    forward = []
    for d in range(ways):
        origin, target = (ay, ax) if d < 2 else (ax, ay)
        at = rows_all.at[block(origin, zb[d])]
        forward.append(to(at, at, target, z))
    to_y[0].wait_recv()
    forward[0].start()

    for d in (1, 2, 3):
        gather[d - 1].wait_recv()
        to_x[d].start()
        to_y[d].start()
        to_b[d].start()

    sums_copies[1].wait_recv()
    sums_acc[1] = sums_acc[0] + sums_recv[1]
    sums_copies[2].start()

    for copy in bc_copies:
        copy.wait_recv()
    bc_out[...] = (bc_own[...] + bc_recv[0]) + (bc_recv[1] + bc_recv[2])

    def chip_rows(seq):
        return pl.ds(pl.multiple_of(lax.div(seq, 2) * (2 * length), 2 * length), 2 * length)

    def up(seq):
        at = chip_rows(seq)

        def tile(t, _):
            both = jnp.dot(
                rows_all[at, :],
                wgu[:, pl.ds(pl.multiple_of(t * 256, 256), 256)],
                preferred_element_type=f32,
            )
            gate, upper = both[:, :128], both[:, 128:]
            value = gate * jax.nn.sigmoid(gate) * upper
            hidden[:, pl.ds(pl.multiple_of(t * 128, 128), 128)] = value.astype(bf16)
            return 0

        lax.fori_loop(0, tiles, tile, 0, unroll=True)

    other = pl.ds(pl.multiple_of((1 - core) * length, length), length)
    mine = pl.ds(pl.multiple_of(core * length, length), length)

    quarter = width // 4

    def cols(h):
        return pl.ds(h * quarter, quarter)

    pair = {}

    def down(r, h):
        part[r, :, cols(h)] = jnp.dot(
            hidden[...], wd[:, cols(h)], preferred_element_type=f32
        ).astype(bf16)
        copy = to(part.at[r, other, cols(h)], psib.at[r, :, cols(h)], sib, z)
        copy.start()
        pair[r, h] = copy

    def paired(r, h):
        pair[r, h].wait_recv()
        acc[r, :, cols(h)] = (
            part[r, mine, cols(h)].astype(f32) + psib[r, :, cols(h)].astype(f32)
        ).astype(bf16)

    for copy in to_b:
        copy.wait_recv()
    for load in loads:
        load.wait()
    up(s)

    to_y[1].wait_recv()
    forward[1].start()
    to_x[2].wait_recv()
    forward[2].start()
    down(0, 0)
    down(0, 1)
    to_x[3].wait_recv()
    forward[3].start()

    def all_of(seq):
        return rows_all.at[pl.ds(pl.multiple_of(seq * length, length), length)]

    share_out = [to(all_of(o), all_of(o), sib, z) for o in (ax, ay, diag)]
    to_x[0].wait_recv()
    to_x[1].wait_recv()
    share_out[0].start()
    to_y[2].wait_recv()
    to_y[3].wait_recv()
    share_out[1].start()
    down(0, 2)
    down(0, 3)
    share_out[0].wait_recv()
    up(ax)
    for h in range(4):
        down(1, h)
    for copy in forward:
        copy.wait_recv()
    share_out[2].start()
    send = {}

    def reduce_out(name, src, dst, seq):
        copy = to(src, dst, seq, z)
        copy.start()
        send[name] = copy

    def small(h):
        return pl.ds((h % 2) * quarter, quarter)

    for h in (0, 1):
        paired(1, h)
        reduce_out("x%d" % h, acc.at[1, :, cols(h)], rx.at[:, cols(h)], ax)
    share_out[1].wait_recv()
    up(ay)
    for h in (2, 3, 0, 1):
        down(2, h)
    for h in (2, 3):
        paired(1, h)
        paired(2, h)
        reduce_out("y%d" % h, acc.at[2, :, cols(h)], ry.at[:, cols(h)], ay)
    share_out[2].wait_recv()
    up(diag)

    def pass_on(h):
        paired(3, h)
        if h < 2:
            reduce_out("d%d" % h, acc.at[3, :, cols(h)], rdx.at[:, small(h)], ax)
        else:
            reduce_out("d%d" % h, acc.at[3, :, cols(h)], rdy.at[:, small(h)], ay)

    down(3, 0)
    down(3, 2)
    pass_on(0)
    down(3, 1)
    pass_on(2)
    down(3, 3)
    pass_on(1)
    pass_on(3)
    for h in (0, 1):
        paired(2, h)
    for h in range(4):
        paired(0, h)

    sums_copies[2].wait_recv()
    summed = sums_acc[1] + sums_recv[2]
    alog_out[...] = summed[:nst]
    taps_out[...] = summed[nst : nst + KW]
    chan_out[...] = summed[nst + KW : nst + KW + 3]

    for h in (0, 2, 1, 3):
        send["d%d" % h].wait_recv()
        r, got = (2, rdx) if h < 2 else (1, rdy)
        acc[r, :, cols(h)] = (
            acc[r, :, cols(h)].astype(f32) + got[:, small(h)].astype(f32)
        ).astype(bf16)
        if h < 2:
            reduce_out("y%d" % h, acc.at[2, :, cols(h)], ry.at[:, cols(h)], ay)
        else:
            reduce_out("x%d" % h, acc.at[1, :, cols(h)], rx.at[:, cols(h)], ax)

    ids, weight = ids_ref[...], weight_ref[...]
    shares = [
        jnp.where(ids[:, 0:1] == zb[d], weight[:, 0:1], 0.0)
        + jnp.where(ids[:, 1:2] == zb[d], weight[:, 1:2], 0.0)
        for d in range(ways)
    ]
    back = {}
    for h in (0, 2, 1, 3):
        send["x%d" % h].wait_recv()
        send["y%d" % h].wait_recv()
        fin[:, cols(h)] = (
            acc[0, :, cols(h)].astype(f32)
            + rx[:, cols(h)].astype(f32)
            + ry[:, cols(h)].astype(f32)
        ).astype(bf16)
        for d in (1, 2, 3):
            copy = to(fin.at[within(zs[d]), cols(h)], zfin.at[d - 1, :, cols(h)], s, zs[d])
            copy.start()
            back[h, d] = copy
    for h in (0, 2, 1, 3):
        total = own_h[:, cols(h)].astype(f32)
        total = total + shares[0] * fin[within(z), cols(h)].astype(f32)
        for d in (1, 2, 3):
            back[h, d].wait_recv()
            total = total + shares[d] * zfin[d - 1, :, cols(h)].astype(f32)
        out_ref[:, cols(h)] = total.astype(bf16)

    for copy in written:
        copy.wait()
    for copy in everything:
        copy.wait_send()


def deliver_kernel(number, *refs):
    sem = refs[2 * number]
    copies = [
        pltpu.make_async_copy(refs[k], refs[number + k], sem.at[k]) for k in range(number)
    ]
    for copy in copies:
        copy.start()
    for copy in copies:
        copy.wait()


def deliver(arrays):
    number = len(arrays)
    anywhere = pl.BlockSpec(memory_space=pl.ANY)
    return pl.pallas_call(
        functools.partial(deliver_kernel, number),
        out_shape=[jax.ShapeDtypeStruct(a.shape, a.dtype) for a in arrays],
        in_specs=[anywhere] * number,
        out_specs=[anywhere] * number,
        scratch_shapes=[pltpu.SemaphoreType.DMA((number,))],
        name="deliver",
    )(*arrays)


def layer(
    x_in,
    z_in,
    dt_raw,
    bc_in,
    a_log,
    taps,
    bias,
    gain,
    dt_bias,
    resid,
    route_ids,
    route_weight,
    out_weight,
    grad_mix,
    w_gate,
    w_up,
    w_down,
):
    rows, width = resid.shape
    length, channels = x_in.shape
    states = a_log.shape[0]
    units = w_gate.shape[2]
    tiles = units // 128
    seqs = lax.axis_size("seq")
    half, scan, groups = width // 2, channels // 2, length // GROUP
    bf16, f32 = jnp.bfloat16, jnp.float32
    vmem = pl.BlockSpec(memory_space=pltpu.VMEM)
    hbm = pl.BlockSpec(memory_space=pl.ANY)
    sem = pltpu.SemaphoreType.DMA
    flat = GROUP * states

    def held(*shape, kind=f32):
        return pltpu.VMEM(shape, kind)

    def rows_of():
        return held(groups, GROUP, channels)

    summed = (states + 8, channels)
    grads = (2, states, length)
    return pl.pallas_call(
        layer_kernel,
        out_shape=[
            jax.ShapeDtypeStruct((rows, width), bf16),
            jax.ShapeDtypeStruct((length, channels), f32),
            jax.ShapeDtypeStruct((length, channels), f32),
            jax.ShapeDtypeStruct((length, channels), f32),
            jax.ShapeDtypeStruct((states, channels), f32),
            jax.ShapeDtypeStruct((KW, channels), f32),
            jax.ShapeDtypeStruct((3, channels), f32),
            jax.ShapeDtypeStruct(grads, f32),
        ],
        in_specs=[vmem] * 12 + [hbm] * 5,
        out_specs=[vmem] + [hbm] * 3 + [vmem] * 4,
        scratch_shapes=[
            held(length, channels),
            held(length, channels),
            held(length, channels),
            held(seqs * length, width, kind=bf16),
            held(width, 2 * units, kind=bf16),
            held(units, width, kind=bf16),
            held(channels, width, kind=bf16),
            held(length, width, kind=bf16),
            held(2 * length, units, kind=bf16),
            held(rows, width, kind=bf16),
            held(3, rows, width, kind=bf16),
            held(3, rows, width, kind=bf16),
            held(4, 2 * length, width, kind=bf16),
            held(4, length, width, kind=bf16),
            held(4, length, width, kind=bf16),
            held(length, width, kind=bf16),
            held(length, width, kind=bf16),
            held(length, half, kind=bf16),
            held(length, half, kind=bf16),
            held(length, width, kind=bf16),
            held(length, width, kind=bf16),
            held(*summed),
            held(3, *summed),
            held(2, *summed),
            held(*grads),
            held(3, *grads),
            held(length, states, channels),
            held((length + 1) * states, channels, kind=bf16),
            held(length, states, LANES),
            held(length, states, LANES),
            held(length, flat, kind=bf16),
            held(length, flat, kind=bf16),
        ]
        + [rows_of() for _ in range(10)]
        + [
            held(length + 8, channels),
            held(length + 8, channels),
            held(GROUP, channels, kind=bf16),
            held(8, channels),
            held(length, channels, kind=bf16),
            held(flat, scan, kind=bf16),
            held(flat, scan, kind=bf16),
            held(groups, GROUP, flat),
            held(groups, GROUP, flat),
            held(2, 3, states, scan, kind=bf16),
            held(2, 3, states, scan, kind=bf16),
            held(2, 3, states, scan, kind=bf16),
            held(2, 3, 3, states, scan, kind=bf16),
            held(states, channels),
            held(states, channels),
            held(states, channels),
            sem((2 * tiles + 6,)),
            sem((2, 112)),
        ],
        compiler_params=pltpu.CompilerParams(
            collective_id=0, has_side_effects=True, vmem_limit_bytes=60 << 20
        ),
        cost_estimate=pl.CostEstimate(
            flops=6 * seqs * length * width * units + 4 * length * width * channels,
            bytes_accessed=6 * width * units,
            transcendentals=seqs * length * units + length * channels * states,
        ),
        name="layer",
    )(
        x_in,
        z_in,
        dt_raw,
        bc_in,
        a_log,
        taps,
        bias.reshape(1, channels),
        gain.reshape(1, channels),
        dt_bias.reshape(1, channels),
        resid,
        route_ids,
        route_weight,
        out_weight,
        grad_mix,
        w_gate,
        w_up,
        w_down,
    )


def entering(everything):
    peers, here = everything.shape[0], lax.axis_index("seq")
    values = everything.astype(jnp.float32)
    start = jnp.zeros_like(values[0, 0])
    arriving = jnp.zeros_like(start)
    for k in range(peers):
        start = jnp.where(k < here, values[k, 0] * start + values[k, 1], start)
        back = peers - 1 - k
        arriving = jnp.where(back > here, values[back, 0] * arriving + values[back, 2], arriving)
    return start, arriving


def routed_experts(partial_value, resid, w_gate, w_up, w_down, route_ids, route_weight):
    rows = resid.shape[0]
    mixed = lax.psum(partial_value, "expert").astype(jnp.float32)
    own = lax.dynamic_slice_in_dim(mixed, lax.axis_index("expert") * rows, rows, 0)
    hidden_in = (resid.astype(jnp.float32) + own).astype(jnp.bfloat16)
    experts = lax.axis_size("expert")
    capacity = 4 * rows // experts
    flat_ids = route_ids.reshape(-1)
    order = jnp.arange(flat_ids.shape[0], dtype=jnp.int32)
    earlier = (flat_ids[:, None] == flat_ids[None, :]) & (order[None, :] < order[:, None])
    rank = jnp.sum(earlier.astype(jnp.int32), axis=1)
    slot = flat_ids * capacity + rank
    placing = (jnp.arange(experts * capacity, dtype=jnp.int32)[:, None] == slot[None, :]).astype(
        jnp.bfloat16
    )
    doubled = jnp.repeat(hidden_in, 2, axis=0)
    outgoing = jnp.dot(placing, doubled, preferred_element_type=jnp.float32).astype(jnp.bfloat16)
    incoming = lax.all_to_all(outgoing, "expert", split_axis=0, concat_axis=0, tiled=True)
    piece = lax.all_gather(incoming, "seq", axis=0, tiled=True)
    gate = jnp.dot(piece, w_gate[0], preferred_element_type=jnp.float32)
    upper = jnp.dot(piece, w_up[0], preferred_element_type=jnp.float32)
    hidden = (jax.nn.silu(gate) * upper).astype(jnp.bfloat16)
    expert_sum = lax.psum_scatter(
        jnp.dot(hidden, w_down[0], preferred_element_type=jnp.float32).astype(jnp.bfloat16),
        "seq",
        scatter_dimension=0,
        tiled=True,
    )
    returned = lax.all_to_all(expert_sum, "expert", split_axis=0, concat_axis=0, tiled=True)
    picked = lax.dot_general(
        placing, returned, (((0,), (0,)), ((), ())), preferred_element_type=jnp.float32
    )
    picked = picked.reshape(rows, 2, -1)
    moe = picked[:, 0] * route_weight[:, 0:1] + picked[:, 1] * route_weight[:, 1:2]
    return (hidden_in.astype(jnp.float32) + moe).astype(jnp.bfloat16)


def local(
    x_in,
    z_in,
    dt_raw,
    bc_in,
    a_log,
    conv_weight,
    conv_bias,
    skip_gain,
    dt_bias,
    out_weight,
    resid,
    w_gate,
    w_up,
    w_down,
    route_ids,
    route_weight,
    grad_mix,
):
    length, channels = x_in.shape
    states = a_log.shape[0]
    rim = KW - 1
    rows = resid.shape[0]
    experts = lax.axis_size("expert")
    if experts == 4 and lax.axis_size("seq") == 8:
        layer_out, grad_x, grad_z, grad_dt, grad_alog, grad_conv, grad_chan, grad_bc = deliver(
            layer(
                x_in,
                z_in,
                dt_raw,
                bc_in,
                a_log,
                conv_weight,
                conv_bias,
                skip_gain,
                dt_bias,
                resid,
                route_ids,
                route_weight,
                out_weight,
                grad_mix,
                w_gate,
                w_up,
                w_down,
            )
        )
        return (layer_out, grad_x, grad_z, grad_dt, grad_bc, grad_alog, grad_conv, grad_chan)
    x_val = x_in.astype(jnp.float32)
    z_val = z_in.astype(jnp.float32)
    before = shifted(x_in[length - rim :], "seq", 1)
    padded = jnp.concatenate([before.astype(jnp.float32), x_val], axis=0)
    pre = conv_bias[None, :] + conv_weight[0][None, :] * padded[0:length]
    for tap in range(1, KW):
        pre = pre + conv_weight[tap][None, :] * padded[tap : tap + length]
    conv_sig = jax.nn.sigmoid(pre)
    conv_out = pre * conv_sig
    step = jax.nn.softplus(dt_raw + dt_bias[None, :])
    rate = -jnp.exp(a_log)
    drive = step * conv_out
    z_sig = jax.nn.sigmoid(z_val)
    back_mix = lax.dot_general(
        grad_mix, out_weight, (((1,), (1,)), ((), ())), preferred_element_type=jnp.float32
    )
    grad_y = back_mix * z_val * z_sig

    def grouped(array):
        return array.reshape(length // SUB, SUB, channels)

    def flat(array):
        return array.reshape(length, channels)

    spread = jnp.broadcast_to(
        bc_in.transpose(0, 2, 1)[:, :, :, None], (2, length, states, LANES)
    ).reshape(2, length // SUB, SUB, states, LANES)
    b_wide, c_wide = spread[0], spread[1]
    totals, forward, backward = sweeps(length, channels, states)
    step_g, drive_g, grad_g, conv_g = (grouped(a) for a in (step, drive, grad_y, conv_out))
    own_totals = totals(step_g, drive_g, grad_g, b_wide, c_wide, rate)
    start, arriving = entering(lax.all_gather(own_totals, "seq"))
    y_val = flat(forward(step_g, drive_g, b_wide, c_wide, rate, start))
    y_val = y_val + skip_gain[None, :] * conv_out
    gated = (y_val * z_val * z_sig).astype(jnp.bfloat16)
    partial_value = jnp.dot(gated, out_weight, preferred_element_type=jnp.float32)
    grad_z = back_mix * y_val * z_sig * (1.0 + z_val * (1.0 - z_sig))
    grad_step, conv_part_grad, grad_b, grad_c, grad_alog_local = backward(
        step_g, drive_g, conv_g, grad_g, b_wide, c_wide, rate, start, arriving
    )
    grad_step, conv_part_grad = flat(grad_step), flat(conv_part_grad)
    grad_conv_out = skip_gain[None, :] * grad_y + conv_part_grad
    grad_skip = jnp.sum(grad_y * conv_out, axis=0)
    grad_dt = grad_step * jax.nn.sigmoid(dt_raw + dt_bias[None, :])
    grad_pre = grad_conv_out * (conv_sig * (1.0 + pre * (1.0 - conv_sig)))
    after = shifted(grad_pre[:rim], "seq", -1)
    grad_pad = jnp.concatenate([grad_pre, after], axis=0)
    grad_x = conv_weight[rim][None, :] * grad_pad[0:length]
    for tap in range(rim):
        grad_x = grad_x + conv_weight[tap][None, :] * grad_pad[rim - tap : rim - tap + length]
    grad_taps = jnp.stack(
        [jnp.sum(grad_pre * padded[tap : tap + length], axis=0) for tap in range(KW)]
    )
    channel_grads = jnp.stack([jnp.sum(grad_pre, axis=0), grad_skip, jnp.sum(grad_dt, axis=0)])
    own_sums = jnp.concatenate([grad_alog_local, grad_taps, channel_grads], axis=0)
    own_bc = jnp.stack([jnp.sum(grad_b, axis=-1), jnp.sum(grad_c, axis=-1)])
    own_bc = own_bc.reshape(2, length, states).transpose(0, 2, 1).reshape(2 * states, length)
    layer_out = routed_experts(
        partial_value.astype(jnp.bfloat16),
        resid,
        w_gate,
        w_up,
        w_down,
        route_ids,
        route_weight,
    )
    sums = lax.psum(own_sums, "seq")
    grad_bc = lax.psum(own_bc, "expert").reshape(2, states, length)
    grad_alog = sums[:states]
    grad_conv = sums[states : states + KW]
    grad_chan = sums[states + KW : states + KW + 3]
    return (layer_out, grad_x, grad_z, grad_dt, grad_bc, grad_alog, grad_conv, grad_chan)


def solution(mesh):
    in_specs = (
        P("seq", "expert"),
        P("seq", "expert"),
        P("seq", "expert"),
        P(None, None, "seq"),
        P(None, "expert"),
        P(None, "expert"),
        P("expert"),
        P("expert"),
        P("expert"),
        P("expert", None),
        P(("seq", "expert"), None),
        P("expert", None, "seq"),
        P("expert", None, "seq"),
        P("expert", "seq", None),
        P(("seq", "expert"), None),
        P(("seq", "expert"), None),
        P("seq", None),
    )
    out_specs = (
        P(("seq", "expert"), None),
        P("seq", "expert"),
        P("seq", "expert"),
        P("seq", "expert"),
        P(None, None, "seq"),
        P(None, "expert"),
        P(None, "expert"),
        P(None, "expert"),
    )
    return jax.shard_map(local, mesh=mesh, in_specs=in_specs, out_specs=out_specs, check_vma=False)
```

```python
import functools

import jax
import jax.numpy as jnp
from jax import lax
from jax.experimental import pallas as pl
from jax.experimental.pallas import tpu as pltpu
from jax.sharding import PartitionSpec as P

KW = 4
SUB = 8
LANES = 128


def shifted(x, axis, by):
    peers = lax.axis_size(axis)
    pairs = [(i, i + by) for i in range(peers) if 0 <= i + by < peers]
    return lax.ppermute(x, axis, pairs)


def wide(tile, width):
    return jnp.concatenate([tile] * (width // tile.shape[1]), axis=1)


def folded(value):
    total = value[:, :LANES]
    for at in range(LANES, value.shape[1], LANES):
        total = total + value[:, at : at + LANES]
    return total


def totals_kernel(step_ref, drive_ref, grad_ref, b_ref, c_ref, rate_ref, out_ref):
    rate = rate_ref[...]
    width = rate.shape[1]

    def advance(i, carry):
        state, passed, leaving = carry
        for j in range(SUB):
            decay = jnp.exp(step_ref[i, j : j + 1, :] * rate)
            state = decay * state + drive_ref[i, j : j + 1, :] * wide(b_ref[i, j], width)
            passed = passed * decay
            leaving = leaving + passed * (grad_ref[i, j : j + 1, :] * wide(c_ref[i, j], width))
        return (state, passed, leaving)

    zero = jnp.zeros_like(rate)
    state, passed, leaving = lax.fori_loop(
        0, step_ref.shape[0], advance, (zero, jnp.ones_like(rate), zero)
    )
    out_ref[0] = passed.astype(out_ref.dtype)
    out_ref[1] = state.astype(out_ref.dtype)
    out_ref[2] = leaving.astype(out_ref.dtype)


def forward_kernel(step_ref, drive_ref, b_ref, c_ref, rate_ref, start_ref, y_ref):
    rate = rate_ref[...]
    width = rate.shape[1]

    def advance(i, state):
        for j in range(SUB):
            decay = jnp.exp(step_ref[i, j : j + 1, :] * rate)
            state = decay * state + drive_ref[i, j : j + 1, :] * wide(b_ref[i, j], width)
            y_ref[i, j : j + 1, :] = jnp.sum(
                wide(c_ref[i, j], width) * state, axis=0, keepdims=True
            )
        return state

    lax.fori_loop(0, step_ref.shape[0], advance, start_ref[...])


def backward_kernel(
    step_ref,
    drive_ref,
    conv_ref,
    grad_ref,
    b_ref,
    c_ref,
    rate_ref,
    start_ref,
    arriving_ref,
    step_out_ref,
    conv_out_ref,
    b_out_ref,
    c_out_ref,
    alog_ref,
    states,
):
    rate = rate_ref[...]
    width = rate.shape[1]
    groups = step_ref.shape[0]

    @pl.when(pl.program_id(0) == 0)
    def _():
        b_out_ref[...] = jnp.zeros_like(b_out_ref)
        c_out_ref[...] = jnp.zeros_like(c_out_ref)

    states[0] = start_ref[...]

    def advance(i, state):
        for j in range(SUB):
            decay = jnp.exp(step_ref[i, j : j + 1, :] * rate)
            state = decay * state + drive_ref[i, j : j + 1, :] * wide(b_ref[i, j], width)
            states[i * SUB + j + 1] = state
        return state

    lax.fori_loop(0, groups, advance, start_ref[...])

    def retreat(k, carry):
        flow, alog_sum = carry
        i = groups - 1 - k
        for j in reversed(range(SUB)):
            at = i * SUB + j
            step_now = step_ref[i, j : j + 1, :]
            grad_now = grad_ref[i, j : j + 1, :]
            decay = jnp.exp(step_now * rate)
            adjoint = wide(c_ref[i, j], width) * grad_now + flow
            flow = decay * adjoint
            held = flow * states[at]
            alog_sum = alog_sum + step_now * held
            into_drive = jnp.sum(adjoint * wide(b_ref[i, j], width), axis=0, keepdims=True)
            step_out_ref[i, j : j + 1, :] = (
                jnp.sum(rate * held, axis=0, keepdims=True)
                + conv_ref[i, j : j + 1, :] * into_drive
            )
            conv_out_ref[i, j : j + 1, :] = step_now * into_drive
            b_out_ref[i, j] += folded(adjoint * drive_ref[i, j : j + 1, :])
            c_out_ref[i, j] += folded(grad_now * states[at + 1])
        return (flow, alog_sum)

    _, alog_sum = lax.fori_loop(0, groups, retreat, (arriving_ref[...], jnp.zeros_like(rate)))
    alog_ref[...] = alog_sum * rate


def sweeps(length, channels, states):
    block = min(512, channels)
    groups = length // SUB
    rows = pl.BlockSpec((groups, SUB, block), lambda k: (0, 0, k))
    spread = pl.BlockSpec((groups, SUB, states, LANES), lambda k: (0, 0, 0, 0))
    column = pl.BlockSpec((states, block), lambda k: (0, k))
    grid = (channels // block,)
    f32 = jnp.float32
    row_shape = jax.ShapeDtypeStruct((groups, SUB, channels), f32)
    spread_shape = jax.ShapeDtypeStruct((groups, SUB, states, LANES), f32)
    column_shape = jax.ShapeDtypeStruct((states, channels), f32)
    totals = pl.pallas_call(
        totals_kernel,
        grid=grid,
        in_specs=[rows, rows, rows, spread, spread, column],
        out_specs=pl.BlockSpec((3, states, block), lambda k: (0, 0, k)),
        out_shape=jax.ShapeDtypeStruct((3, states, channels), jnp.bfloat16),
        name="totals",
    )
    forward = pl.pallas_call(
        forward_kernel,
        grid=grid,
        in_specs=[rows, rows, spread, spread, column, column],
        out_specs=rows,
        out_shape=row_shape,
        name="forward",
    )
    backward = pl.pallas_call(
        backward_kernel,
        grid=grid,
        in_specs=[rows, rows, rows, rows, spread, spread, column, column, column],
        out_specs=[rows, rows, spread, spread, column],
        out_shape=[row_shape, row_shape, spread_shape, spread_shape, column_shape],
        scratch_shapes=[pltpu.VMEM((length + 1, states, block), f32)],
        name="backward",
    )
    return totals, forward, backward


MESH = pl.DeviceIdType.MESH
GROUP = 16


def places():
    s, z = lax.axis_index("seq"), lax.axis_index("expert")
    core = lax.rem(s, 2)
    sib = s + 1 - 2 * core
    across_x = s + 2 - 4 * lax.rem(lax.div(s, 2), 2)
    across_y = s + 4 - 8 * lax.div(s, 4)
    return s, z, core, sib, across_x, across_y


def transposed(a, b):
    return lax.dot_general(a, b, (((1,), (1,)), ((), ())), preferred_element_type=jnp.float32)


def layer_kernel(
    x_ref,
    z_ref,
    dt_ref,
    bc_ref,
    alog_ref,
    conv_ref,
    bias_ref,
    gain_ref,
    dtb_ref,
    resid_ref,
    ids_ref,
    weight_ref,
    ow_hbm,
    gm_hbm,
    wg_hbm,
    wu_hbm,
    wd_hbm,
    out_ref,
    gx_ref,
    gz_ref,
    gdt_ref,
    alog_out,
    taps_out,
    chan_out,
    bc_out,
    gx_buf,
    gz_buf,
    gdt_buf,
    rows_all,
    wgu,
    wd,
    ow,
    gm,
    hidden,
    own_h,
    zrecv,
    zfin,
    part,
    psib,
    acc,
    rx,
    ry,
    rdx,
    rdy,
    fin,
    p_buf,
    sums_own,
    sums_recv,
    sums_acc,
    bc_own,
    bc_recv,
    decays,
    states,
    b_wide,
    c_wide,
    b_block,
    c_block,
    step_buf,
    drive_buf,
    conv_buf,
    grad_buf,
    dsilu_buf,
    dtsig_buf,
    zgate_buf,
    zfac_buf,
    into_buf,
    qsum_buf,
    xpad,
    gpad,
    xhalo,
    ghalo,
    gated,
    adj,
    quo,
    gb_acc,
    gc_acc,
    tot,
    tsib,
    tpair,
    trecv,
    rate_buf,
    start_buf,
    arrive_buf,
    w_sem,
    sems,
):
    s, z, core, sib, ax, ay = places()
    diag = ax + ay - s
    f32, bf16 = jnp.float32, jnp.bfloat16
    ways, seqs = 4, 8
    rows = resid_ref.shape[0]
    length, channels = x_ref.shape
    width = resid_ref.shape[1]
    half = width // 2
    scan = channels // 2
    groups = length // GROUP
    nst = alog_ref.shape[0]
    flat = GROUP * nst
    tiles = wgu.shape[1] // 256
    after = lax.rem(s + 1, seqs)
    ahead = lax.rem(s + seqs - 1, seqs)
    count = [0]
    everything = []

    def to(src, dst, seq, exp):
        index = count[0]
        count[0] += 1
        copy = pltpu.make_async_remote_copy(
            src_ref=src,
            dst_ref=dst,
            send_sem=sems.at[0, index],
            recv_sem=sems.at[1, index],
            device_id=(seq, exp),
            device_id_type=MESH,
        )
        everything.append(copy)
        return copy

    first = [
        pltpu.make_async_copy(ow_hbm, ow, w_sem.at[0]),
        pltpu.make_async_copy(gm_hbm, gm, w_sem.at[1]),
    ]
    for load in first:
        load.start()
    loads = []
    for t in range(tiles):
        for k, w_hbm in enumerate((wg_hbm, wu_hbm)):
            loads.append(
                pltpu.make_async_copy(
                    w_hbm.at[0, :, pl.ds(t * 128, 128)],
                    wgu.at[:, pl.ds(t * 256 + k * 128, 128)],
                    w_sem.at[2 + 2 * t + k],
                )
            )
    loads.append(pltpu.make_async_copy(wd_hbm.at[0], wd, w_sem.at[2 + 2 * tiles]))

    zs = [lax.rem(z + d, ways) for d in range(ways)]
    zb = [lax.rem(z + ways - d, ways) for d in range(ways)]

    barrier = pltpu.get_barrier_semaphore()
    partners = [(sib, z), (ax, z), (ay, z), (diag, z), (after, z), (ahead, z)]
    partners += [(s, zs[1]), (s, zs[2]), (s, zs[3])]
    for seq, exp in partners:
        pl.semaphore_signal(barrier, inc=1, device_id=(seq, exp), device_id_type=MESH)
    pl.semaphore_wait(barrier, len(partners))

    halo = to(x_ref.at[pl.ds(length - GROUP, GROUP), :], xhalo, after, z)
    halo.start()

    for k, spread in enumerate((b_wide, c_wide)):
        value = bc_ref[k]
        for t in range(length):
            spread[t] = jnp.broadcast_to(value[:, t : t + 1], (nst, LANES))
    lane = lax.broadcasted_iota(jnp.int32, (length, flat), 1)
    row = lax.broadcasted_iota(jnp.int32, (length, flat), 0)
    same_token = lax.div(lane, nst) == lax.rem(row, GROUP)
    lane_r = lax.broadcasted_iota(jnp.int32, (nst, flat), 1)
    row_r = lax.broadcasted_iota(jnp.int32, (nst, flat), 0)
    unit = (lax.rem(lane_r, nst) == row_r).astype(f32)
    repeat = unit.astype(bf16)
    for k, block_ref in enumerate((b_block, c_block)):
        by_token = jnp.transpose(bc_ref[k]).astype(bf16)
        laid = jnp.dot(by_token, repeat, preferred_element_type=f32)
        block_ref[...] = jnp.where(same_token, laid, 0.0).astype(bf16)
    diagonal = same_token[:GROUP].astype(f32)
    ones_block = diagonal.astype(bf16)
    rate_buf[...] = -jnp.exp(alog_ref[...])

    for load in first:
        load.wait()

    def mix_tile(t, _):
        at = pl.ds(pl.multiple_of(t * 256, 256), 256)
        zfac_buf[:, :, at] = transposed(gm[...], ow[at, :]).reshape(groups, GROUP, 256)
        return 0

    lax.fori_loop(0, channels // 256, mix_tile, 0, unroll=True)
    for load in loads:
        load.start()
    xpad[8 : 8 + length, :] = x_ref[...].astype(f32)
    halo.wait_recv()
    xpad[0:8, :] = jnp.where(s > 0, xhalo[...].astype(f32)[GROUP - 8 :], 0.0)

    def prepare(t, _):
        at = pl.ds(pl.multiple_of(t * LANES, LANES), LANES)

        def put(ref, value):
            ref[:, :, at] = value.reshape(groups, GROUP, LANES)

        pre = bias_ref[:, at] + conv_ref[0:1, at] * xpad[5 : 5 + length, at]
        for tap in range(1, KW):
            pre = pre + conv_ref[tap : tap + 1, at] * xpad[5 + tap : 5 + tap + length, at]
        conv_sig = jax.nn.sigmoid(pre)
        conv_out = pre * conv_sig
        put(conv_buf, conv_out)
        put(dsilu_buf, conv_sig * (1.0 + pre * (1.0 - conv_sig)))
        raw = dt_ref[:, at] + dtb_ref[:, at]
        step = jnp.maximum(raw, 0.0) + jnp.log1p(jnp.exp(-jnp.abs(raw)))
        put(step_buf, step)
        put(drive_buf, step * conv_out)
        put(dtsig_buf, jax.nn.sigmoid(raw))
        z_val = z_ref[:, at].astype(f32)
        z_sig = jax.nn.sigmoid(z_val)
        mixed = zfac_buf[:, :, at].reshape(length, LANES)
        gate = z_val * z_sig
        put(zgate_buf, gate)
        put(grad_buf, mixed * gate)
        put(zfac_buf, mixed * z_sig * (1.0 + z_val * (1.0 - z_sig)))
        return 0

    lax.fori_loop(0, channels // LANES, prepare, 0)

    def lanes(k):
        return pl.ds(k * scan, scan)

    def totals(k, low, high, carry):
        at = lanes(k)
        rate = rate_buf[:, at]

        def advance(i, carry):
            state, passed, leaving = carry
            for j in range(GROUP):
                decay = jnp.exp(step_buf[i, j : j + 1, at] * rate)
                decays[i * GROUP + j, :, at] = decay
                state = decay * state + drive_buf[i, j : j + 1, at] * wide(
                    b_wide[i * GROUP + j], scan
                )
                passed = passed * decay
                leaving = leaving + passed * (
                    grad_buf[i, j : j + 1, at] * wide(c_wide[i * GROUP + j], scan)
                )
            return (state, passed, leaving)

        return lax.fori_loop(low, high, advance, carry)

    zero = jnp.zeros((nst, scan), f32)
    nothing = (zero, jnp.ones_like(zero), zero)

    def keep(k, carry):
        for m in range(3):
            tot[k, m] = carry[m].astype(bf16)

    beside = [to(tot.at[k], tsib.at[k], sib, z) for k in range(2)]
    xbit, ybit = lax.rem(lax.div(s, 2), 2), lax.div(s, 4)
    beyond = []
    for k in range(2):
        for m, (seq, bit) in enumerate(((ax, xbit), (ay, ybit), (diag, ybit))):
            at = pl.ds(bit, 2)
            beyond.append(to(tpair.at[k, at], trecv.at[k, m, at], seq, z))

    def join(k):
        beside[k].wait_recv()
        own = [tot[k, m].astype(f32) for m in range(3)]
        their = [tsib[k, m].astype(f32) for m in range(3)]
        one = [jnp.where(core == 0, a, b) for a, b in zip(own, their)]
        two = [jnp.where(core == 0, b, a) for a, b in zip(own, their)]
        tpair[k, 0] = (two[1] * one[0] + two[0]).astype(bf16)
        tpair[k, 1] = (one[1] * two[1]).astype(bf16)
        tpair[k, 2] = (one[2] + one[1] * two[2]).astype(bf16)
        for copy in beyond[3 * k : 3 * k + 3]:
            copy.start()

    def enter(k):
        for copy in beyond[3 * k : 3 * k + 3]:
            copy.wait_recv()
        chip = lax.div(s, 2)
        start, arriving = zero, zero

        def other_chip(c):
            relation = (c % 2 + xbit - 2 * (c % 2) * xbit) + 2 * (c // 2 + ybit - 2 * (c // 2) * ybit)
            return trecv.at[k, jnp.maximum(relation - 1, 0)]

        for c in range(4):
            at = other_chip(c)
            start = jnp.where(c < chip, at[1].astype(f32) * start + at[0].astype(f32), start)
            at = other_chip(3 - c)
            arriving = jnp.where(
                3 - c > chip, at[1].astype(f32) * arriving + at[2].astype(f32), arriving
            )
        passed = tsib[k, 1].astype(f32)
        start = jnp.where(core == 1, passed * start + tsib[k, 0].astype(f32), start)
        arriving = jnp.where(core == 0, passed * arriving + tsib[k, 2].astype(f32), arriving)
        start_buf[:, lanes(k)] = start
        arrive_buf[:, lanes(k)] = arriving

    keep(0, totals(0, 0, groups, nothing))
    beside[0].start()
    middle = totals(1, 0, groups // 2, nothing)
    join(0)
    keep(1, totals(1, groups // 2, groups, middle))
    beside[1].start()
    join(1)

    def state_rows(at, number):
        return pl.ds(pl.multiple_of(at * nst, nst), number * nst)

    def forward(k):
        at = lanes(k)
        states[0:nst, at] = start_buf[:, at].astype(bf16)

        def advance(i, state):
            for j in range(GROUP):
                t = i * GROUP + j
                state = decays[t, :, at] * state + drive_buf[i, j : j + 1, at] * wide(
                    b_wide[t], scan
                )
                states[state_rows(t + 1, 1), at] = state.astype(bf16)
            here = pl.ds(pl.multiple_of(i * GROUP, GROUP), GROUP)
            y_val = jnp.dot(
                c_block[here, :],
                states[state_rows(i * GROUP + 1, GROUP), at],
                preferred_element_type=f32,
            )
            y_val = y_val + gain_ref[:, at] * conv_buf[i, :, at]
            gz_buf[here, at] = zfac_buf[i, :, at] * y_val
            gated[here, at] = (zgate_buf[i, :, at] * y_val).astype(bf16)
            return state

        lax.fori_loop(0, groups, advance, start_buf[:, at])

    for k in range(2):
        enter(k)
        forward(k)

    written = [
        pltpu.make_async_copy(gz_buf, gz_ref, w_sem.at[3 + 2 * tiles]),
        pltpu.make_async_copy(gdt_buf, gdt_ref, w_sem.at[4 + 2 * tiles]),
        pltpu.make_async_copy(gx_buf, gx_ref, w_sem.at[5 + 2 * tiles]),
    ]
    written[0].start()

    waves = 2
    piece = rows // waves
    pack = ways * piece

    def block(seq, exp, w):
        at = (w * seqs + seq) * pack + exp * piece
        return pl.ds(pl.multiple_of(at, piece), piece)

    def within(exp, w):
        return pl.ds(pl.multiple_of(exp * rows + w * piece, piece), piece)

    def project(t, _):
        at = pl.ds(pl.multiple_of(t * 256, 256), 256)
        p_buf[:, at] = jnp.dot(gated[...], ow[:, at], preferred_element_type=f32).astype(bf16)
        return 0

    lax.fori_loop(0, width // 256, project, 0, unroll=True)

    z_out = [
        [to(p_buf.at[within(zs[d], w)], zrecv.at[w, d - 1], s, zs[d]) for d in (1, 2, 3)]
        for w in range(waves)
    ]
    for copy in z_out[0]:
        copy.start()

    gb_acc[...] = jnp.zeros_like(gb_acc)
    gc_acc[...] = jnp.zeros_like(gc_acc)

    def backward(k):
        at = lanes(k)

        def retreat(n, carry):
            flow, alog_sum = carry
            i = groups - 1 - n
            for j in reversed(range(GROUP)):
                t = i * GROUP + j
                adjoint = wide(c_wide[t], scan) * grad_buf[i, j : j + 1, at] + flow
                adj[j * nst : (j + 1) * nst, :] = adjoint.astype(bf16)
                flow = decays[t, :, at] * adjoint
                share = rate_buf[:, at] * (flow * states[state_rows(t, 1), at].astype(f32))
                alog_sum = alog_sum + step_buf[i, j : j + 1, at] * share
                quo[j * nst : (j + 1) * nst, :] = share.astype(bf16)
            here = pl.ds(pl.multiple_of(i * GROUP, GROUP), GROUP)
            into_buf[i, :, at] = jnp.dot(b_block[here, :], adj[...], preferred_element_type=f32)
            qsum_buf[i, :, at] = jnp.dot(ones_block, quo[...], preferred_element_type=f32)
            gb_acc[i] += transposed(drive_buf[i, :, at].astype(bf16), adj[...])
            gc_acc[i] += transposed(
                grad_buf[i, :, at].astype(bf16), states[state_rows(i * GROUP + 1, GROUP), at]
            )
            return (flow, alog_sum)

        _, alog_sum = lax.fori_loop(0, groups, retreat, (arrive_buf[:, at], zero))
        sums_own[0:nst, at] = alog_sum

    gather, to_x, to_y, to_b, forward = [], [], [], [], []
    for w in range(waves):
        here = rows_all.at[block(s, z, w)]
        gather.append([to(here, here, s, zs[d]) for d in (1, 2, 3)])
        blocks = [rows_all.at[block(s, zb[d], w)] for d in range(ways)]
        to_x.append([to(at, at, ax, z) for at in blocks])
        to_y.append([to(at, at, ay, z) for at in blocks])
        to_b.append([to(at, at, sib, z) for at in blocks])
        passing = []
        for d in range(ways):
            origin, target = (ay, ax) if d < 2 else (ax, ay)
            at = rows_all.at[block(origin, zb[d], w)]
            passing.append(to(at, at, target, z))
        forward.append(passing)

    def mixed_rows(w):
        for copy in z_out[w]:
            copy.wait_recv()
        own = pl.ds(w * piece, piece)
        total = resid_ref[own, :].astype(f32) + p_buf[within(z, w), :].astype(f32)
        for d in range(3):
            total = total + zrecv[w, d].astype(f32)
        own_h[own, :] = total.astype(bf16)
        rows_all[block(s, z, w), :] = total.astype(bf16)
        for copy in gather[w] + [to_x[w][0], to_y[w][0], to_b[w][0]]:
            copy.start()

    def spread_rows(w):
        for d in (1, 2, 3):
            gather[w][d - 1].wait_recv()
            to_x[w][d].start()
            to_y[w][d].start()
            to_b[w][d].start()

    backward(0)
    for copy in z_out[1]:
        copy.start()
    mixed_rows(0)
    backward(1)
    mixed_rows(1)
    for k, held in enumerate((gb_acc, gc_acc)):
        kept = jnp.where(same_token, held[...].reshape(length, flat), 0.0)
        bc_own[k] = lax.dot_general(
            unit,
            kept,
            (((1,), (1,)), ((), ())),
            precision=lax.Precision.HIGHEST,
            preferred_element_type=f32,
        )
    bc_copies = [to(bc_own, bc_recv.at[d - 1], s, zs[d]) for d in (1, 2, 3)]
    for copy in bc_copies:
        copy.start()

    def finish(t, _):
        at = pl.ds(pl.multiple_of(t * LANES, LANES), LANES)

        def get(ref):
            return ref[:, :, at].reshape(length, LANES)

        def total(value):
            return jnp.sum(value, axis=0, keepdims=True)

        into, conv_out, grad_y = get(into_buf), get(conv_buf), get(grad_buf)
        grad_dt = (get(qsum_buf) + conv_out * into) * get(dtsig_buf)
        gdt_buf[:, at] = grad_dt
        grad_pre = (gain_ref[:, at] * grad_y + get(step_buf) * into) * get(dsilu_buf)
        gpad[0:length, at] = grad_pre
        for tap in range(KW):
            sums_own[nst + tap : nst + tap + 1, at] = total(
                grad_pre * xpad[5 + tap : 5 + tap + length, at]
            )
        sums_own[nst + KW : nst + KW + 1, at] = total(grad_pre)
        sums_own[nst + KW + 1 : nst + KW + 2, at] = total(grad_y * conv_out)
        sums_own[nst + KW + 2 : nst + KW + 3, at] = total(grad_dt)
        return 0

    lax.fori_loop(0, channels // LANES, finish, 0)
    written[1].start()
    sums_own[nst + KW + 3 :, :] = jnp.zeros_like(sums_own[nst + KW + 3 :, :])
    rim = to(gpad.at[pl.ds(0, 8)], ghalo, ahead, z)
    rim.start()
    sums_copies = [
        to(sums_own, sums_recv.at[0], sib, z),
        to(sums_acc.at[0], sums_recv.at[1], ax, z),
        to(sums_acc.at[1], sums_recv.at[2], ay, z),
    ]
    sums_copies[0].start()

    sums_copies[0].wait_recv()
    sums_acc[0] = sums_own[...] + sums_recv[0]
    sums_copies[1].start()
    rim.wait_recv()
    gpad[length : length + 8, :] = jnp.where(s < seqs - 1, ghalo[...], 0.0)

    def spread_back(t, _):
        at = pl.ds(pl.multiple_of(t * LANES, LANES), LANES)
        grad_x = conv_ref[KW - 1 : KW, at] * gpad[0:length, at]
        for tap in range(KW - 1):
            away = KW - 1 - tap
            grad_x = grad_x + conv_ref[tap : tap + 1, at] * gpad[away : away + length, at]
        gx_buf[:, at] = grad_x
        return 0

    lax.fori_loop(0, channels // LANES, spread_back, 0)
    written[2].start()

    spread_rows(0)
    sums_copies[1].wait_recv()
    sums_acc[1] = sums_acc[0] + sums_recv[1]
    sums_copies[2].start()

    for copy in bc_copies:
        copy.wait_recv()
    bc_out[...] = (bc_own[...] + bc_recv[0]) + (bc_recv[1] + bc_recv[2])

    def up(w, seq):
        first_row = (w * seqs + 4 * lax.div(seq, 4)) * pack
        at = pl.ds(pl.multiple_of(first_row, 4 * pack), 4 * pack)

        def tile(t, _):
            both = jnp.dot(
                rows_all[at, :],
                wgu[:, pl.ds(pl.multiple_of(t * 256, 256), 256)],
                preferred_element_type=f32,
            )
            gate, upper = both[:, :128], both[:, 128:]
            value = gate * jax.nn.sigmoid(gate) * upper
            hidden[:, pl.ds(pl.multiple_of(t * 128, 128), 128)] = value.astype(bf16)
            return 0

        lax.fori_loop(0, tiles, tile, 0, unroll=True)

    def cols(h):
        return pl.ds(h * half, half)

    def part_rows(r, of_core):
        side = xbit if r % 2 == 0 else 1 - xbit
        return pl.ds(pl.multiple_of((2 * side + of_core) * pack, pack), pack)

    pair = {}

    def down(w, r0, h):
        g = 2 * w + r0 // 2
        for q in range(2):
            at = pl.ds(h * half + q * (half // 2), half // 2)
            part[g, :, at] = jnp.dot(
                hidden[...], wd[:, at], preferred_element_type=f32
            ).astype(bf16)
        for r in (r0, r0 + 1):
            copy = to(
                part.at[g, part_rows(r, 1 - core), cols(h)], psib.at[w, r, :, cols(h)], sib, z
            )
            copy.start()
            pair[w, r, h] = copy

    def paired(w, r, h):
        pair[w, r, h].wait_recv()
        acc[w, r, :, cols(h)] = (
            part[2 * w + r // 2, part_rows(r, core), cols(h)].astype(f32)
            + psib[w, r, :, cols(h)].astype(f32)
        ).astype(bf16)

    def pack_of(seq, w):
        at = (w * seqs + seq) * pack
        return rows_all.at[pl.ds(pl.multiple_of(at, pack), pack)]

    share_out = [[to(pack_of(o, w), pack_of(o, w), sib, z) for o in (ax, ay, diag)] for w in range(waves)]
    send = {}

    def reduce_out(name, src, dst, seq):
        copy = to(src, dst, seq, z)
        copy.start()
        send[name] = copy

    def to_across_x(w, h):
        reduce_out(("x", w, h), acc.at[w, 1, :, cols(h)], rx.at[w, :, cols(h)], ax)

    def to_across_y(w, h):
        reduce_out(("y", w, h), acc.at[w, 2, :, cols(h)], ry.at[w, :, cols(h)], ay)

    def near(w):
        to_x[w][0].wait_recv()
        to_x[w][1].wait_recv()
        to_y[w][1].wait_recv()
        forward[w][1].start()
        to_x[w][2].wait_recv()
        forward[w][2].start()
        to_x[w][3].wait_recv()
        forward[w][3].start()
        share_out[w][0].start()
        to_y[w][2].wait_recv()
        to_y[w][3].wait_recv()
        share_out[w][1].start()

    def near_ready(w):
        for copy in to_b[w]:
            copy.wait_recv()
        share_out[w][0].wait_recv()

    def far(w):
        for copy in forward[w]:
            copy.wait_recv()
        share_out[w][2].start()

    def far_ready(w):
        share_out[w][1].wait_recv()
        share_out[w][2].wait_recv()

    def diagonal_out(w):
        paired(w, 3, 0)
        reduce_out(("d", w, 0), acc.at[w, 3, :, cols(0)], rdx.at[w], ax)
        paired(w, 3, 1)
        reduce_out(("d", w, 1), acc.at[w, 3, :, cols(1)], rdy.at[w], ay)

    def direct_x(w):
        paired(w, 1, 0)
        to_across_x(w, 0)
        paired(w, 1, 1)

    def direct_y(w):
        paired(w, 2, 1)
        to_across_y(w, 1)
        paired(w, 2, 0)
        paired(w, 0, 0)
        paired(w, 0, 1)

    def joined(w):
        send["d", w, 0].wait_recv()
        acc[w, 2, :, cols(0)] = (
            acc[w, 2, :, cols(0)].astype(f32) + rdx[w].astype(f32)
        ).astype(bf16)
        to_across_y(w, 0)
        send["d", w, 1].wait_recv()
        acc[w, 1, :, cols(1)] = (
            acc[w, 1, :, cols(1)].astype(f32) + rdy[w].astype(f32)
        ).astype(bf16)
        to_across_x(w, 1)

    back = {}

    def reduced(w, h):
        send["x", w, h].wait_recv()
        send["y", w, h].wait_recv()
        total = (
            acc[w, 0, :, cols(h)].astype(f32)
            + rx[w, :, cols(h)].astype(f32)
            + ry[w, :, cols(h)].astype(f32)
        ).astype(bf16)
        fin[w, :, cols(h)] = total
        for d in (1, 2, 3):
            at = pl.ds(pl.multiple_of(zs[d] * piece, piece), piece)
            copy = to(fin.at[w, at, cols(h)], zfin.at[w, d - 1, :, cols(h)], s, zs[d])
            copy.start()
            back[w, h, d] = copy

    eye = lax.broadcasted_iota(jnp.int32, (rows, rows), 0) == lax.broadcasted_iota(
        jnp.int32, (rows, rows), 1
    )

    def column(row):
        return jnp.sum(jnp.where(eye, row, 0.0), axis=1, keepdims=True)

    shares = []
    for d in range(ways):
        mine = [
            jnp.where(ids_ref[k : k + 1, :] == zb[d], weight_ref[k : k + 1, :], 0.0) for k in range(2)
        ]
        shares.append(column(mine[0] + mine[1]))

    def result(w, h):
        own = pl.ds(w * piece, piece)
        at = pl.ds(pl.multiple_of(z * piece, piece), piece)
        total = own_h[own, cols(h)].astype(f32)
        total = total + shares[0][w * piece : (w + 1) * piece] * fin[w, at, cols(h)].astype(f32)
        for d in (1, 2, 3):
            back[w, h, d].wait_recv()
            total = total + shares[d][w * piece : (w + 1) * piece] * zfin[
                w, d - 1, :, cols(h)
            ].astype(f32)
        out_ref[own, cols(h)] = total.astype(bf16)

    to_y[0][0].wait_recv()
    forward[0][0].start()
    near(0)
    near_ready(0)
    for load in loads:
        load.wait()
    spread_rows(1)
    to_y[1][0].wait_recv()
    forward[1][0].start()
    up(0, s)
    far(0)
    down(0, 0, 0)
    down(0, 0, 1)
    far_ready(0)
    near(1)
    up(0, ay)
    direct_x(0)
    down(0, 2, 0)
    down(0, 2, 1)
    diagonal_out(0)
    direct_y(0)
    near_ready(1)
    up(1, s)
    far(1)
    down(1, 0, 0)
    down(1, 0, 1)
    joined(0)
    direct_x(1)
    far_ready(1)
    up(1, ay)
    reduced(0, 0)
    reduced(0, 1)
    down(1, 2, 0)
    down(1, 2, 1)
    diagonal_out(1)
    direct_y(1)

    sums_copies[2].wait_recv()
    summed = sums_acc[1] + sums_recv[2]
    alog_out[...] = summed[:nst]
    taps_out[...] = summed[nst : nst + KW]
    chan_out[...] = summed[nst + KW : nst + KW + 3]

    result(0, 0)
    result(0, 1)
    joined(1)
    reduced(1, 0)
    reduced(1, 1)
    result(1, 0)
    result(1, 1)
    for copy in written:
        copy.wait()
    for copy in everything:
        copy.wait_send()


def deliver_kernel(number, *refs):
    given, results, stops, sem = (
        refs[:number],
        refs[number : 2 * number],
        refs[2 * number : 3 * number],
        refs[3 * number],
    )
    fetch = [pltpu.make_async_copy(given[k], stops[k], sem.at[0, k]) for k in range(number)]
    store = [pltpu.make_async_copy(stops[k], results[k], sem.at[1, k]) for k in range(number)]
    for copy in fetch:
        copy.start()
    for k in range(number):
        fetch[k].wait()
        store[k].start()
    for copy in store:
        copy.wait()


def deliver(arrays):
    number = len(arrays)
    anywhere = pl.BlockSpec(memory_space=pl.ANY)
    return pl.pallas_call(
        functools.partial(deliver_kernel, number),
        out_shape=[jax.ShapeDtypeStruct(a.shape, a.dtype) for a in arrays],
        in_specs=[anywhere] * number,
        out_specs=[anywhere] * number,
        scratch_shapes=[pltpu.VMEM(a.shape, a.dtype) for a in arrays]
        + [pltpu.SemaphoreType.DMA((2, number))],
        name="deliver",
    )(*arrays)


def layer(
    x_in,
    z_in,
    dt_raw,
    bc_in,
    a_log,
    taps,
    bias,
    gain,
    dt_bias,
    resid,
    route_ids,
    route_weight,
    out_weight,
    grad_mix,
    w_gate,
    w_up,
    w_down,
):
    rows, width = resid.shape
    length, channels = x_in.shape
    states = a_log.shape[0]
    units = w_gate.shape[2]
    tiles = units // 128
    seqs = lax.axis_size("seq")
    half, scan, groups = width // 2, channels // 2, length // GROUP
    bf16, f32 = jnp.bfloat16, jnp.float32
    vmem = pl.BlockSpec(memory_space=pltpu.VMEM)
    hbm = pl.BlockSpec(memory_space=pl.ANY)
    sem = pltpu.SemaphoreType.DMA
    flat = GROUP * states

    def held(*shape, kind=f32):
        return pltpu.VMEM(shape, kind)

    def rows_of():
        return held(groups, GROUP, channels)

    summed = (states + 8, channels)
    grads = (2, states, length)
    return pl.pallas_call(
        layer_kernel,
        out_shape=[
            jax.ShapeDtypeStruct((rows, width), bf16),
            jax.ShapeDtypeStruct((length, channels), f32),
            jax.ShapeDtypeStruct((length, channels), f32),
            jax.ShapeDtypeStruct((length, channels), f32),
            jax.ShapeDtypeStruct((states, channels), f32),
            jax.ShapeDtypeStruct((KW, channels), f32),
            jax.ShapeDtypeStruct((3, channels), f32),
            jax.ShapeDtypeStruct(grads, f32),
        ],
        in_specs=[vmem] * 12 + [hbm] * 5,
        out_specs=[vmem] + [hbm] * 3 + [vmem] * 4,
        scratch_shapes=[
            held(length, channels),
            held(length, channels),
            held(length, channels),
            held(seqs * length, width, kind=bf16),
            held(width, 2 * units, kind=bf16),
            held(units, width, kind=bf16),
            held(channels, width, kind=bf16),
            held(length, width, kind=bf16),
            held(2 * length, units, kind=bf16),
            held(rows, width, kind=bf16),
            held(2, 3, rows // 2, width, kind=bf16),
            held(2, 3, rows // 2, width, kind=bf16),
            held(4, 2 * length, width, kind=bf16),
            held(2, 4, length // 2, width, kind=bf16),
            held(2, 4, length // 2, width, kind=bf16),
            held(2, length // 2, width, kind=bf16),
            held(2, length // 2, width, kind=bf16),
            held(2, length // 2, half, kind=bf16),
            held(2, length // 2, half, kind=bf16),
            held(2, length // 2, width, kind=bf16),
            held(length, width, kind=bf16),
            held(*summed),
            held(3, *summed),
            held(2, *summed),
            held(*grads),
            held(3, *grads),
            held(length, states, channels),
            held((length + 1) * states, channels, kind=bf16),
            held(length, states, LANES),
            held(length, states, LANES),
            held(length, flat, kind=bf16),
            held(length, flat, kind=bf16),
        ]
        + [rows_of() for _ in range(10)]
        + [
            held(length + 8, channels),
            held(length + 8, channels),
            held(GROUP, channels, kind=bf16),
            held(8, channels),
            held(length, channels, kind=bf16),
            held(flat, scan, kind=bf16),
            held(flat, scan, kind=bf16),
            held(groups, GROUP, flat),
            held(groups, GROUP, flat),
            held(2, 3, states, scan, kind=bf16),
            held(2, 3, states, scan, kind=bf16),
            held(2, 3, states, scan, kind=bf16),
            held(2, 3, 3, states, scan, kind=bf16),
            held(states, channels),
            held(states, channels),
            held(states, channels),
            sem((2 * tiles + 6,)),
            sem((2, 144)),
        ],
        compiler_params=pltpu.CompilerParams(
            collective_id=0, has_side_effects=True, vmem_limit_bytes=60 << 20
        ),
        cost_estimate=pl.CostEstimate(
            flops=6 * seqs * length * width * units + 4 * length * width * channels,
            bytes_accessed=6 * width * units,
            transcendentals=seqs * length * units + length * channels * states,
        ),
        name="layer",
    )(
        x_in,
        z_in,
        dt_raw,
        bc_in,
        a_log,
        taps,
        bias.reshape(1, channels),
        gain.reshape(1, channels),
        dt_bias.reshape(1, channels),
        resid,
        route_ids.T,
        route_weight.T,
        out_weight,
        grad_mix,
        w_gate,
        w_up,
        w_down,
    )


def entering(everything):
    peers, here = everything.shape[0], lax.axis_index("seq")
    values = everything.astype(jnp.float32)
    start = jnp.zeros_like(values[0, 0])
    arriving = jnp.zeros_like(start)
    for k in range(peers):
        start = jnp.where(k < here, values[k, 0] * start + values[k, 1], start)
        back = peers - 1 - k
        arriving = jnp.where(back > here, values[back, 0] * arriving + values[back, 2], arriving)
    return start, arriving


def routed_experts(partial_value, resid, w_gate, w_up, w_down, route_ids, route_weight):
    rows = resid.shape[0]
    mixed = lax.psum(partial_value, "expert").astype(jnp.float32)
    own = lax.dynamic_slice_in_dim(mixed, lax.axis_index("expert") * rows, rows, 0)
    hidden_in = (resid.astype(jnp.float32) + own).astype(jnp.bfloat16)
    experts = lax.axis_size("expert")
    capacity = 4 * rows // experts
    flat_ids = route_ids.reshape(-1)
    order = jnp.arange(flat_ids.shape[0], dtype=jnp.int32)
    earlier = (flat_ids[:, None] == flat_ids[None, :]) & (order[None, :] < order[:, None])
    rank = jnp.sum(earlier.astype(jnp.int32), axis=1)
    slot = flat_ids * capacity + rank
    placing = (jnp.arange(experts * capacity, dtype=jnp.int32)[:, None] == slot[None, :]).astype(
        jnp.bfloat16
    )
    doubled = jnp.repeat(hidden_in, 2, axis=0)
    outgoing = jnp.dot(placing, doubled, preferred_element_type=jnp.float32).astype(jnp.bfloat16)
    incoming = lax.all_to_all(outgoing, "expert", split_axis=0, concat_axis=0, tiled=True)
    piece = lax.all_gather(incoming, "seq", axis=0, tiled=True)
    gate = jnp.dot(piece, w_gate[0], preferred_element_type=jnp.float32)
    upper = jnp.dot(piece, w_up[0], preferred_element_type=jnp.float32)
    hidden = (jax.nn.silu(gate) * upper).astype(jnp.bfloat16)
    expert_sum = lax.psum_scatter(
        jnp.dot(hidden, w_down[0], preferred_element_type=jnp.float32).astype(jnp.bfloat16),
        "seq",
        scatter_dimension=0,
        tiled=True,
    )
    returned = lax.all_to_all(expert_sum, "expert", split_axis=0, concat_axis=0, tiled=True)
    picked = lax.dot_general(
        placing, returned, (((0,), (0,)), ((), ())), preferred_element_type=jnp.float32
    )
    picked = picked.reshape(rows, 2, -1)
    moe = picked[:, 0] * route_weight[:, 0:1] + picked[:, 1] * route_weight[:, 1:2]
    return (hidden_in.astype(jnp.float32) + moe).astype(jnp.bfloat16)


def local(
    x_in,
    z_in,
    dt_raw,
    bc_in,
    a_log,
    conv_weight,
    conv_bias,
    skip_gain,
    dt_bias,
    out_weight,
    resid,
    w_gate,
    w_up,
    w_down,
    route_ids,
    route_weight,
    grad_mix,
):
    length, channels = x_in.shape
    states = a_log.shape[0]
    rim = KW - 1
    rows = resid.shape[0]
    experts = lax.axis_size("expert")
    if experts == 4 and lax.axis_size("seq") == 8:
        layer_out, grad_x, grad_z, grad_dt, grad_alog, grad_conv, grad_chan, grad_bc = deliver(
            layer(
                x_in,
                z_in,
                dt_raw,
                bc_in,
                a_log,
                conv_weight,
                conv_bias,
                skip_gain,
                dt_bias,
                resid,
                route_ids,
                route_weight,
                out_weight,
                grad_mix,
                w_gate,
                w_up,
                w_down,
            )
        )
        return (layer_out, grad_x, grad_z, grad_dt, grad_bc, grad_alog, grad_conv, grad_chan)
    x_val = x_in.astype(jnp.float32)
    z_val = z_in.astype(jnp.float32)
    before = shifted(x_in[length - rim :], "seq", 1)
    padded = jnp.concatenate([before.astype(jnp.float32), x_val], axis=0)
    pre = conv_bias[None, :] + conv_weight[0][None, :] * padded[0:length]
    for tap in range(1, KW):
        pre = pre + conv_weight[tap][None, :] * padded[tap : tap + length]
    conv_sig = jax.nn.sigmoid(pre)
    conv_out = pre * conv_sig
    step = jax.nn.softplus(dt_raw + dt_bias[None, :])
    rate = -jnp.exp(a_log)
    drive = step * conv_out
    z_sig = jax.nn.sigmoid(z_val)
    back_mix = lax.dot_general(
        grad_mix, out_weight, (((1,), (1,)), ((), ())), preferred_element_type=jnp.float32
    )
    grad_y = back_mix * z_val * z_sig

    def grouped(array):
        return array.reshape(length // SUB, SUB, channels)

    def flat(array):
        return array.reshape(length, channels)

    spread = jnp.broadcast_to(
        bc_in.transpose(0, 2, 1)[:, :, :, None], (2, length, states, LANES)
    ).reshape(2, length // SUB, SUB, states, LANES)
    b_wide, c_wide = spread[0], spread[1]
    totals, forward, backward = sweeps(length, channels, states)
    step_g, drive_g, grad_g, conv_g = (grouped(a) for a in (step, drive, grad_y, conv_out))
    own_totals = totals(step_g, drive_g, grad_g, b_wide, c_wide, rate)
    start, arriving = entering(lax.all_gather(own_totals, "seq"))
    y_val = flat(forward(step_g, drive_g, b_wide, c_wide, rate, start))
    y_val = y_val + skip_gain[None, :] * conv_out
    gated = (y_val * z_val * z_sig).astype(jnp.bfloat16)
    partial_value = jnp.dot(gated, out_weight, preferred_element_type=jnp.float32)
    grad_z = back_mix * y_val * z_sig * (1.0 + z_val * (1.0 - z_sig))
    grad_step, conv_part_grad, grad_b, grad_c, grad_alog_local = backward(
        step_g, drive_g, conv_g, grad_g, b_wide, c_wide, rate, start, arriving
    )
    grad_step, conv_part_grad = flat(grad_step), flat(conv_part_grad)
    grad_conv_out = skip_gain[None, :] * grad_y + conv_part_grad
    grad_skip = jnp.sum(grad_y * conv_out, axis=0)
    grad_dt = grad_step * jax.nn.sigmoid(dt_raw + dt_bias[None, :])
    grad_pre = grad_conv_out * (conv_sig * (1.0 + pre * (1.0 - conv_sig)))
    after = shifted(grad_pre[:rim], "seq", -1)
    grad_pad = jnp.concatenate([grad_pre, after], axis=0)
    grad_x = conv_weight[rim][None, :] * grad_pad[0:length]
    for tap in range(rim):
        grad_x = grad_x + conv_weight[tap][None, :] * grad_pad[rim - tap : rim - tap + length]
    grad_taps = jnp.stack(
        [jnp.sum(grad_pre * padded[tap : tap + length], axis=0) for tap in range(KW)]
    )
    channel_grads = jnp.stack([jnp.sum(grad_pre, axis=0), grad_skip, jnp.sum(grad_dt, axis=0)])
    own_sums = jnp.concatenate([grad_alog_local, grad_taps, channel_grads], axis=0)
    own_bc = jnp.stack([jnp.sum(grad_b, axis=-1), jnp.sum(grad_c, axis=-1)])
    own_bc = own_bc.reshape(2, length, states).transpose(0, 2, 1).reshape(2 * states, length)
    layer_out = routed_experts(
        partial_value.astype(jnp.bfloat16),
        resid,
        w_gate,
        w_up,
        w_down,
        route_ids,
        route_weight,
    )
    sums = lax.psum(own_sums, "seq")
    grad_bc = lax.psum(own_bc, "expert").reshape(2, states, length)
    grad_alog = sums[:states]
    grad_conv = sums[states : states + KW]
    grad_chan = sums[states + KW : states + KW + 3]
    return (layer_out, grad_x, grad_z, grad_dt, grad_bc, grad_alog, grad_conv, grad_chan)


def solution(mesh):
    in_specs = (
        P("seq", "expert"),
        P("seq", "expert"),
        P("seq", "expert"),
        P(None, None, "seq"),
        P(None, "expert"),
        P(None, "expert"),
        P("expert"),
        P("expert"),
        P("expert"),
        P("expert", None),
        P(("seq", "expert"), None),
        P("expert", None, "seq"),
        P("expert", None, "seq"),
        P("expert", "seq", None),
        P(("seq", "expert"), None),
        P(("seq", "expert"), None),
        P("seq", None),
    )
    out_specs = (
        P(("seq", "expert"), None),
        P("seq", "expert"),
        P("seq", "expert"),
        P("seq", "expert"),
        P(None, None, "seq"),
        P(None, "expert"),
        P(None, "expert"),
        P(None, "expert"),
    )
    return jax.shard_map(local, mesh=mesh, in_specs=in_specs, out_specs=out_specs, check_vma=False)
```

```python
import functools

import jax
import jax.numpy as jnp
from jax import lax
from jax.experimental import pallas as pl
from jax.experimental.pallas import tpu as pltpu
from jax.sharding import PartitionSpec as P

KW = 4
SUB = 8
LANES = 128


def shifted(x, axis, by):
    peers = lax.axis_size(axis)
    pairs = [(i, i + by) for i in range(peers) if 0 <= i + by < peers]
    return lax.ppermute(x, axis, pairs)


def wide(tile, width):
    return jnp.concatenate([tile] * (width // tile.shape[1]), axis=1)


def folded(value):
    total = value[:, :LANES]
    for at in range(LANES, value.shape[1], LANES):
        total = total + value[:, at : at + LANES]
    return total


def totals_kernel(step_ref, drive_ref, grad_ref, b_ref, c_ref, rate_ref, out_ref):
    rate = rate_ref[...]
    width = rate.shape[1]

    def advance(i, carry):
        state, passed, leaving = carry
        for j in range(SUB):
            decay = jnp.exp(step_ref[i, j : j + 1, :] * rate)
            state = decay * state + drive_ref[i, j : j + 1, :] * wide(b_ref[i, j], width)
            passed = passed * decay
            leaving = leaving + passed * (grad_ref[i, j : j + 1, :] * wide(c_ref[i, j], width))
        return (state, passed, leaving)

    zero = jnp.zeros_like(rate)
    state, passed, leaving = lax.fori_loop(
        0, step_ref.shape[0], advance, (zero, jnp.ones_like(rate), zero)
    )
    out_ref[0] = passed.astype(out_ref.dtype)
    out_ref[1] = state.astype(out_ref.dtype)
    out_ref[2] = leaving.astype(out_ref.dtype)


def forward_kernel(step_ref, drive_ref, b_ref, c_ref, rate_ref, start_ref, y_ref):
    rate = rate_ref[...]
    width = rate.shape[1]

    def advance(i, state):
        for j in range(SUB):
            decay = jnp.exp(step_ref[i, j : j + 1, :] * rate)
            state = decay * state + drive_ref[i, j : j + 1, :] * wide(b_ref[i, j], width)
            y_ref[i, j : j + 1, :] = jnp.sum(
                wide(c_ref[i, j], width) * state, axis=0, keepdims=True
            )
        return state

    lax.fori_loop(0, step_ref.shape[0], advance, start_ref[...])


def backward_kernel(
    step_ref,
    drive_ref,
    conv_ref,
    grad_ref,
    b_ref,
    c_ref,
    rate_ref,
    start_ref,
    arriving_ref,
    step_out_ref,
    conv_out_ref,
    b_out_ref,
    c_out_ref,
    alog_ref,
    states,
):
    rate = rate_ref[...]
    width = rate.shape[1]
    groups = step_ref.shape[0]

    @pl.when(pl.program_id(0) == 0)
    def _():
        b_out_ref[...] = jnp.zeros_like(b_out_ref)
        c_out_ref[...] = jnp.zeros_like(c_out_ref)

    states[0] = start_ref[...]

    def advance(i, state):
        for j in range(SUB):
            decay = jnp.exp(step_ref[i, j : j + 1, :] * rate)
            state = decay * state + drive_ref[i, j : j + 1, :] * wide(b_ref[i, j], width)
            states[i * SUB + j + 1] = state
        return state

    lax.fori_loop(0, groups, advance, start_ref[...])

    def retreat(k, carry):
        flow, alog_sum = carry
        i = groups - 1 - k
        for j in reversed(range(SUB)):
            at = i * SUB + j
            step_now = step_ref[i, j : j + 1, :]
            grad_now = grad_ref[i, j : j + 1, :]
            decay = jnp.exp(step_now * rate)
            adjoint = wide(c_ref[i, j], width) * grad_now + flow
            flow = decay * adjoint
            held = flow * states[at]
            alog_sum = alog_sum + step_now * held
            into_drive = jnp.sum(adjoint * wide(b_ref[i, j], width), axis=0, keepdims=True)
            step_out_ref[i, j : j + 1, :] = (
                jnp.sum(rate * held, axis=0, keepdims=True)
                + conv_ref[i, j : j + 1, :] * into_drive
            )
            conv_out_ref[i, j : j + 1, :] = step_now * into_drive
            b_out_ref[i, j] += folded(adjoint * drive_ref[i, j : j + 1, :])
            c_out_ref[i, j] += folded(grad_now * states[at + 1])
        return (flow, alog_sum)

    _, alog_sum = lax.fori_loop(0, groups, retreat, (arriving_ref[...], jnp.zeros_like(rate)))
    alog_ref[...] = alog_sum * rate


def sweeps(length, channels, states):
    block = min(512, channels)
    groups = length // SUB
    rows = pl.BlockSpec((groups, SUB, block), lambda k: (0, 0, k))
    spread = pl.BlockSpec((groups, SUB, states, LANES), lambda k: (0, 0, 0, 0))
    column = pl.BlockSpec((states, block), lambda k: (0, k))
    grid = (channels // block,)
    f32 = jnp.float32
    row_shape = jax.ShapeDtypeStruct((groups, SUB, channels), f32)
    spread_shape = jax.ShapeDtypeStruct((groups, SUB, states, LANES), f32)
    column_shape = jax.ShapeDtypeStruct((states, channels), f32)
    totals = pl.pallas_call(
        totals_kernel,
        grid=grid,
        in_specs=[rows, rows, rows, spread, spread, column],
        out_specs=pl.BlockSpec((3, states, block), lambda k: (0, 0, k)),
        out_shape=jax.ShapeDtypeStruct((3, states, channels), jnp.bfloat16),
        name="totals",
    )
    forward = pl.pallas_call(
        forward_kernel,
        grid=grid,
        in_specs=[rows, rows, spread, spread, column, column],
        out_specs=rows,
        out_shape=row_shape,
        name="forward",
    )
    backward = pl.pallas_call(
        backward_kernel,
        grid=grid,
        in_specs=[rows, rows, rows, rows, spread, spread, column, column, column],
        out_specs=[rows, rows, spread, spread, column],
        out_shape=[row_shape, row_shape, spread_shape, spread_shape, column_shape],
        scratch_shapes=[pltpu.VMEM((length + 1, states, block), f32)],
        name="backward",
    )
    return totals, forward, backward


MESH = pl.DeviceIdType.MESH
GROUP = 16


def places():
    s, z = lax.axis_index("seq"), lax.axis_index("expert")
    core = lax.rem(s, 2)
    sib = s + 1 - 2 * core
    across_x = s + 2 - 4 * lax.rem(lax.div(s, 2), 2)
    across_y = s + 4 - 8 * lax.div(s, 4)
    return s, z, core, sib, across_x, across_y


def transposed(a, b):
    return lax.dot_general(a, b, (((1,), (1,)), ((), ())), preferred_element_type=jnp.float32)


def layer_kernel(
    x_ref,
    z_ref,
    dt_ref,
    bc_ref,
    alog_ref,
    conv_ref,
    bias_ref,
    gain_ref,
    dtb_ref,
    resid_ref,
    ids_ref,
    weight_ref,
    ow_hbm,
    gm_hbm,
    wg_hbm,
    wu_hbm,
    wd_hbm,
    out_ref,
    gx_ref,
    gz_ref,
    gdt_ref,
    alog_out,
    taps_out,
    chan_out,
    bc_out,
    gx_buf,
    gz_buf,
    gdt_buf,
    rows_all,
    wgu,
    wd,
    ow,
    gm,
    hidden,
    own_h,
    zrecv,
    zfin,
    part,
    psib,
    acc,
    rx,
    ry,
    rdx,
    rdy,
    fin,
    p_buf,
    sums_own,
    sums_recv,
    sums_acc,
    bc_own,
    bc_recv,
    decays,
    states,
    b_wide,
    c_wide,
    b_block,
    c_block,
    step_buf,
    drive_buf,
    conv_buf,
    grad_buf,
    dsilu_buf,
    dtsig_buf,
    zgate_buf,
    zfac_buf,
    into_buf,
    qsum_buf,
    xpad,
    gpad,
    xhalo,
    ghalo,
    gated,
    adj,
    quo,
    gb_acc,
    gc_acc,
    tot,
    tsib,
    tpair,
    trecv,
    rate_buf,
    start_buf,
    arrive_buf,
    w_sem,
    sems,
):
    s, z, core, sib, ax, ay = places()
    diag = ax + ay - s
    f32, bf16 = jnp.float32, jnp.bfloat16
    ways, seqs = 4, 8
    rows = resid_ref.shape[0]
    length, channels = x_ref.shape
    width = resid_ref.shape[1]
    half = width // 2
    scan = channels // 2
    groups = length // GROUP
    nst = alog_ref.shape[0]
    flat = GROUP * nst
    tiles = wgu.shape[1] // 256
    after = lax.rem(s + 1, seqs)
    ahead = lax.rem(s + seqs - 1, seqs)
    count = [0]
    everything = []

    def to(src, dst, seq, exp):
        index = count[0]
        count[0] += 1
        copy = pltpu.make_async_remote_copy(
            src_ref=src,
            dst_ref=dst,
            send_sem=sems.at[0, index],
            recv_sem=sems.at[1, index],
            device_id=(seq, exp),
            device_id_type=MESH,
        )
        everything.append(copy)
        return copy

    first = [
        pltpu.make_async_copy(ow_hbm, ow, w_sem.at[0]),
        pltpu.make_async_copy(gm_hbm, gm, w_sem.at[1]),
    ]
    for load in first:
        load.start()
    loads = []
    for t in range(tiles):
        for k, w_hbm in enumerate((wg_hbm, wu_hbm)):
            loads.append(
                pltpu.make_async_copy(
                    w_hbm.at[0, :, pl.ds(t * 128, 128)],
                    wgu.at[:, pl.ds(t * 256 + k * 128, 128)],
                    w_sem.at[2 + 2 * t + k],
                )
            )
    loads.append(pltpu.make_async_copy(wd_hbm.at[0], wd, w_sem.at[2 + 2 * tiles]))

    zs = [lax.rem(z + d, ways) for d in range(ways)]
    zb = [lax.rem(z + ways - d, ways) for d in range(ways)]

    barrier = pltpu.get_barrier_semaphore()
    partners = [(sib, z), (ax, z), (ay, z), (diag, z), (after, z), (ahead, z)]
    partners += [(s, zs[1]), (s, zs[2]), (s, zs[3])]
    for seq, exp in partners:
        pl.semaphore_signal(barrier, inc=1, device_id=(seq, exp), device_id_type=MESH)
    pl.semaphore_wait(barrier, len(partners))

    halo = to(x_ref.at[pl.ds(length - GROUP, GROUP), :], xhalo, after, z)
    halo.start()

    for k, spread in enumerate((b_wide, c_wide)):
        value = bc_ref[k]
        for t in range(length):
            spread[t] = jnp.broadcast_to(value[:, t : t + 1], (nst, LANES))
    lane = lax.broadcasted_iota(jnp.int32, (length, flat), 1)
    row = lax.broadcasted_iota(jnp.int32, (length, flat), 0)
    same_token = lax.div(lane, nst) == lax.rem(row, GROUP)
    lane_r = lax.broadcasted_iota(jnp.int32, (nst, flat), 1)
    row_r = lax.broadcasted_iota(jnp.int32, (nst, flat), 0)
    unit = (lax.rem(lane_r, nst) == row_r).astype(f32)
    repeat = unit.astype(bf16)
    for k, block_ref in enumerate((b_block, c_block)):
        by_token = jnp.transpose(bc_ref[k]).astype(bf16)
        laid = jnp.dot(by_token, repeat, preferred_element_type=f32)
        block_ref[...] = jnp.where(same_token, laid, 0.0).astype(bf16)
    diagonal = same_token[:GROUP].astype(f32)
    ones_block = diagonal.astype(bf16)
    rate_buf[...] = -jnp.exp(alog_ref[...])

    for load in first:
        load.wait()

    def mix_tile(t, _):
        at = pl.ds(pl.multiple_of(t * 256, 256), 256)
        zfac_buf[:, :, at] = transposed(gm[...], ow[at, :]).reshape(groups, GROUP, 256)
        return 0

    lax.fori_loop(0, channels // 256, mix_tile, 0, unroll=True)
    for load in loads:
        load.start()
    xpad[8 : 8 + length, :] = x_ref[...].astype(f32)
    halo.wait_recv()
    xpad[0:8, :] = jnp.where(s > 0, xhalo[...].astype(f32)[GROUP - 8 :], 0.0)

    def prepare(t, _):
        at = pl.ds(pl.multiple_of(t * LANES, LANES), LANES)

        def put(ref, value):
            ref[:, :, at] = value.reshape(groups, GROUP, LANES)

        pre = bias_ref[:, at] + conv_ref[0:1, at] * xpad[5 : 5 + length, at]
        for tap in range(1, KW):
            pre = pre + conv_ref[tap : tap + 1, at] * xpad[5 + tap : 5 + tap + length, at]
        conv_sig = jax.nn.sigmoid(pre)
        conv_out = pre * conv_sig
        put(conv_buf, conv_out)
        put(dsilu_buf, conv_sig * (1.0 + pre * (1.0 - conv_sig)))
        raw = dt_ref[:, at] + dtb_ref[:, at]
        step = jnp.maximum(raw, 0.0) + jnp.log1p(jnp.exp(-jnp.abs(raw)))
        put(step_buf, step)
        put(drive_buf, step * conv_out)
        put(dtsig_buf, jax.nn.sigmoid(raw))
        z_val = z_ref[:, at].astype(f32)
        z_sig = jax.nn.sigmoid(z_val)
        mixed = zfac_buf[:, :, at].reshape(length, LANES)
        gate = z_val * z_sig
        put(zgate_buf, gate)
        put(grad_buf, mixed * gate)
        put(zfac_buf, mixed * z_sig * (1.0 + z_val * (1.0 - z_sig)))
        return 0

    lax.fori_loop(0, channels // LANES, prepare, 0)

    def lanes(k):
        return pl.ds(k * scan, scan)

    def totals(k, low, high, carry):
        at = lanes(k)
        rate = rate_buf[:, at]

        def advance(i, carry):
            state, passed, leaving = carry
            for j in range(GROUP):
                decay = jnp.exp(step_buf[i, j : j + 1, at] * rate)
                decays[i * GROUP + j, :, at] = decay
                state = decay * state + drive_buf[i, j : j + 1, at] * wide(
                    b_wide[i * GROUP + j], scan
                )
                passed = passed * decay
                leaving = leaving + passed * (
                    grad_buf[i, j : j + 1, at] * wide(c_wide[i * GROUP + j], scan)
                )
            return (state, passed, leaving)

        return lax.fori_loop(low, high, advance, carry)

    zero = jnp.zeros((nst, scan), f32)
    nothing = (zero, jnp.ones_like(zero), zero)

    def keep(k, carry):
        for m in range(3):
            tot[k, m] = carry[m].astype(bf16)

    beside = [to(tot.at[k], tsib.at[k], sib, z) for k in range(2)]
    xbit, ybit = lax.rem(lax.div(s, 2), 2), lax.div(s, 4)
    beyond = []
    for k in range(2):
        for m, (seq, bit) in enumerate(((ax, xbit), (ay, ybit), (diag, ybit))):
            at = pl.ds(bit, 2)
            beyond.append(to(tpair.at[k, at], trecv.at[k, m, at], seq, z))

    def join(k):
        beside[k].wait_recv()
        own = [tot[k, m].astype(f32) for m in range(3)]
        their = [tsib[k, m].astype(f32) for m in range(3)]
        one = [jnp.where(core == 0, a, b) for a, b in zip(own, their)]
        two = [jnp.where(core == 0, b, a) for a, b in zip(own, their)]
        tpair[k, 0] = (two[1] * one[0] + two[0]).astype(bf16)
        tpair[k, 1] = (one[1] * two[1]).astype(bf16)
        tpair[k, 2] = (one[2] + one[1] * two[2]).astype(bf16)
        for copy in beyond[3 * k : 3 * k + 3]:
            copy.start()

    def enter(k):
        for copy in beyond[3 * k : 3 * k + 3]:
            copy.wait_recv()
        chip = lax.div(s, 2)
        start, arriving = zero, zero

        def other_chip(c):
            relation = (c % 2 + xbit - 2 * (c % 2) * xbit) + 2 * (c // 2 + ybit - 2 * (c // 2) * ybit)
            return trecv.at[k, jnp.maximum(relation - 1, 0)]

        for c in range(4):
            at = other_chip(c)
            start = jnp.where(c < chip, at[1].astype(f32) * start + at[0].astype(f32), start)
            at = other_chip(3 - c)
            arriving = jnp.where(
                3 - c > chip, at[1].astype(f32) * arriving + at[2].astype(f32), arriving
            )
        passed = tsib[k, 1].astype(f32)
        start = jnp.where(core == 1, passed * start + tsib[k, 0].astype(f32), start)
        arriving = jnp.where(core == 0, passed * arriving + tsib[k, 2].astype(f32), arriving)
        start_buf[:, lanes(k)] = start
        arrive_buf[:, lanes(k)] = arriving

    keep(0, totals(0, 0, groups, nothing))
    beside[0].start()
    middle = totals(1, 0, groups // 2, nothing)
    join(0)
    keep(1, totals(1, groups // 2, groups, middle))
    beside[1].start()
    join(1)

    def state_rows(at, number):
        return pl.ds(pl.multiple_of(at * nst, nst), number * nst)

    def forward(k):
        at = lanes(k)
        states[0:nst, at] = start_buf[:, at].astype(bf16)

        def advance(i, state):
            for j in range(GROUP):
                t = i * GROUP + j
                state = decays[t, :, at] * state + drive_buf[i, j : j + 1, at] * wide(
                    b_wide[t], scan
                )
                states[state_rows(t + 1, 1), at] = state.astype(bf16)
            here = pl.ds(pl.multiple_of(i * GROUP, GROUP), GROUP)
            y_val = jnp.dot(
                c_block[here, :],
                states[state_rows(i * GROUP + 1, GROUP), at],
                preferred_element_type=f32,
            )
            y_val = y_val + gain_ref[:, at] * conv_buf[i, :, at]
            gz_buf[here, at] = zfac_buf[i, :, at] * y_val
            gated[here, at] = (zgate_buf[i, :, at] * y_val).astype(bf16)
            return state

        lax.fori_loop(0, groups, advance, start_buf[:, at])

    for k in range(2):
        enter(k)
        forward(k)

    written = [
        pltpu.make_async_copy(gz_buf, gz_ref, w_sem.at[3 + 2 * tiles]),
        pltpu.make_async_copy(gdt_buf, gdt_ref, w_sem.at[4 + 2 * tiles]),
        pltpu.make_async_copy(gx_buf, gx_ref, w_sem.at[5 + 2 * tiles]),
    ]
    written[0].start()

    waves = 2
    piece = rows // waves
    pack = ways * piece

    def block(seq, exp, w):
        at = (w * seqs + seq) * pack + exp * piece
        return pl.ds(pl.multiple_of(at, piece), piece)

    def within(exp, w):
        return pl.ds(pl.multiple_of(exp * rows + w * piece, piece), piece)

    def project(t, _):
        at = pl.ds(pl.multiple_of(t * 256, 256), 256)
        p_buf[:, at] = jnp.dot(gated[...], ow[:, at], preferred_element_type=f32).astype(bf16)
        return 0

    lax.fori_loop(0, width // 256, project, 0, unroll=True)

    z_out = [
        [to(p_buf.at[within(zs[d], w)], zrecv.at[w, d - 1], s, zs[d]) for d in (1, 2, 3)]
        for w in range(waves)
    ]
    for copy in z_out[0]:
        copy.start()

    gb_acc[...] = jnp.zeros_like(gb_acc)
    gc_acc[...] = jnp.zeros_like(gc_acc)

    def backward(k):
        at = lanes(k)

        def retreat(n, carry):
            flow, alog_sum = carry
            i = groups - 1 - n
            for j in reversed(range(GROUP)):
                t = i * GROUP + j
                adjoint = wide(c_wide[t], scan) * grad_buf[i, j : j + 1, at] + flow
                adj[j * nst : (j + 1) * nst, :] = adjoint.astype(bf16)
                flow = decays[t, :, at] * adjoint
                share = rate_buf[:, at] * (flow * states[state_rows(t, 1), at].astype(f32))
                alog_sum = alog_sum + step_buf[i, j : j + 1, at] * share
                quo[j * nst : (j + 1) * nst, :] = share.astype(bf16)
            here = pl.ds(pl.multiple_of(i * GROUP, GROUP), GROUP)
            into_buf[i, :, at] = jnp.dot(b_block[here, :], adj[...], preferred_element_type=f32)
            qsum_buf[i, :, at] = jnp.dot(ones_block, quo[...], preferred_element_type=f32)
            gb_acc[i] += transposed(drive_buf[i, :, at].astype(bf16), adj[...])
            gc_acc[i] += transposed(
                grad_buf[i, :, at].astype(bf16), states[state_rows(i * GROUP + 1, GROUP), at]
            )
            return (flow, alog_sum)

        _, alog_sum = lax.fori_loop(0, groups, retreat, (arrive_buf[:, at], zero))
        sums_own[0:nst, at] = alog_sum

    gather, to_x, to_y, to_b, forward = [], [], [], [], []
    for w in range(waves):
        here = rows_all.at[block(s, z, w)]
        gather.append([to(here, here, s, zs[d]) for d in (1, 2, 3)])
        blocks = [rows_all.at[block(s, zb[d], w)] for d in range(ways)]
        to_x.append([to(at, at, ax, z) for at in blocks])
        to_y.append([to(at, at, ay, z) for at in blocks])
        to_b.append([to(at, at, sib, z) for at in blocks])
        passing = []
        for d in range(ways):
            origin, target = (ay, ax) if d < 2 else (ax, ay)
            at = rows_all.at[block(origin, zb[d], w)]
            passing.append(to(at, at, target, z))
        forward.append(passing)

    def mixed_rows(w):
        for copy in z_out[w]:
            copy.wait_recv()
        own = pl.ds(w * piece, piece)
        total = resid_ref[own, :].astype(f32) + p_buf[within(z, w), :].astype(f32)
        for d in range(3):
            total = total + zrecv[w, d].astype(f32)
        own_h[own, :] = total.astype(bf16)
        rows_all[block(s, z, w), :] = total.astype(bf16)
        for copy in gather[w] + [to_x[w][0], to_y[w][0], to_b[w][0]]:
            copy.start()

    def spread_rows(w):
        for d in (1, 2, 3):
            gather[w][d - 1].wait_recv()
            to_x[w][d].start()
            to_y[w][d].start()
            to_b[w][d].start()

    backward(0)
    for copy in z_out[1]:
        copy.start()
    mixed_rows(0)
    backward(1)
    mixed_rows(1)
    for k, held in enumerate((gb_acc, gc_acc)):
        kept = jnp.where(same_token, held[...].reshape(length, flat), 0.0)
        bc_own[k] = lax.dot_general(
            unit,
            kept,
            (((1,), (1,)), ((), ())),
            precision=lax.Precision.HIGHEST,
            preferred_element_type=f32,
        )
    bc_copies = [to(bc_own, bc_recv.at[d - 1], s, zs[d]) for d in (1, 2, 3)]
    for copy in bc_copies:
        copy.start()

    def finish(t, _):
        at = pl.ds(pl.multiple_of(t * LANES, LANES), LANES)

        def get(ref):
            return ref[:, :, at].reshape(length, LANES)

        def total(value):
            return jnp.sum(value, axis=0, keepdims=True)

        into, conv_out, grad_y = get(into_buf), get(conv_buf), get(grad_buf)
        grad_dt = (get(qsum_buf) + conv_out * into) * get(dtsig_buf)
        gdt_buf[:, at] = grad_dt
        grad_pre = (gain_ref[:, at] * grad_y + get(step_buf) * into) * get(dsilu_buf)
        gpad[0:length, at] = grad_pre
        for tap in range(KW):
            sums_own[nst + tap : nst + tap + 1, at] = total(
                grad_pre * xpad[5 + tap : 5 + tap + length, at]
            )
        sums_own[nst + KW : nst + KW + 1, at] = total(grad_pre)
        sums_own[nst + KW + 1 : nst + KW + 2, at] = total(grad_y * conv_out)
        sums_own[nst + KW + 2 : nst + KW + 3, at] = total(grad_dt)
        return 0

    lax.fori_loop(0, channels // LANES, finish, 0)
    spread_rows(0)
    written[1].start()
    sums_own[nst + KW + 3 :, :] = jnp.zeros_like(sums_own[nst + KW + 3 :, :])
    rim = to(gpad.at[pl.ds(0, 8)], ghalo, ahead, z)
    rim.start()
    sums_copies = [
        to(sums_own, sums_recv.at[0], sib, z),
        to(sums_acc.at[0], sums_recv.at[1], ax, z),
        to(sums_acc.at[1], sums_recv.at[2], ay, z),
    ]
    sums_copies[0].start()

    sums_copies[0].wait_recv()
    sums_acc[0] = sums_own[...] + sums_recv[0]
    sums_copies[1].start()
    rim.wait_recv()
    gpad[length : length + 8, :] = jnp.where(s < seqs - 1, ghalo[...], 0.0)

    def spread_back(t, _):
        at = pl.ds(pl.multiple_of(t * LANES, LANES), LANES)
        grad_x = conv_ref[KW - 1 : KW, at] * gpad[0:length, at]
        for tap in range(KW - 1):
            away = KW - 1 - tap
            grad_x = grad_x + conv_ref[tap : tap + 1, at] * gpad[away : away + length, at]
        gx_buf[:, at] = grad_x
        return 0

    lax.fori_loop(0, channels // LANES, spread_back, 0)
    written[2].start()
    to_y[0][0].wait_recv()
    forward[0][0].start()

    sums_copies[1].wait_recv()
    sums_acc[1] = sums_acc[0] + sums_recv[1]
    sums_copies[2].start()

    for copy in bc_copies:
        copy.wait_recv()
    bc_out[...] = (bc_own[...] + bc_recv[0]) + (bc_recv[1] + bc_recv[2])

    def up(w, seq):
        first_row = (w * seqs + 4 * lax.div(seq, 4)) * pack
        at = pl.ds(pl.multiple_of(first_row, 4 * pack), 4 * pack)

        def tile(t, _):
            both = jnp.dot(
                rows_all[at, :],
                wgu[:, pl.ds(pl.multiple_of(t * 256, 256), 256)],
                preferred_element_type=f32,
            )
            gate, upper = both[:, :128], both[:, 128:]
            value = gate * jax.nn.sigmoid(gate) * upper
            hidden[:, pl.ds(pl.multiple_of(t * 128, 128), 128)] = value.astype(bf16)
            return 0

        lax.fori_loop(0, tiles, tile, 0, unroll=True)

    quarter = width // 4
    order = (0, 2, 1, 3)

    def cols(h):
        return pl.ds(h * quarter, quarter)

    def small(h):
        return pl.ds((h % 2) * quarter, quarter)

    def part_rows(r, of_core):
        side = xbit if r % 2 == 0 else 1 - xbit
        return pl.ds(pl.multiple_of((2 * side + of_core) * pack, pack), pack)

    pair = {}

    def down(w, r0, h):
        g = 2 * w + r0 // 2
        part[g, :, cols(h)] = jnp.dot(
            hidden[...], wd[:, cols(h)], preferred_element_type=f32
        ).astype(bf16)
        for r in (r0, r0 + 1):
            copy = to(
                part.at[g, part_rows(r, 1 - core), cols(h)], psib.at[w, r, :, cols(h)], sib, z
            )
            copy.start()
            pair[w, r, h] = copy

    def paired(w, r, h):
        pair[w, r, h].wait_recv()
        acc[w, r, :, cols(h)] = (
            part[2 * w + r // 2, part_rows(r, core), cols(h)].astype(f32)
            + psib[w, r, :, cols(h)].astype(f32)
        ).astype(bf16)

    def pack_of(seq, w):
        at = (w * seqs + seq) * pack
        return rows_all.at[pl.ds(pl.multiple_of(at, pack), pack)]

    share_out = [[to(pack_of(o, w), pack_of(o, w), sib, z) for o in (ax, ay, diag)] for w in range(waves)]
    send = {}

    def reduce_out(name, src, dst, seq):
        copy = to(src, dst, seq, z)
        copy.start()
        send[name] = copy

    def to_across_x(w, h):
        reduce_out(("x", w, h), acc.at[w, 1, :, cols(h)], rx.at[w, :, cols(h)], ax)

    def to_across_y(w, h):
        reduce_out(("y", w, h), acc.at[w, 2, :, cols(h)], ry.at[w, :, cols(h)], ay)

    def near(w):
        to_x[w][0].wait_recv()
        to_x[w][1].wait_recv()
        to_y[w][1].wait_recv()
        forward[w][1].start()
        to_x[w][2].wait_recv()
        forward[w][2].start()
        to_x[w][3].wait_recv()
        forward[w][3].start()
        share_out[w][0].start()
        to_y[w][2].wait_recv()
        to_y[w][3].wait_recv()
        share_out[w][1].start()

    def near_ready(w):
        for copy in to_b[w]:
            copy.wait_recv()
        share_out[w][0].wait_recv()

    def far(w):
        for copy in forward[w]:
            copy.wait_recv()
        share_out[w][2].start()

    def far_ready(w):
        share_out[w][1].wait_recv()
        share_out[w][2].wait_recv()

    def diagonal_out(w, h):
        paired(w, 3, h)
        if h < 2:
            reduce_out(("d", w, h), acc.at[w, 3, :, cols(h)], rdx.at[w, :, small(h)], ax)
        else:
            reduce_out(("d", w, h), acc.at[w, 3, :, cols(h)], rdy.at[w, :, small(h)], ay)

    def direct_x(w):
        for h in (0, 1):
            paired(w, 1, h)
            to_across_x(w, h)
        for h in (2, 3):
            paired(w, 1, h)

    def direct_y(w):
        for h in (2, 3):
            paired(w, 2, h)
            to_across_y(w, h)
        for h in (0, 1):
            paired(w, 2, h)
        for h in range(4):
            paired(w, 0, h)

    def joined(w):
        for h in order:
            send["d", w, h].wait_recv()
            r, got = (2, rdx) if h < 2 else (1, rdy)
            acc[w, r, :, cols(h)] = (
                acc[w, r, :, cols(h)].astype(f32) + got[w, :, small(h)].astype(f32)
            ).astype(bf16)
            if h < 2:
                to_across_y(w, h)
            else:
                to_across_x(w, h)

    back = {}

    def reduced(w, h):
        send["x", w, h].wait_recv()
        send["y", w, h].wait_recv()
        total = (
            acc[w, 0, :, cols(h)].astype(f32)
            + rx[w, :, cols(h)].astype(f32)
            + ry[w, :, cols(h)].astype(f32)
        ).astype(bf16)
        fin[w, :, cols(h)] = total
        for d in (1, 2, 3):
            at = pl.ds(pl.multiple_of(zs[d] * piece, piece), piece)
            copy = to(fin.at[w, at, cols(h)], zfin.at[w, d - 1, :, cols(h)], s, zs[d])
            copy.start()
            back[w, h, d] = copy

    eye = lax.broadcasted_iota(jnp.int32, (rows, rows), 0) == lax.broadcasted_iota(
        jnp.int32, (rows, rows), 1
    )

    def column(row):
        return jnp.sum(jnp.where(eye, row, 0.0), axis=1, keepdims=True)

    shares = []
    for d in range(ways):
        mine = [
            jnp.where(ids_ref[k : k + 1, :] == zb[d], weight_ref[k : k + 1, :], 0.0) for k in range(2)
        ]
        shares.append(column(mine[0] + mine[1]))

    def result(w, h):
        own = pl.ds(w * piece, piece)
        at = pl.ds(pl.multiple_of(z * piece, piece), piece)
        total = own_h[own, cols(h)].astype(f32)
        total = total + shares[0][w * piece : (w + 1) * piece] * fin[w, at, cols(h)].astype(f32)
        for d in (1, 2, 3):
            back[w, h, d].wait_recv()
            total = total + shares[d][w * piece : (w + 1) * piece] * zfin[
                w, d - 1, :, cols(h)
            ].astype(f32)
        out_ref[own, cols(h)] = total.astype(bf16)

    spread_rows(1)
    near(0)
    near_ready(0)
    for load in loads:
        load.wait()
    to_y[1][0].wait_recv()
    forward[1][0].start()
    up(0, s)
    far(0)
    for h in range(4):
        down(0, 0, h)
    far_ready(0)
    near(1)
    up(0, ay)
    direct_x(0)
    for h in order:
        down(0, 2, h)
    for h in order:
        diagonal_out(0, h)
    direct_y(0)
    near_ready(1)
    up(1, s)
    far(1)
    for h in range(4):
        down(1, 0, h)
    joined(0)
    direct_x(1)
    far_ready(1)
    up(1, ay)
    for h in order:
        reduced(0, h)
    down(1, 2, 0)
    down(1, 2, 2)
    diagonal_out(1, 0)
    down(1, 2, 1)
    diagonal_out(1, 2)
    down(1, 2, 3)
    diagonal_out(1, 1)
    diagonal_out(1, 3)
    direct_y(1)

    sums_copies[2].wait_recv()
    summed = sums_acc[1] + sums_recv[2]
    alog_out[...] = summed[:nst]
    taps_out[...] = summed[nst : nst + KW]
    chan_out[...] = summed[nst + KW : nst + KW + 3]

    for h in order:
        result(0, h)
    joined(1)
    for h in order:
        reduced(1, h)
    for h in order:
        result(1, h)
    for copy in written:
        copy.wait()
    for copy in everything:
        copy.wait_send()


def deliver_kernel(number, *refs):
    given, results, stops, sem = (
        refs[:number],
        refs[number : 2 * number],
        refs[2 * number : 3 * number],
        refs[3 * number],
    )
    fetch = [pltpu.make_async_copy(given[k], stops[k], sem.at[0, k]) for k in range(number)]
    store = [pltpu.make_async_copy(stops[k], results[k], sem.at[1, k]) for k in range(number)]
    for copy in fetch:
        copy.start()
    for k in range(number):
        fetch[k].wait()
        store[k].start()
    for copy in store:
        copy.wait()


def deliver(arrays):
    number = len(arrays)
    anywhere = pl.BlockSpec(memory_space=pl.ANY)
    return pl.pallas_call(
        functools.partial(deliver_kernel, number),
        out_shape=[jax.ShapeDtypeStruct(a.shape, a.dtype) for a in arrays],
        in_specs=[anywhere] * number,
        out_specs=[anywhere] * number,
        scratch_shapes=[pltpu.VMEM(a.shape, a.dtype) for a in arrays]
        + [pltpu.SemaphoreType.DMA((2, number))],
        name="deliver",
    )(*arrays)


def layer(
    x_in,
    z_in,
    dt_raw,
    bc_in,
    a_log,
    taps,
    bias,
    gain,
    dt_bias,
    resid,
    route_ids,
    route_weight,
    out_weight,
    grad_mix,
    w_gate,
    w_up,
    w_down,
):
    rows, width = resid.shape
    length, channels = x_in.shape
    states = a_log.shape[0]
    units = w_gate.shape[2]
    tiles = units // 128
    seqs = lax.axis_size("seq")
    half, scan, groups = width // 2, channels // 2, length // GROUP
    bf16, f32 = jnp.bfloat16, jnp.float32
    vmem = pl.BlockSpec(memory_space=pltpu.VMEM)
    hbm = pl.BlockSpec(memory_space=pl.ANY)
    sem = pltpu.SemaphoreType.DMA
    flat = GROUP * states

    def held(*shape, kind=f32):
        return pltpu.VMEM(shape, kind)

    def rows_of():
        return held(groups, GROUP, channels)

    summed = (states + 8, channels)
    grads = (2, states, length)
    return pl.pallas_call(
        layer_kernel,
        out_shape=[
            jax.ShapeDtypeStruct((rows, width), bf16),
            jax.ShapeDtypeStruct((length, channels), f32),
            jax.ShapeDtypeStruct((length, channels), f32),
            jax.ShapeDtypeStruct((length, channels), f32),
            jax.ShapeDtypeStruct((states, channels), f32),
            jax.ShapeDtypeStruct((KW, channels), f32),
            jax.ShapeDtypeStruct((3, channels), f32),
            jax.ShapeDtypeStruct(grads, f32),
        ],
        in_specs=[vmem] * 12 + [hbm] * 5,
        out_specs=[vmem] + [hbm] * 3 + [vmem] * 4,
        scratch_shapes=[
            held(length, channels),
            held(length, channels),
            held(length, channels),
            held(seqs * length, width, kind=bf16),
            held(width, 2 * units, kind=bf16),
            held(units, width, kind=bf16),
            held(channels, width, kind=bf16),
            held(length, width, kind=bf16),
            held(2 * length, units, kind=bf16),
            held(rows, width, kind=bf16),
            held(2, 3, rows // 2, width, kind=bf16),
            held(2, 3, rows // 2, width, kind=bf16),
            held(4, 2 * length, width, kind=bf16),
            held(2, 4, length // 2, width, kind=bf16),
            held(2, 4, length // 2, width, kind=bf16),
            held(2, length // 2, width, kind=bf16),
            held(2, length // 2, width, kind=bf16),
            held(2, length // 2, half, kind=bf16),
            held(2, length // 2, half, kind=bf16),
            held(2, length // 2, width, kind=bf16),
            held(length, width, kind=bf16),
            held(*summed),
            held(3, *summed),
            held(2, *summed),
            held(*grads),
            held(3, *grads),
            held(length, states, channels),
            held((length + 1) * states, channels, kind=bf16),
            held(length, states, LANES),
            held(length, states, LANES),
            held(length, flat, kind=bf16),
            held(length, flat, kind=bf16),
        ]
        + [rows_of() for _ in range(10)]
        + [
            held(length + 8, channels),
            held(length + 8, channels),
            held(GROUP, channels, kind=bf16),
            held(8, channels),
            held(length, channels, kind=bf16),
            held(flat, scan, kind=bf16),
            held(flat, scan, kind=bf16),
            held(groups, GROUP, flat),
            held(groups, GROUP, flat),
            held(2, 3, states, scan, kind=bf16),
            held(2, 3, states, scan, kind=bf16),
            held(2, 3, states, scan, kind=bf16),
            held(2, 3, 3, states, scan, kind=bf16),
            held(states, channels),
            held(states, channels),
            held(states, channels),
            sem((2 * tiles + 6,)),
            sem((2, 192)),
        ],
        compiler_params=pltpu.CompilerParams(
            collective_id=0, has_side_effects=True, vmem_limit_bytes=60 << 20
        ),
        cost_estimate=pl.CostEstimate(
            flops=6 * seqs * length * width * units + 4 * length * width * channels,
            bytes_accessed=6 * width * units,
            transcendentals=seqs * length * units + length * channels * states,
        ),
        name="layer",
    )(
        x_in,
        z_in,
        dt_raw,
        bc_in,
        a_log,
        taps,
        bias.reshape(1, channels),
        gain.reshape(1, channels),
        dt_bias.reshape(1, channels),
        resid,
        route_ids.T,
        route_weight.T,
        out_weight,
        grad_mix,
        w_gate,
        w_up,
        w_down,
    )


def entering(everything):
    peers, here = everything.shape[0], lax.axis_index("seq")
    values = everything.astype(jnp.float32)
    start = jnp.zeros_like(values[0, 0])
    arriving = jnp.zeros_like(start)
    for k in range(peers):
        start = jnp.where(k < here, values[k, 0] * start + values[k, 1], start)
        back = peers - 1 - k
        arriving = jnp.where(back > here, values[back, 0] * arriving + values[back, 2], arriving)
    return start, arriving


def routed_experts(partial_value, resid, w_gate, w_up, w_down, route_ids, route_weight):
    rows = resid.shape[0]
    mixed = lax.psum(partial_value, "expert").astype(jnp.float32)
    own = lax.dynamic_slice_in_dim(mixed, lax.axis_index("expert") * rows, rows, 0)
    hidden_in = (resid.astype(jnp.float32) + own).astype(jnp.bfloat16)
    experts = lax.axis_size("expert")
    capacity = 4 * rows // experts
    flat_ids = route_ids.reshape(-1)
    order = jnp.arange(flat_ids.shape[0], dtype=jnp.int32)
    earlier = (flat_ids[:, None] == flat_ids[None, :]) & (order[None, :] < order[:, None])
    rank = jnp.sum(earlier.astype(jnp.int32), axis=1)
    slot = flat_ids * capacity + rank
    placing = (jnp.arange(experts * capacity, dtype=jnp.int32)[:, None] == slot[None, :]).astype(
        jnp.bfloat16
    )
    doubled = jnp.repeat(hidden_in, 2, axis=0)
    outgoing = jnp.dot(placing, doubled, preferred_element_type=jnp.float32).astype(jnp.bfloat16)
    incoming = lax.all_to_all(outgoing, "expert", split_axis=0, concat_axis=0, tiled=True)
    piece = lax.all_gather(incoming, "seq", axis=0, tiled=True)
    gate = jnp.dot(piece, w_gate[0], preferred_element_type=jnp.float32)
    upper = jnp.dot(piece, w_up[0], preferred_element_type=jnp.float32)
    hidden = (jax.nn.silu(gate) * upper).astype(jnp.bfloat16)
    expert_sum = lax.psum_scatter(
        jnp.dot(hidden, w_down[0], preferred_element_type=jnp.float32).astype(jnp.bfloat16),
        "seq",
        scatter_dimension=0,
        tiled=True,
    )
    returned = lax.all_to_all(expert_sum, "expert", split_axis=0, concat_axis=0, tiled=True)
    picked = lax.dot_general(
        placing, returned, (((0,), (0,)), ((), ())), preferred_element_type=jnp.float32
    )
    picked = picked.reshape(rows, 2, -1)
    moe = picked[:, 0] * route_weight[:, 0:1] + picked[:, 1] * route_weight[:, 1:2]
    return (hidden_in.astype(jnp.float32) + moe).astype(jnp.bfloat16)


def local(
    x_in,
    z_in,
    dt_raw,
    bc_in,
    a_log,
    conv_weight,
    conv_bias,
    skip_gain,
    dt_bias,
    out_weight,
    resid,
    w_gate,
    w_up,
    w_down,
    route_ids,
    route_weight,
    grad_mix,
):
    length, channels = x_in.shape
    states = a_log.shape[0]
    rim = KW - 1
    rows = resid.shape[0]
    experts = lax.axis_size("expert")
    if experts == 4 and lax.axis_size("seq") == 8:
        layer_out, grad_x, grad_z, grad_dt, grad_alog, grad_conv, grad_chan, grad_bc = deliver(
            layer(
                x_in,
                z_in,
                dt_raw,
                bc_in,
                a_log,
                conv_weight,
                conv_bias,
                skip_gain,
                dt_bias,
                resid,
                route_ids,
                route_weight,
                out_weight,
                grad_mix,
                w_gate,
                w_up,
                w_down,
            )
        )
        return (layer_out, grad_x, grad_z, grad_dt, grad_bc, grad_alog, grad_conv, grad_chan)
    x_val = x_in.astype(jnp.float32)
    z_val = z_in.astype(jnp.float32)
    before = shifted(x_in[length - rim :], "seq", 1)
    padded = jnp.concatenate([before.astype(jnp.float32), x_val], axis=0)
    pre = conv_bias[None, :] + conv_weight[0][None, :] * padded[0:length]
    for tap in range(1, KW):
        pre = pre + conv_weight[tap][None, :] * padded[tap : tap + length]
    conv_sig = jax.nn.sigmoid(pre)
    conv_out = pre * conv_sig
    step = jax.nn.softplus(dt_raw + dt_bias[None, :])
    rate = -jnp.exp(a_log)
    drive = step * conv_out
    z_sig = jax.nn.sigmoid(z_val)
    back_mix = lax.dot_general(
        grad_mix, out_weight, (((1,), (1,)), ((), ())), preferred_element_type=jnp.float32
    )
    grad_y = back_mix * z_val * z_sig

    def grouped(array):
        return array.reshape(length // SUB, SUB, channels)

    def flat(array):
        return array.reshape(length, channels)

    spread = jnp.broadcast_to(
        bc_in.transpose(0, 2, 1)[:, :, :, None], (2, length, states, LANES)
    ).reshape(2, length // SUB, SUB, states, LANES)
    b_wide, c_wide = spread[0], spread[1]
    totals, forward, backward = sweeps(length, channels, states)
    step_g, drive_g, grad_g, conv_g = (grouped(a) for a in (step, drive, grad_y, conv_out))
    own_totals = totals(step_g, drive_g, grad_g, b_wide, c_wide, rate)
    start, arriving = entering(lax.all_gather(own_totals, "seq"))
    y_val = flat(forward(step_g, drive_g, b_wide, c_wide, rate, start))
    y_val = y_val + skip_gain[None, :] * conv_out
    gated = (y_val * z_val * z_sig).astype(jnp.bfloat16)
    partial_value = jnp.dot(gated, out_weight, preferred_element_type=jnp.float32)
    grad_z = back_mix * y_val * z_sig * (1.0 + z_val * (1.0 - z_sig))
    grad_step, conv_part_grad, grad_b, grad_c, grad_alog_local = backward(
        step_g, drive_g, conv_g, grad_g, b_wide, c_wide, rate, start, arriving
    )
    grad_step, conv_part_grad = flat(grad_step), flat(conv_part_grad)
    grad_conv_out = skip_gain[None, :] * grad_y + conv_part_grad
    grad_skip = jnp.sum(grad_y * conv_out, axis=0)
    grad_dt = grad_step * jax.nn.sigmoid(dt_raw + dt_bias[None, :])
    grad_pre = grad_conv_out * (conv_sig * (1.0 + pre * (1.0 - conv_sig)))
    after = shifted(grad_pre[:rim], "seq", -1)
    grad_pad = jnp.concatenate([grad_pre, after], axis=0)
    grad_x = conv_weight[rim][None, :] * grad_pad[0:length]
    for tap in range(rim):
        grad_x = grad_x + conv_weight[tap][None, :] * grad_pad[rim - tap : rim - tap + length]
    grad_taps = jnp.stack(
        [jnp.sum(grad_pre * padded[tap : tap + length], axis=0) for tap in range(KW)]
    )
    channel_grads = jnp.stack([jnp.sum(grad_pre, axis=0), grad_skip, jnp.sum(grad_dt, axis=0)])
    own_sums = jnp.concatenate([grad_alog_local, grad_taps, channel_grads], axis=0)
    own_bc = jnp.stack([jnp.sum(grad_b, axis=-1), jnp.sum(grad_c, axis=-1)])
    own_bc = own_bc.reshape(2, length, states).transpose(0, 2, 1).reshape(2 * states, length)
    layer_out = routed_experts(
        partial_value.astype(jnp.bfloat16),
        resid,
        w_gate,
        w_up,
        w_down,
        route_ids,
        route_weight,
    )
    sums = lax.psum(own_sums, "seq")
    grad_bc = lax.psum(own_bc, "expert").reshape(2, states, length)
    grad_alog = sums[:states]
    grad_conv = sums[states : states + KW]
    grad_chan = sums[states + KW : states + KW + 3]
    return (layer_out, grad_x, grad_z, grad_dt, grad_bc, grad_alog, grad_conv, grad_chan)


def solution(mesh):
    in_specs = (
        P("seq", "expert"),
        P("seq", "expert"),
        P("seq", "expert"),
        P(None, None, "seq"),
        P(None, "expert"),
        P(None, "expert"),
        P("expert"),
        P("expert"),
        P("expert"),
        P("expert", None),
        P(("seq", "expert"), None),
        P("expert", None, "seq"),
        P("expert", None, "seq"),
        P("expert", "seq", None),
        P(("seq", "expert"), None),
        P(("seq", "expert"), None),
        P("seq", None),
    )
    out_specs = (
        P(("seq", "expert"), None),
        P("seq", "expert"),
        P("seq", "expert"),
        P("seq", "expert"),
        P(None, None, "seq"),
        P(None, "expert"),
        P(None, "expert"),
        P(None, "expert"),
    )
    return jax.shard_map(local, mesh=mesh, in_specs=in_specs, out_specs=out_specs, check_vma=False)
```

```python
import functools

import jax
import jax.numpy as jnp
from jax import lax
from jax.experimental import pallas as pl
from jax.experimental.pallas import tpu as pltpu
from jax.sharding import PartitionSpec as P

KW = 4
SUB = 8
LANES = 128


def shifted(x, axis, by):
    peers = lax.axis_size(axis)
    pairs = [(i, i + by) for i in range(peers) if 0 <= i + by < peers]
    return lax.ppermute(x, axis, pairs)


def wide(tile, width):
    return jnp.concatenate([tile] * (width // tile.shape[1]), axis=1)


def folded(value):
    total = value[:, :LANES]
    for at in range(LANES, value.shape[1], LANES):
        total = total + value[:, at : at + LANES]
    return total


def totals_kernel(step_ref, drive_ref, grad_ref, b_ref, c_ref, rate_ref, out_ref):
    rate = rate_ref[...]
    width = rate.shape[1]

    def advance(i, carry):
        state, passed, leaving = carry
        for j in range(SUB):
            decay = jnp.exp(step_ref[i, j : j + 1, :] * rate)
            state = decay * state + drive_ref[i, j : j + 1, :] * wide(b_ref[i, j], width)
            passed = passed * decay
            leaving = leaving + passed * (grad_ref[i, j : j + 1, :] * wide(c_ref[i, j], width))
        return (state, passed, leaving)

    zero = jnp.zeros_like(rate)
    state, passed, leaving = lax.fori_loop(
        0, step_ref.shape[0], advance, (zero, jnp.ones_like(rate), zero)
    )
    out_ref[0] = passed.astype(out_ref.dtype)
    out_ref[1] = state.astype(out_ref.dtype)
    out_ref[2] = leaving.astype(out_ref.dtype)


def forward_kernel(step_ref, drive_ref, b_ref, c_ref, rate_ref, start_ref, y_ref):
    rate = rate_ref[...]
    width = rate.shape[1]

    def advance(i, state):
        for j in range(SUB):
            decay = jnp.exp(step_ref[i, j : j + 1, :] * rate)
            state = decay * state + drive_ref[i, j : j + 1, :] * wide(b_ref[i, j], width)
            y_ref[i, j : j + 1, :] = jnp.sum(
                wide(c_ref[i, j], width) * state, axis=0, keepdims=True
            )
        return state

    lax.fori_loop(0, step_ref.shape[0], advance, start_ref[...])


def backward_kernel(
    step_ref,
    drive_ref,
    conv_ref,
    grad_ref,
    b_ref,
    c_ref,
    rate_ref,
    start_ref,
    arriving_ref,
    step_out_ref,
    conv_out_ref,
    b_out_ref,
    c_out_ref,
    alog_ref,
    states,
):
    rate = rate_ref[...]
    width = rate.shape[1]
    groups = step_ref.shape[0]

    @pl.when(pl.program_id(0) == 0)
    def _():
        b_out_ref[...] = jnp.zeros_like(b_out_ref)
        c_out_ref[...] = jnp.zeros_like(c_out_ref)

    states[0] = start_ref[...]

    def advance(i, state):
        for j in range(SUB):
            decay = jnp.exp(step_ref[i, j : j + 1, :] * rate)
            state = decay * state + drive_ref[i, j : j + 1, :] * wide(b_ref[i, j], width)
            states[i * SUB + j + 1] = state
        return state

    lax.fori_loop(0, groups, advance, start_ref[...])

    def retreat(k, carry):
        flow, alog_sum = carry
        i = groups - 1 - k
        for j in reversed(range(SUB)):
            at = i * SUB + j
            step_now = step_ref[i, j : j + 1, :]
            grad_now = grad_ref[i, j : j + 1, :]
            decay = jnp.exp(step_now * rate)
            adjoint = wide(c_ref[i, j], width) * grad_now + flow
            flow = decay * adjoint
            held = flow * states[at]
            alog_sum = alog_sum + step_now * held
            into_drive = jnp.sum(adjoint * wide(b_ref[i, j], width), axis=0, keepdims=True)
            step_out_ref[i, j : j + 1, :] = (
                jnp.sum(rate * held, axis=0, keepdims=True)
                + conv_ref[i, j : j + 1, :] * into_drive
            )
            conv_out_ref[i, j : j + 1, :] = step_now * into_drive
            b_out_ref[i, j] += folded(adjoint * drive_ref[i, j : j + 1, :])
            c_out_ref[i, j] += folded(grad_now * states[at + 1])
        return (flow, alog_sum)

    _, alog_sum = lax.fori_loop(0, groups, retreat, (arriving_ref[...], jnp.zeros_like(rate)))
    alog_ref[...] = alog_sum * rate


def sweeps(length, channels, states):
    block = min(512, channels)
    groups = length // SUB
    rows = pl.BlockSpec((groups, SUB, block), lambda k: (0, 0, k))
    spread = pl.BlockSpec((groups, SUB, states, LANES), lambda k: (0, 0, 0, 0))
    column = pl.BlockSpec((states, block), lambda k: (0, k))
    grid = (channels // block,)
    f32 = jnp.float32
    row_shape = jax.ShapeDtypeStruct((groups, SUB, channels), f32)
    spread_shape = jax.ShapeDtypeStruct((groups, SUB, states, LANES), f32)
    column_shape = jax.ShapeDtypeStruct((states, channels), f32)
    totals = pl.pallas_call(
        totals_kernel,
        grid=grid,
        in_specs=[rows, rows, rows, spread, spread, column],
        out_specs=pl.BlockSpec((3, states, block), lambda k: (0, 0, k)),
        out_shape=jax.ShapeDtypeStruct((3, states, channels), jnp.bfloat16),
        name="totals",
    )
    forward = pl.pallas_call(
        forward_kernel,
        grid=grid,
        in_specs=[rows, rows, spread, spread, column, column],
        out_specs=rows,
        out_shape=row_shape,
        name="forward",
    )
    backward = pl.pallas_call(
        backward_kernel,
        grid=grid,
        in_specs=[rows, rows, rows, rows, spread, spread, column, column, column],
        out_specs=[rows, rows, spread, spread, column],
        out_shape=[row_shape, row_shape, spread_shape, spread_shape, column_shape],
        scratch_shapes=[pltpu.VMEM((length + 1, states, block), f32)],
        name="backward",
    )
    return totals, forward, backward


MESH = pl.DeviceIdType.MESH
GROUP = 16


def places():
    s, z = lax.axis_index("seq"), lax.axis_index("expert")
    core = lax.rem(s, 2)
    sib = s + 1 - 2 * core
    across_x = s + 2 - 4 * lax.rem(lax.div(s, 2), 2)
    across_y = s + 4 - 8 * lax.div(s, 4)
    return s, z, core, sib, across_x, across_y


def transposed(a, b):
    return lax.dot_general(a, b, (((1,), (1,)), ((), ())), preferred_element_type=jnp.float32)


def layer_kernel(
    x_ref,
    z_ref,
    dt_ref,
    bc_ref,
    alog_ref,
    conv_ref,
    bias_ref,
    gain_ref,
    dtb_ref,
    resid_ref,
    ids_ref,
    weight_ref,
    ow_hbm,
    gm_hbm,
    wg_hbm,
    wu_hbm,
    wd_hbm,
    out_ref,
    gx_ref,
    gz_ref,
    gdt_ref,
    alog_out,
    taps_out,
    chan_out,
    bc_out,
    gx_buf,
    gz_buf,
    gdt_buf,
    rows_all,
    wgu,
    wd,
    ow,
    gm,
    hidden,
    own_h,
    zrecv,
    zfin,
    part,
    psib,
    acc,
    rx,
    ry,
    rdx,
    rdy,
    fin,
    p_buf,
    sums_own,
    sums_recv,
    sums_acc,
    bc_own,
    bc_recv,
    decays,
    states,
    b_wide,
    c_wide,
    b_block,
    c_block,
    step_buf,
    drive_buf,
    conv_buf,
    grad_buf,
    dsilu_buf,
    dtsig_buf,
    zgate_buf,
    zfac_buf,
    into_buf,
    qsum_buf,
    xpad,
    gpad,
    xhalo,
    ghalo,
    gated,
    adj,
    quo,
    gb_acc,
    gc_acc,
    tot,
    tsib,
    tpair,
    trecv,
    rate_buf,
    start_buf,
    arrive_buf,
    w_sem,
    sems,
):
    s, z, core, sib, ax, ay = places()
    diag = ax + ay - s
    f32, bf16 = jnp.float32, jnp.bfloat16
    ways, seqs = 4, 8
    rows = resid_ref.shape[0]
    length, channels = x_ref.shape
    width = resid_ref.shape[1]
    half = width // 2
    scan = channels // 2
    groups = length // GROUP
    nst = alog_ref.shape[0]
    flat = GROUP * nst
    tiles = wgu.shape[1] // 256
    after = lax.rem(s + 1, seqs)
    ahead = lax.rem(s + seqs - 1, seqs)
    count = [0]
    everything = []

    def to(src, dst, seq, exp):
        index = count[0]
        count[0] += 1
        copy = pltpu.make_async_remote_copy(
            src_ref=src,
            dst_ref=dst,
            send_sem=sems.at[0, index],
            recv_sem=sems.at[1, index],
            device_id=(seq, exp),
            device_id_type=MESH,
        )
        everything.append(copy)
        return copy

    first = [
        pltpu.make_async_copy(ow_hbm, ow, w_sem.at[0]),
        pltpu.make_async_copy(gm_hbm, gm, w_sem.at[1]),
    ]
    for load in first:
        load.start()
    loads = []
    for t in range(tiles):
        for k, w_hbm in enumerate((wg_hbm, wu_hbm)):
            loads.append(
                pltpu.make_async_copy(
                    w_hbm.at[0, :, pl.ds(t * 128, 128)],
                    wgu.at[:, pl.ds(t * 256 + k * 128, 128)],
                    w_sem.at[2 + 2 * t + k],
                )
            )
    loads.append(pltpu.make_async_copy(wd_hbm.at[0], wd, w_sem.at[2 + 2 * tiles]))

    zs = [lax.rem(z + d, ways) for d in range(ways)]
    zb = [lax.rem(z + ways - d, ways) for d in range(ways)]

    barrier = pltpu.get_barrier_semaphore()
    partners = [(sib, z), (ax, z), (ay, z), (diag, z), (after, z), (ahead, z)]
    partners += [(s, zs[1]), (s, zs[2]), (s, zs[3])]
    for seq, exp in partners:
        pl.semaphore_signal(barrier, inc=1, device_id=(seq, exp), device_id_type=MESH)
    pl.semaphore_wait(barrier, len(partners))

    halo = to(x_ref.at[pl.ds(length - GROUP, GROUP), :], xhalo, after, z)
    halo.start()

    for k, spread in enumerate((b_wide, c_wide)):
        value = bc_ref[k]
        for t in range(length):
            spread[t] = jnp.broadcast_to(value[:, t : t + 1], (nst, LANES))
    lane = lax.broadcasted_iota(jnp.int32, (length, flat), 1)
    row = lax.broadcasted_iota(jnp.int32, (length, flat), 0)
    same_token = lax.div(lane, nst) == lax.rem(row, GROUP)
    lane_r = lax.broadcasted_iota(jnp.int32, (nst, flat), 1)
    row_r = lax.broadcasted_iota(jnp.int32, (nst, flat), 0)
    unit = (lax.rem(lane_r, nst) == row_r).astype(f32)
    repeat = unit.astype(bf16)
    for k, block_ref in enumerate((b_block, c_block)):
        by_token = jnp.transpose(bc_ref[k]).astype(bf16)
        laid = jnp.dot(by_token, repeat, preferred_element_type=f32)
        block_ref[...] = jnp.where(same_token, laid, 0.0).astype(bf16)
    diagonal = same_token[:GROUP].astype(f32)
    ones_block = diagonal.astype(bf16)
    rate_buf[...] = -jnp.exp(alog_ref[...])

    for load in first:
        load.wait()

    def mix_tile(t, _):
        at = pl.ds(pl.multiple_of(t * 256, 256), 256)
        zfac_buf[:, :, at] = transposed(gm[...], ow[at, :]).reshape(groups, GROUP, 256)
        return 0

    lax.fori_loop(0, channels // 256, mix_tile, 0, unroll=True)
    for load in loads:
        load.start()
    xpad[8 : 8 + length, :] = x_ref[...].astype(f32)
    halo.wait_recv()
    xpad[0:8, :] = jnp.where(s > 0, xhalo[...].astype(f32)[GROUP - 8 :], 0.0)

    def prepare(t, _):
        at = pl.ds(pl.multiple_of(t * LANES, LANES), LANES)

        def put(ref, value):
            ref[:, :, at] = value.reshape(groups, GROUP, LANES)

        pre = bias_ref[:, at] + conv_ref[0:1, at] * xpad[5 : 5 + length, at]
        for tap in range(1, KW):
            pre = pre + conv_ref[tap : tap + 1, at] * xpad[5 + tap : 5 + tap + length, at]
        conv_sig = jax.nn.sigmoid(pre)
        conv_out = pre * conv_sig
        put(conv_buf, conv_out)
        put(dsilu_buf, conv_sig * (1.0 + pre * (1.0 - conv_sig)))
        raw = dt_ref[:, at] + dtb_ref[:, at]
        step = jnp.maximum(raw, 0.0) + jnp.log1p(jnp.exp(-jnp.abs(raw)))
        put(step_buf, step)
        put(drive_buf, step * conv_out)
        put(dtsig_buf, jax.nn.sigmoid(raw))
        z_val = z_ref[:, at].astype(f32)
        z_sig = jax.nn.sigmoid(z_val)
        mixed = zfac_buf[:, :, at].reshape(length, LANES)
        gate = z_val * z_sig
        put(zgate_buf, gate)
        put(grad_buf, mixed * gate)
        put(zfac_buf, mixed * z_sig * (1.0 + z_val * (1.0 - z_sig)))
        return 0

    lax.fori_loop(0, channels // LANES, prepare, 0)

    def lanes(k):
        return pl.ds(k * scan, scan)

    def totals(k, low, high, carry):
        at = lanes(k)
        rate = rate_buf[:, at]

        def advance(i, carry):
            state, passed, leaving = carry
            for j in range(GROUP):
                decay = jnp.exp(step_buf[i, j : j + 1, at] * rate)
                decays[i * GROUP + j, :, at] = decay
                state = decay * state + drive_buf[i, j : j + 1, at] * wide(
                    b_wide[i * GROUP + j], scan
                )
                passed = passed * decay
                leaving = leaving + passed * (
                    grad_buf[i, j : j + 1, at] * wide(c_wide[i * GROUP + j], scan)
                )
            return (state, passed, leaving)

        return lax.fori_loop(low, high, advance, carry)

    zero = jnp.zeros((nst, scan), f32)
    nothing = (zero, jnp.ones_like(zero), zero)

    def keep(k, carry):
        for m in range(3):
            tot[k, m] = carry[m].astype(bf16)

    beside = [to(tot.at[k], tsib.at[k], sib, z) for k in range(2)]
    xbit, ybit = lax.rem(lax.div(s, 2), 2), lax.div(s, 4)
    beyond = []
    for k in range(2):
        for m, (seq, bit) in enumerate(((ax, xbit), (ay, ybit), (diag, ybit))):
            at = pl.ds(bit, 2)
            beyond.append(to(tpair.at[k, at], trecv.at[k, m, at], seq, z))

    def join(k):
        beside[k].wait_recv()
        own = [tot[k, m].astype(f32) for m in range(3)]
        their = [tsib[k, m].astype(f32) for m in range(3)]
        one = [jnp.where(core == 0, a, b) for a, b in zip(own, their)]
        two = [jnp.where(core == 0, b, a) for a, b in zip(own, their)]
        tpair[k, 0] = (two[1] * one[0] + two[0]).astype(bf16)
        tpair[k, 1] = (one[1] * two[1]).astype(bf16)
        tpair[k, 2] = (one[2] + one[1] * two[2]).astype(bf16)
        for copy in beyond[3 * k : 3 * k + 3]:
            copy.start()

    def enter(k):
        for copy in beyond[3 * k : 3 * k + 3]:
            copy.wait_recv()
        chip = lax.div(s, 2)
        start, arriving = zero, zero

        def other_chip(c):
            relation = (c % 2 + xbit - 2 * (c % 2) * xbit) + 2 * (c // 2 + ybit - 2 * (c // 2) * ybit)
            return trecv.at[k, jnp.maximum(relation - 1, 0)]

        for c in range(4):
            at = other_chip(c)
            start = jnp.where(c < chip, at[1].astype(f32) * start + at[0].astype(f32), start)
            at = other_chip(3 - c)
            arriving = jnp.where(
                3 - c > chip, at[1].astype(f32) * arriving + at[2].astype(f32), arriving
            )
        passed = tsib[k, 1].astype(f32)
        start = jnp.where(core == 1, passed * start + tsib[k, 0].astype(f32), start)
        arriving = jnp.where(core == 0, passed * arriving + tsib[k, 2].astype(f32), arriving)
        start_buf[:, lanes(k)] = start
        arrive_buf[:, lanes(k)] = arriving

    keep(0, totals(0, 0, groups, nothing))
    beside[0].start()
    middle = totals(1, 0, groups // 2, nothing)
    join(0)
    keep(1, totals(1, groups // 2, groups, middle))
    beside[1].start()
    join(1)

    def state_rows(at, number):
        return pl.ds(pl.multiple_of(at * nst, nst), number * nst)

    def forward(k):
        at = lanes(k)
        states[0:nst, at] = start_buf[:, at].astype(bf16)

        def advance(i, state):
            for j in range(GROUP):
                t = i * GROUP + j
                state = decays[t, :, at] * state + drive_buf[i, j : j + 1, at] * wide(
                    b_wide[t], scan
                )
                states[state_rows(t + 1, 1), at] = state.astype(bf16)
            here = pl.ds(pl.multiple_of(i * GROUP, GROUP), GROUP)
            y_val = jnp.dot(
                c_block[here, :],
                states[state_rows(i * GROUP + 1, GROUP), at],
                preferred_element_type=f32,
            )
            y_val = y_val + gain_ref[:, at] * conv_buf[i, :, at]
            gz_buf[here, at] = zfac_buf[i, :, at] * y_val
            gated[here, at] = (zgate_buf[i, :, at] * y_val).astype(bf16)
            return state

        lax.fori_loop(0, groups, advance, start_buf[:, at])

    for k in range(2):
        enter(k)
        forward(k)

    written = [
        pltpu.make_async_copy(gz_buf, gz_ref, w_sem.at[3 + 2 * tiles]),
        pltpu.make_async_copy(gdt_buf, gdt_ref, w_sem.at[4 + 2 * tiles]),
        pltpu.make_async_copy(gx_buf, gx_ref, w_sem.at[5 + 2 * tiles]),
    ]
    written[0].start()

    waves = 2
    piece = rows // waves
    pack = ways * piece

    def block(seq, exp, w):
        at = (w * seqs + seq) * pack + exp * piece
        return pl.ds(pl.multiple_of(at, piece), piece)

    def within(exp, w):
        return pl.ds(pl.multiple_of(exp * rows + w * piece, piece), piece)

    def project(t, _):
        at = pl.ds(pl.multiple_of(t * 256, 256), 256)
        p_buf[:, at] = jnp.dot(gated[...], ow[:, at], preferred_element_type=f32).astype(bf16)
        return 0

    lax.fori_loop(0, width // 256, project, 0, unroll=True)

    z_out = [
        [to(p_buf.at[within(zs[d], w)], zrecv.at[w, d - 1], s, zs[d]) for d in (1, 2, 3)]
        for w in range(waves)
    ]
    for copy in z_out[0]:
        copy.start()

    gb_acc[...] = jnp.zeros_like(gb_acc)
    gc_acc[...] = jnp.zeros_like(gc_acc)

    def backward(k):
        at = lanes(k)

        def retreat(n, carry):
            flow, alog_sum = carry
            i = groups - 1 - n
            for j in reversed(range(GROUP)):
                t = i * GROUP + j
                adjoint = wide(c_wide[t], scan) * grad_buf[i, j : j + 1, at] + flow
                adj[j * nst : (j + 1) * nst, :] = adjoint.astype(bf16)
                flow = decays[t, :, at] * adjoint
                share = rate_buf[:, at] * (flow * states[state_rows(t, 1), at].astype(f32))
                alog_sum = alog_sum + step_buf[i, j : j + 1, at] * share
                quo[j * nst : (j + 1) * nst, :] = share.astype(bf16)
            here = pl.ds(pl.multiple_of(i * GROUP, GROUP), GROUP)
            into_buf[i, :, at] = jnp.dot(b_block[here, :], adj[...], preferred_element_type=f32)
            qsum_buf[i, :, at] = jnp.dot(ones_block, quo[...], preferred_element_type=f32)
            gb_acc[i] += transposed(drive_buf[i, :, at].astype(bf16), adj[...])
            gc_acc[i] += transposed(
                grad_buf[i, :, at].astype(bf16), states[state_rows(i * GROUP + 1, GROUP), at]
            )
            return (flow, alog_sum)

        _, alog_sum = lax.fori_loop(0, groups, retreat, (arrive_buf[:, at], zero))
        sums_own[0:nst, at] = alog_sum

    gather, to_x, to_y, to_b, forward = [], [], [], [], []
    for w in range(waves):
        here = rows_all.at[block(s, z, w)]
        gather.append([to(here, here, s, zs[d]) for d in (1, 2, 3)])
        blocks = [rows_all.at[block(s, zb[d], w)] for d in range(ways)]
        to_x.append([to(at, at, ax, z) for at in blocks])
        to_y.append([to(at, at, ay, z) for at in blocks])
        to_b.append([to(at, at, sib, z) for at in blocks])
        passing = []
        for d in range(ways):
            origin, target = (ay, ax) if d < 2 else (ax, ay)
            at = rows_all.at[block(origin, zb[d], w)]
            passing.append(to(at, at, target, z))
        forward.append(passing)

    def mixed_rows(w):
        for copy in z_out[w]:
            copy.wait_recv()
        own = pl.ds(w * piece, piece)
        total = resid_ref[own, :].astype(f32) + p_buf[within(z, w), :].astype(f32)
        for d in range(3):
            total = total + zrecv[w, d].astype(f32)
        own_h[own, :] = total.astype(bf16)
        rows_all[block(s, z, w), :] = total.astype(bf16)
        for copy in gather[w] + [to_x[w][0], to_y[w][0], to_b[w][0]]:
            copy.start()

    def spread_rows(w):
        for d in (1, 2, 3):
            gather[w][d - 1].wait_recv()
            to_x[w][d].start()
            to_y[w][d].start()
            to_b[w][d].start()

    backward(0)
    for copy in z_out[1]:
        copy.start()
    mixed_rows(0)
    backward(1)
    for k, held in enumerate((gb_acc, gc_acc)):
        kept = jnp.where(same_token, held[...].reshape(length, flat), 0.0)
        bc_own[k] = lax.dot_general(
            unit,
            kept,
            (((1,), (1,)), ((), ())),
            precision=lax.Precision.HIGHEST,
            preferred_element_type=f32,
        )
    bc_copies = [to(bc_own, bc_recv.at[d - 1], s, zs[d]) for d in (1, 2, 3)]
    for copy in bc_copies:
        copy.start()

    def finish(t, _):
        at = pl.ds(pl.multiple_of(t * LANES, LANES), LANES)

        def get(ref):
            return ref[:, :, at].reshape(length, LANES)

        def total(value):
            return jnp.sum(value, axis=0, keepdims=True)

        into, conv_out, grad_y = get(into_buf), get(conv_buf), get(grad_buf)
        grad_dt = (get(qsum_buf) + conv_out * into) * get(dtsig_buf)
        gdt_buf[:, at] = grad_dt
        grad_pre = (gain_ref[:, at] * grad_y + get(step_buf) * into) * get(dsilu_buf)
        gpad[0:length, at] = grad_pre
        for tap in range(KW):
            sums_own[nst + tap : nst + tap + 1, at] = total(
                grad_pre * xpad[5 + tap : 5 + tap + length, at]
            )
        sums_own[nst + KW : nst + KW + 1, at] = total(grad_pre)
        sums_own[nst + KW + 1 : nst + KW + 2, at] = total(grad_y * conv_out)
        sums_own[nst + KW + 2 : nst + KW + 3, at] = total(grad_dt)
        return 0

    lax.fori_loop(0, channels // LANES, finish, 0)
    written[1].start()
    sums_own[nst + KW + 3 :, :] = jnp.zeros_like(sums_own[nst + KW + 3 :, :])
    rim = to(gpad.at[pl.ds(0, 8)], ghalo, ahead, z)
    rim.start()
    sums_copies = [
        to(sums_own, sums_recv.at[0], sib, z),
        to(sums_acc.at[0], sums_recv.at[1], ax, z),
        to(sums_acc.at[1], sums_recv.at[2], ay, z),
    ]
    sums_copies[0].start()
    mixed_rows(1)
    sums_copies[0].wait_recv()
    sums_acc[0] = sums_own[...] + sums_recv[0]
    sums_copies[1].start()
    spread_rows(0)
    rim.wait_recv()
    gpad[length : length + 8, :] = jnp.where(s < seqs - 1, ghalo[...], 0.0)

    def spread_back(t, _):
        at = pl.ds(pl.multiple_of(t * LANES, LANES), LANES)
        grad_x = conv_ref[KW - 1 : KW, at] * gpad[0:length, at]
        for tap in range(KW - 1):
            away = KW - 1 - tap
            grad_x = grad_x + conv_ref[tap : tap + 1, at] * gpad[away : away + length, at]
        gx_buf[:, at] = grad_x
        return 0

    lax.fori_loop(0, channels // LANES, spread_back, 0)
    written[2].start()
    to_y[0][0].wait_recv()
    forward[0][0].start()

    sums_copies[1].wait_recv()
    sums_acc[1] = sums_acc[0] + sums_recv[1]
    sums_copies[2].start()

    for copy in bc_copies:
        copy.wait_recv()
    bc_out[...] = (bc_own[...] + bc_recv[0]) + (bc_recv[1] + bc_recv[2])

    def up(w, seq):
        first_row = (w * seqs + 4 * lax.div(seq, 4)) * pack
        at = pl.ds(pl.multiple_of(first_row, 4 * pack), 4 * pack)

        def tile(t, _):
            both = jnp.dot(
                rows_all[at, :],
                wgu[:, pl.ds(pl.multiple_of(t * 256, 256), 256)],
                preferred_element_type=f32,
            )
            gate, upper = both[:, :128], both[:, 128:]
            value = gate * jax.nn.sigmoid(gate) * upper
            hidden[:, pl.ds(pl.multiple_of(t * 128, 128), 128)] = value.astype(bf16)
            return 0

        lax.fori_loop(0, tiles, tile, 0, unroll=True)

    quarter = width // 4
    order = (0, 2, 1, 3)

    def cols(h):
        return pl.ds(h * quarter, quarter)

    def small(h):
        return pl.ds((h % 2) * quarter, quarter)

    def part_rows(r, of_core):
        side = xbit if r % 2 == 0 else 1 - xbit
        return pl.ds(pl.multiple_of((2 * side + of_core) * pack, pack), pack)

    pair = {}

    def down(w, r0, h):
        g = 2 * w + r0 // 2
        part[g, :, cols(h)] = jnp.dot(
            hidden[...], wd[:, cols(h)], preferred_element_type=f32
        ).astype(bf16)
        for r in (r0, r0 + 1):
            copy = to(
                part.at[g, part_rows(r, 1 - core), cols(h)], psib.at[w, r, :, cols(h)], sib, z
            )
            copy.start()
            pair[w, r, h] = copy

    def paired(w, r, h):
        pair[w, r, h].wait_recv()
        acc[w, r, :, cols(h)] = (
            part[2 * w + r // 2, part_rows(r, core), cols(h)].astype(f32)
            + psib[w, r, :, cols(h)].astype(f32)
        ).astype(bf16)

    def pack_of(seq, w):
        at = (w * seqs + seq) * pack
        return rows_all.at[pl.ds(pl.multiple_of(at, pack), pack)]

    share_out = [[to(pack_of(o, w), pack_of(o, w), sib, z) for o in (ax, ay, diag)] for w in range(waves)]
    send = {}

    def reduce_out(name, src, dst, seq):
        copy = to(src, dst, seq, z)
        copy.start()
        send[name] = copy

    def to_across_x(w, h):
        reduce_out(("x", w, h), acc.at[w, 1, :, cols(h)], rx.at[w, :, cols(h)], ax)

    def to_across_y(w, h):
        reduce_out(("y", w, h), acc.at[w, 2, :, cols(h)], ry.at[w, :, cols(h)], ay)

    def near(w):
        to_x[w][0].wait_recv()
        to_x[w][1].wait_recv()
        to_y[w][1].wait_recv()
        forward[w][1].start()
        to_x[w][2].wait_recv()
        forward[w][2].start()
        to_x[w][3].wait_recv()
        forward[w][3].start()
        share_out[w][0].start()
        to_y[w][2].wait_recv()
        to_y[w][3].wait_recv()
        share_out[w][1].start()

    def near_ready(w):
        for copy in to_b[w]:
            copy.wait_recv()
        share_out[w][0].wait_recv()

    def far(w):
        for copy in forward[w]:
            copy.wait_recv()
        share_out[w][2].start()

    def far_ready(w):
        share_out[w][1].wait_recv()
        share_out[w][2].wait_recv()

    def diagonal_out(w, h):
        paired(w, 3, h)
        if h < 2:
            reduce_out(("d", w, h), acc.at[w, 3, :, cols(h)], rdx.at[w, :, small(h)], ax)
        else:
            reduce_out(("d", w, h), acc.at[w, 3, :, cols(h)], rdy.at[w, :, small(h)], ay)

    def direct_x(w):
        for h in (0, 1):
            paired(w, 1, h)
            to_across_x(w, h)
        for h in (2, 3):
            paired(w, 1, h)

    def direct_y(w):
        for h in (2, 3):
            paired(w, 2, h)
            to_across_y(w, h)
        for h in (0, 1):
            paired(w, 2, h)
        for h in range(4):
            paired(w, 0, h)

    def joined(w):
        for h in order:
            send["d", w, h].wait_recv()
            r, got = (2, rdx) if h < 2 else (1, rdy)
            acc[w, r, :, cols(h)] = (
                acc[w, r, :, cols(h)].astype(f32) + got[w, :, small(h)].astype(f32)
            ).astype(bf16)
            if h < 2:
                to_across_y(w, h)
            else:
                to_across_x(w, h)

    back = {}

    def reduced(w, h):
        send["x", w, h].wait_recv()
        send["y", w, h].wait_recv()
        total = (
            acc[w, 0, :, cols(h)].astype(f32)
            + rx[w, :, cols(h)].astype(f32)
            + ry[w, :, cols(h)].astype(f32)
        ).astype(bf16)
        fin[w, :, cols(h)] = total
        for d in (1, 2, 3):
            at = pl.ds(pl.multiple_of(zs[d] * piece, piece), piece)
            copy = to(fin.at[w, at, cols(h)], zfin.at[w, d - 1, :, cols(h)], s, zs[d])
            copy.start()
            back[w, h, d] = copy

    eye = lax.broadcasted_iota(jnp.int32, (rows, rows), 0) == lax.broadcasted_iota(
        jnp.int32, (rows, rows), 1
    )

    def column(row):
        return jnp.sum(jnp.where(eye, row, 0.0), axis=1, keepdims=True)

    shares = []
    for d in range(ways):
        mine = [
            jnp.where(ids_ref[k : k + 1, :] == zb[d], weight_ref[k : k + 1, :], 0.0) for k in range(2)
        ]
        shares.append(column(mine[0] + mine[1]))

    def result(w, h):
        own = pl.ds(w * piece, piece)
        at = pl.ds(pl.multiple_of(z * piece, piece), piece)
        total = own_h[own, cols(h)].astype(f32)
        total = total + shares[0][w * piece : (w + 1) * piece] * fin[w, at, cols(h)].astype(f32)
        for d in (1, 2, 3):
            back[w, h, d].wait_recv()
            total = total + shares[d][w * piece : (w + 1) * piece] * zfin[
                w, d - 1, :, cols(h)
            ].astype(f32)
        out_ref[own, cols(h)] = total.astype(bf16)

    near(0)
    spread_rows(1)
    near_ready(0)
    for load in loads:
        load.wait()
    to_y[1][0].wait_recv()
    forward[1][0].start()
    up(0, s)
    far(0)
    for h in range(4):
        down(0, 0, h)
    far_ready(0)
    up(0, ay)
    for h in order:
        down(0, 2, h)
    near(1)
    direct_x(0)
    for h in order:
        diagonal_out(0, h)
    direct_y(0)
    near_ready(1)
    up(1, s)
    far(1)
    for h in range(4):
        down(1, 0, h)
    joined(0)
    direct_x(1)
    far_ready(1)
    up(1, ay)
    for h in order:
        reduced(0, h)
    down(1, 2, 0)
    down(1, 2, 2)
    diagonal_out(1, 0)
    down(1, 2, 1)
    diagonal_out(1, 2)
    down(1, 2, 3)
    diagonal_out(1, 1)
    diagonal_out(1, 3)
    direct_y(1)

    sums_copies[2].wait_recv()
    summed = sums_acc[1] + sums_recv[2]
    alog_out[...] = summed[:nst]
    taps_out[...] = summed[nst : nst + KW]
    chan_out[...] = summed[nst + KW : nst + KW + 3]

    for h in order:
        result(0, h)
    joined(1)
    for h in order:
        reduced(1, h)
    for h in order:
        result(1, h)
    for copy in written:
        copy.wait()
    for copy in everything:
        copy.wait_send()


def deliver_kernel(number, *refs):
    given, results, stops, sem = (
        refs[:number],
        refs[number : 2 * number],
        refs[2 * number : 3 * number],
        refs[3 * number],
    )
    fetch = [pltpu.make_async_copy(given[k], stops[k], sem.at[0, k]) for k in range(number)]
    store = [pltpu.make_async_copy(stops[k], results[k], sem.at[1, k]) for k in range(number)]
    for copy in fetch:
        copy.start()
    for k in range(number):
        fetch[k].wait()
        store[k].start()
    for copy in store:
        copy.wait()


def deliver(arrays):
    number = len(arrays)
    anywhere = pl.BlockSpec(memory_space=pl.ANY)
    return pl.pallas_call(
        functools.partial(deliver_kernel, number),
        out_shape=[jax.ShapeDtypeStruct(a.shape, a.dtype) for a in arrays],
        in_specs=[anywhere] * number,
        out_specs=[anywhere] * number,
        scratch_shapes=[pltpu.VMEM(a.shape, a.dtype) for a in arrays]
        + [pltpu.SemaphoreType.DMA((2, number))],
        name="deliver",
    )(*arrays)


def layer(
    x_in,
    z_in,
    dt_raw,
    bc_in,
    a_log,
    taps,
    bias,
    gain,
    dt_bias,
    resid,
    route_ids,
    route_weight,
    out_weight,
    grad_mix,
    w_gate,
    w_up,
    w_down,
):
    rows, width = resid.shape
    length, channels = x_in.shape
    states = a_log.shape[0]
    units = w_gate.shape[2]
    tiles = units // 128
    seqs = lax.axis_size("seq")
    half, scan, groups = width // 2, channels // 2, length // GROUP
    bf16, f32 = jnp.bfloat16, jnp.float32
    vmem = pl.BlockSpec(memory_space=pltpu.VMEM)
    hbm = pl.BlockSpec(memory_space=pl.ANY)
    sem = pltpu.SemaphoreType.DMA
    flat = GROUP * states

    def held(*shape, kind=f32):
        return pltpu.VMEM(shape, kind)

    def rows_of():
        return held(groups, GROUP, channels)

    summed = (states + 8, channels)
    grads = (2, states, length)
    return pl.pallas_call(
        layer_kernel,
        out_shape=[
            jax.ShapeDtypeStruct((rows, width), bf16),
            jax.ShapeDtypeStruct((length, channels), f32),
            jax.ShapeDtypeStruct((length, channels), f32),
            jax.ShapeDtypeStruct((length, channels), f32),
            jax.ShapeDtypeStruct((states, channels), f32),
            jax.ShapeDtypeStruct((KW, channels), f32),
            jax.ShapeDtypeStruct((3, channels), f32),
            jax.ShapeDtypeStruct(grads, f32),
        ],
        in_specs=[vmem] * 12 + [hbm] * 5,
        out_specs=[vmem] + [hbm] * 3 + [vmem] * 4,
        scratch_shapes=[
            held(length, channels),
            held(length, channels),
            held(length, channels),
            held(seqs * length, width, kind=bf16),
            held(width, 2 * units, kind=bf16),
            held(units, width, kind=bf16),
            held(channels, width, kind=bf16),
            held(length, width, kind=bf16),
            held(2 * length, units, kind=bf16),
            held(rows, width, kind=bf16),
            held(2, 3, rows // 2, width, kind=bf16),
            held(2, 3, rows // 2, width, kind=bf16),
            held(4, 2 * length, width, kind=bf16),
            held(2, 4, length // 2, width, kind=bf16),
            held(2, 4, length // 2, width, kind=bf16),
            held(2, length // 2, width, kind=bf16),
            held(2, length // 2, width, kind=bf16),
            held(2, length // 2, half, kind=bf16),
            held(2, length // 2, half, kind=bf16),
            held(2, length // 2, width, kind=bf16),
            held(length, width, kind=bf16),
            held(*summed),
            held(3, *summed),
            held(2, *summed),
            held(*grads),
            held(3, *grads),
            held(length, states, channels),
            held((length + 1) * states, channels, kind=bf16),
            held(length, states, LANES),
            held(length, states, LANES),
            held(length, flat, kind=bf16),
            held(length, flat, kind=bf16),
        ]
        + [rows_of() for _ in range(10)]
        + [
            held(length + 8, channels),
            held(length + 8, channels),
            held(GROUP, channels, kind=bf16),
            held(8, channels),
            held(length, channels, kind=bf16),
            held(flat, scan, kind=bf16),
            held(flat, scan, kind=bf16),
            held(groups, GROUP, flat),
            held(groups, GROUP, flat),
            held(2, 3, states, scan, kind=bf16),
            held(2, 3, states, scan, kind=bf16),
            held(2, 3, states, scan, kind=bf16),
            held(2, 3, 3, states, scan, kind=bf16),
            held(states, channels),
            held(states, channels),
            held(states, channels),
            sem((2 * tiles + 6,)),
            sem((2, 192)),
        ],
        compiler_params=pltpu.CompilerParams(
            collective_id=0, has_side_effects=True, vmem_limit_bytes=60 << 20
        ),
        cost_estimate=pl.CostEstimate(
            flops=6 * seqs * length * width * units + 4 * length * width * channels,
            bytes_accessed=6 * width * units,
            transcendentals=seqs * length * units + length * channels * states,
        ),
        name="layer",
    )(
        x_in,
        z_in,
        dt_raw,
        bc_in,
        a_log,
        taps,
        bias.reshape(1, channels),
        gain.reshape(1, channels),
        dt_bias.reshape(1, channels),
        resid,
        route_ids.T,
        route_weight.T,
        out_weight,
        grad_mix,
        w_gate,
        w_up,
        w_down,
    )


def entering(everything):
    peers, here = everything.shape[0], lax.axis_index("seq")
    values = everything.astype(jnp.float32)
    start = jnp.zeros_like(values[0, 0])
    arriving = jnp.zeros_like(start)
    for k in range(peers):
        start = jnp.where(k < here, values[k, 0] * start + values[k, 1], start)
        back = peers - 1 - k
        arriving = jnp.where(back > here, values[back, 0] * arriving + values[back, 2], arriving)
    return start, arriving


def routed_experts(partial_value, resid, w_gate, w_up, w_down, route_ids, route_weight):
    rows = resid.shape[0]
    mixed = lax.psum(partial_value, "expert").astype(jnp.float32)
    own = lax.dynamic_slice_in_dim(mixed, lax.axis_index("expert") * rows, rows, 0)
    hidden_in = (resid.astype(jnp.float32) + own).astype(jnp.bfloat16)
    experts = lax.axis_size("expert")
    capacity = 4 * rows // experts
    flat_ids = route_ids.reshape(-1)
    order = jnp.arange(flat_ids.shape[0], dtype=jnp.int32)
    earlier = (flat_ids[:, None] == flat_ids[None, :]) & (order[None, :] < order[:, None])
    rank = jnp.sum(earlier.astype(jnp.int32), axis=1)
    slot = flat_ids * capacity + rank
    placing = (jnp.arange(experts * capacity, dtype=jnp.int32)[:, None] == slot[None, :]).astype(
        jnp.bfloat16
    )
    doubled = jnp.repeat(hidden_in, 2, axis=0)
    outgoing = jnp.dot(placing, doubled, preferred_element_type=jnp.float32).astype(jnp.bfloat16)
    incoming = lax.all_to_all(outgoing, "expert", split_axis=0, concat_axis=0, tiled=True)
    piece = lax.all_gather(incoming, "seq", axis=0, tiled=True)
    gate = jnp.dot(piece, w_gate[0], preferred_element_type=jnp.float32)
    upper = jnp.dot(piece, w_up[0], preferred_element_type=jnp.float32)
    hidden = (jax.nn.silu(gate) * upper).astype(jnp.bfloat16)
    expert_sum = lax.psum_scatter(
        jnp.dot(hidden, w_down[0], preferred_element_type=jnp.float32).astype(jnp.bfloat16),
        "seq",
        scatter_dimension=0,
        tiled=True,
    )
    returned = lax.all_to_all(expert_sum, "expert", split_axis=0, concat_axis=0, tiled=True)
    picked = lax.dot_general(
        placing, returned, (((0,), (0,)), ((), ())), preferred_element_type=jnp.float32
    )
    picked = picked.reshape(rows, 2, -1)
    moe = picked[:, 0] * route_weight[:, 0:1] + picked[:, 1] * route_weight[:, 1:2]
    return (hidden_in.astype(jnp.float32) + moe).astype(jnp.bfloat16)


def local(
    x_in,
    z_in,
    dt_raw,
    bc_in,
    a_log,
    conv_weight,
    conv_bias,
    skip_gain,
    dt_bias,
    out_weight,
    resid,
    w_gate,
    w_up,
    w_down,
    route_ids,
    route_weight,
    grad_mix,
):
    length, channels = x_in.shape
    states = a_log.shape[0]
    rim = KW - 1
    rows = resid.shape[0]
    experts = lax.axis_size("expert")
    if experts == 4 and lax.axis_size("seq") == 8:
        layer_out, grad_x, grad_z, grad_dt, grad_alog, grad_conv, grad_chan, grad_bc = deliver(
            layer(
                x_in,
                z_in,
                dt_raw,
                bc_in,
                a_log,
                conv_weight,
                conv_bias,
                skip_gain,
                dt_bias,
                resid,
                route_ids,
                route_weight,
                out_weight,
                grad_mix,
                w_gate,
                w_up,
                w_down,
            )
        )
        return (layer_out, grad_x, grad_z, grad_dt, grad_bc, grad_alog, grad_conv, grad_chan)
    x_val = x_in.astype(jnp.float32)
    z_val = z_in.astype(jnp.float32)
    before = shifted(x_in[length - rim :], "seq", 1)
    padded = jnp.concatenate([before.astype(jnp.float32), x_val], axis=0)
    pre = conv_bias[None, :] + conv_weight[0][None, :] * padded[0:length]
    for tap in range(1, KW):
        pre = pre + conv_weight[tap][None, :] * padded[tap : tap + length]
    conv_sig = jax.nn.sigmoid(pre)
    conv_out = pre * conv_sig
    step = jax.nn.softplus(dt_raw + dt_bias[None, :])
    rate = -jnp.exp(a_log)
    drive = step * conv_out
    z_sig = jax.nn.sigmoid(z_val)
    back_mix = lax.dot_general(
        grad_mix, out_weight, (((1,), (1,)), ((), ())), preferred_element_type=jnp.float32
    )
    grad_y = back_mix * z_val * z_sig

    def grouped(array):
        return array.reshape(length // SUB, SUB, channels)

    def flat(array):
        return array.reshape(length, channels)

    spread = jnp.broadcast_to(
        bc_in.transpose(0, 2, 1)[:, :, :, None], (2, length, states, LANES)
    ).reshape(2, length // SUB, SUB, states, LANES)
    b_wide, c_wide = spread[0], spread[1]
    totals, forward, backward = sweeps(length, channels, states)
    step_g, drive_g, grad_g, conv_g = (grouped(a) for a in (step, drive, grad_y, conv_out))
    own_totals = totals(step_g, drive_g, grad_g, b_wide, c_wide, rate)
    start, arriving = entering(lax.all_gather(own_totals, "seq"))
    y_val = flat(forward(step_g, drive_g, b_wide, c_wide, rate, start))
    y_val = y_val + skip_gain[None, :] * conv_out
    gated = (y_val * z_val * z_sig).astype(jnp.bfloat16)
    partial_value = jnp.dot(gated, out_weight, preferred_element_type=jnp.float32)
    grad_z = back_mix * y_val * z_sig * (1.0 + z_val * (1.0 - z_sig))
    grad_step, conv_part_grad, grad_b, grad_c, grad_alog_local = backward(
        step_g, drive_g, conv_g, grad_g, b_wide, c_wide, rate, start, arriving
    )
    grad_step, conv_part_grad = flat(grad_step), flat(conv_part_grad)
    grad_conv_out = skip_gain[None, :] * grad_y + conv_part_grad
    grad_skip = jnp.sum(grad_y * conv_out, axis=0)
    grad_dt = grad_step * jax.nn.sigmoid(dt_raw + dt_bias[None, :])
    grad_pre = grad_conv_out * (conv_sig * (1.0 + pre * (1.0 - conv_sig)))
    after = shifted(grad_pre[:rim], "seq", -1)
    grad_pad = jnp.concatenate([grad_pre, after], axis=0)
    grad_x = conv_weight[rim][None, :] * grad_pad[0:length]
    for tap in range(rim):
        grad_x = grad_x + conv_weight[tap][None, :] * grad_pad[rim - tap : rim - tap + length]
    grad_taps = jnp.stack(
        [jnp.sum(grad_pre * padded[tap : tap + length], axis=0) for tap in range(KW)]
    )
    channel_grads = jnp.stack([jnp.sum(grad_pre, axis=0), grad_skip, jnp.sum(grad_dt, axis=0)])
    own_sums = jnp.concatenate([grad_alog_local, grad_taps, channel_grads], axis=0)
    own_bc = jnp.stack([jnp.sum(grad_b, axis=-1), jnp.sum(grad_c, axis=-1)])
    own_bc = own_bc.reshape(2, length, states).transpose(0, 2, 1).reshape(2 * states, length)
    layer_out = routed_experts(
        partial_value.astype(jnp.bfloat16),
        resid,
        w_gate,
        w_up,
        w_down,
        route_ids,
        route_weight,
    )
    sums = lax.psum(own_sums, "seq")
    grad_bc = lax.psum(own_bc, "expert").reshape(2, states, length)
    grad_alog = sums[:states]
    grad_conv = sums[states : states + KW]
    grad_chan = sums[states + KW : states + KW + 3]
    return (layer_out, grad_x, grad_z, grad_dt, grad_bc, grad_alog, grad_conv, grad_chan)


def solution(mesh):
    in_specs = (
        P("seq", "expert"),
        P("seq", "expert"),
        P("seq", "expert"),
        P(None, None, "seq"),
        P(None, "expert"),
        P(None, "expert"),
        P("expert"),
        P("expert"),
        P("expert"),
        P("expert", None),
        P(("seq", "expert"), None),
        P("expert", None, "seq"),
        P("expert", None, "seq"),
        P("expert", "seq", None),
        P(("seq", "expert"), None),
        P(("seq", "expert"), None),
        P("seq", None),
    )
    out_specs = (
        P(("seq", "expert"), None),
        P("seq", "expert"),
        P("seq", "expert"),
        P("seq", "expert"),
        P(None, None, "seq"),
        P(None, "expert"),
        P(None, "expert"),
        P(None, "expert"),
    )
    return jax.shard_map(local, mesh=mesh, in_specs=in_specs, out_specs=out_specs, check_vma=False)
```

```python
import functools

import jax
import jax.numpy as jnp
from jax import lax
from jax.experimental import pallas as pl
from jax.experimental.pallas import tpu as pltpu
from jax.sharding import PartitionSpec as P

KW = 4
SUB = 8
LANES = 128


def shifted(x, axis, by):
    peers = lax.axis_size(axis)
    pairs = [(i, i + by) for i in range(peers) if 0 <= i + by < peers]
    return lax.ppermute(x, axis, pairs)


def wide(tile, width):
    return jnp.concatenate([tile] * (width // tile.shape[1]), axis=1)


def folded(value):
    total = value[:, :LANES]
    for at in range(LANES, value.shape[1], LANES):
        total = total + value[:, at : at + LANES]
    return total


def totals_kernel(step_ref, drive_ref, grad_ref, b_ref, c_ref, rate_ref, out_ref):
    rate = rate_ref[...]
    width = rate.shape[1]

    def advance(i, carry):
        state, passed, leaving = carry
        for j in range(SUB):
            decay = jnp.exp(step_ref[i, j : j + 1, :] * rate)
            state = decay * state + drive_ref[i, j : j + 1, :] * wide(b_ref[i, j], width)
            passed = passed * decay
            leaving = leaving + passed * (grad_ref[i, j : j + 1, :] * wide(c_ref[i, j], width))
        return (state, passed, leaving)

    zero = jnp.zeros_like(rate)
    state, passed, leaving = lax.fori_loop(
        0, step_ref.shape[0], advance, (zero, jnp.ones_like(rate), zero)
    )
    out_ref[0] = passed.astype(out_ref.dtype)
    out_ref[1] = state.astype(out_ref.dtype)
    out_ref[2] = leaving.astype(out_ref.dtype)


def forward_kernel(step_ref, drive_ref, b_ref, c_ref, rate_ref, start_ref, y_ref):
    rate = rate_ref[...]
    width = rate.shape[1]

    def advance(i, state):
        for j in range(SUB):
            decay = jnp.exp(step_ref[i, j : j + 1, :] * rate)
            state = decay * state + drive_ref[i, j : j + 1, :] * wide(b_ref[i, j], width)
            y_ref[i, j : j + 1, :] = jnp.sum(
                wide(c_ref[i, j], width) * state, axis=0, keepdims=True
            )
        return state

    lax.fori_loop(0, step_ref.shape[0], advance, start_ref[...])


def backward_kernel(
    step_ref,
    drive_ref,
    conv_ref,
    grad_ref,
    b_ref,
    c_ref,
    rate_ref,
    start_ref,
    arriving_ref,
    step_out_ref,
    conv_out_ref,
    b_out_ref,
    c_out_ref,
    alog_ref,
    states,
):
    rate = rate_ref[...]
    width = rate.shape[1]
    groups = step_ref.shape[0]

    @pl.when(pl.program_id(0) == 0)
    def _():
        b_out_ref[...] = jnp.zeros_like(b_out_ref)
        c_out_ref[...] = jnp.zeros_like(c_out_ref)

    states[0] = start_ref[...]

    def advance(i, state):
        for j in range(SUB):
            decay = jnp.exp(step_ref[i, j : j + 1, :] * rate)
            state = decay * state + drive_ref[i, j : j + 1, :] * wide(b_ref[i, j], width)
            states[i * SUB + j + 1] = state
        return state

    lax.fori_loop(0, groups, advance, start_ref[...])

    def retreat(k, carry):
        flow, alog_sum = carry
        i = groups - 1 - k
        for j in reversed(range(SUB)):
            at = i * SUB + j
            step_now = step_ref[i, j : j + 1, :]
            grad_now = grad_ref[i, j : j + 1, :]
            decay = jnp.exp(step_now * rate)
            adjoint = wide(c_ref[i, j], width) * grad_now + flow
            flow = decay * adjoint
            held = flow * states[at]
            alog_sum = alog_sum + step_now * held
            into_drive = jnp.sum(adjoint * wide(b_ref[i, j], width), axis=0, keepdims=True)
            step_out_ref[i, j : j + 1, :] = (
                jnp.sum(rate * held, axis=0, keepdims=True)
                + conv_ref[i, j : j + 1, :] * into_drive
            )
            conv_out_ref[i, j : j + 1, :] = step_now * into_drive
            b_out_ref[i, j] += folded(adjoint * drive_ref[i, j : j + 1, :])
            c_out_ref[i, j] += folded(grad_now * states[at + 1])
        return (flow, alog_sum)

    _, alog_sum = lax.fori_loop(0, groups, retreat, (arriving_ref[...], jnp.zeros_like(rate)))
    alog_ref[...] = alog_sum * rate


def sweeps(length, channels, states):
    block = min(512, channels)
    groups = length // SUB
    rows = pl.BlockSpec((groups, SUB, block), lambda k: (0, 0, k))
    spread = pl.BlockSpec((groups, SUB, states, LANES), lambda k: (0, 0, 0, 0))
    column = pl.BlockSpec((states, block), lambda k: (0, k))
    grid = (channels // block,)
    f32 = jnp.float32
    row_shape = jax.ShapeDtypeStruct((groups, SUB, channels), f32)
    spread_shape = jax.ShapeDtypeStruct((groups, SUB, states, LANES), f32)
    column_shape = jax.ShapeDtypeStruct((states, channels), f32)
    totals = pl.pallas_call(
        totals_kernel,
        grid=grid,
        in_specs=[rows, rows, rows, spread, spread, column],
        out_specs=pl.BlockSpec((3, states, block), lambda k: (0, 0, k)),
        out_shape=jax.ShapeDtypeStruct((3, states, channels), jnp.bfloat16),
        name="totals",
    )
    forward = pl.pallas_call(
        forward_kernel,
        grid=grid,
        in_specs=[rows, rows, spread, spread, column, column],
        out_specs=rows,
        out_shape=row_shape,
        name="forward",
    )
    backward = pl.pallas_call(
        backward_kernel,
        grid=grid,
        in_specs=[rows, rows, rows, rows, spread, spread, column, column, column],
        out_specs=[rows, rows, spread, spread, column],
        out_shape=[row_shape, row_shape, spread_shape, spread_shape, column_shape],
        scratch_shapes=[pltpu.VMEM((length + 1, states, block), f32)],
        name="backward",
    )
    return totals, forward, backward


MESH = pl.DeviceIdType.MESH
GROUP = 16


def places():
    s, z = lax.axis_index("seq"), lax.axis_index("expert")
    core = lax.rem(s, 2)
    sib = s + 1 - 2 * core
    across_x = s + 2 - 4 * lax.rem(lax.div(s, 2), 2)
    across_y = s + 4 - 8 * lax.div(s, 4)
    return s, z, core, sib, across_x, across_y


def transposed(a, b):
    return lax.dot_general(a, b, (((1,), (1,)), ((), ())), preferred_element_type=jnp.float32)


def layer_kernel(
    x_hbm,
    z_hbm,
    dt_hbm,
    bc_ref,
    alog_ref,
    conv_ref,
    bias_ref,
    gain_ref,
    dtb_ref,
    resid_ref,
    ids_ref,
    weight_ref,
    ow_hbm,
    gm_hbm,
    wg_hbm,
    wu_hbm,
    wd_hbm,
    out_ref,
    gx_ref,
    gz_ref,
    gdt_ref,
    alog_out,
    taps_out,
    chan_out,
    bc_out,
    gx_buf,
    gz_buf,
    gdt_buf,
    x_ref,
    z_ref,
    dt_ref,
    rows_all,
    wgu,
    wd,
    ow,
    gm,
    hidden,
    own_h,
    zrecv,
    zfin,
    part,
    psib,
    acc,
    rx,
    ry,
    rdx,
    rdy,
    fin,
    p_buf,
    sums_own,
    sums_recv,
    sums_acc,
    bc_own,
    bc_recv,
    decays,
    states,
    b_wide,
    c_wide,
    b_block,
    c_block,
    step_buf,
    drive_buf,
    conv_buf,
    grad_buf,
    dsilu_buf,
    dtsig_buf,
    zgate_buf,
    zfac_buf,
    into_buf,
    qsum_buf,
    xpad,
    gpad,
    xhalo,
    ghalo,
    gated,
    adj,
    quo,
    gb_acc,
    gc_acc,
    tot,
    tsib,
    tpair,
    trecv,
    rate_buf,
    start_buf,
    arrive_buf,
    w_sem,
    sems,
):
    s, z, core, sib, ax, ay = places()
    diag = ax + ay - s
    f32, bf16 = jnp.float32, jnp.bfloat16
    ways, seqs = 4, 8
    rows = resid_ref.shape[0]
    length, channels = x_ref.shape
    width = resid_ref.shape[1]
    half = width // 2
    scan = channels // 2
    groups = length // GROUP
    nst = alog_ref.shape[0]
    flat = GROUP * nst
    tiles = wgu.shape[1] // 256
    after = lax.rem(s + 1, seqs)
    ahead = lax.rem(s + seqs - 1, seqs)
    count = [0]
    everything = []

    def to(src, dst, seq, exp):
        index = count[0]
        count[0] += 1
        copy = pltpu.make_async_remote_copy(
            src_ref=src,
            dst_ref=dst,
            send_sem=sems.at[0, index],
            recv_sem=sems.at[1, index],
            device_id=(seq, exp),
            device_id_type=MESH,
        )
        everything.append(copy)
        return copy

    first = [
        pltpu.make_async_copy(x_hbm, x_ref, w_sem.at[6 + 2 * tiles]),
        pltpu.make_async_copy(z_hbm, z_ref, w_sem.at[7 + 2 * tiles]),
        pltpu.make_async_copy(dt_hbm, dt_ref, w_sem.at[8 + 2 * tiles]),
        pltpu.make_async_copy(ow_hbm, ow, w_sem.at[0]),
        pltpu.make_async_copy(gm_hbm, gm, w_sem.at[1]),
    ]
    for load in first:
        load.start()
    loads = []
    for t in range(tiles):
        for k, w_hbm in enumerate((wg_hbm, wu_hbm)):
            loads.append(
                pltpu.make_async_copy(
                    w_hbm.at[0, :, pl.ds(t * 128, 128)],
                    wgu.at[:, pl.ds(t * 256 + k * 128, 128)],
                    w_sem.at[2 + 2 * t + k],
                )
            )
    loads.append(pltpu.make_async_copy(wd_hbm.at[0], wd, w_sem.at[2 + 2 * tiles]))

    zs = [lax.rem(z + d, ways) for d in range(ways)]
    zb = [lax.rem(z + ways - d, ways) for d in range(ways)]

    barrier = pltpu.get_barrier_semaphore()
    partners = [(sib, z), (ax, z), (ay, z), (diag, z), (after, z), (ahead, z)]
    partners += [(s, zs[1]), (s, zs[2]), (s, zs[3])]
    for seq, exp in partners:
        pl.semaphore_signal(barrier, inc=1, device_id=(seq, exp), device_id_type=MESH)
    pl.semaphore_wait(barrier, len(partners))

    first[0].wait()
    halo = to(x_ref.at[pl.ds(length - GROUP, GROUP), :], xhalo, after, z)
    halo.start()

    for k, spread in enumerate((b_wide, c_wide)):
        value = bc_ref[k]
        for t in range(length):
            spread[t] = jnp.broadcast_to(value[:, t : t + 1], (nst, LANES))
    lane = lax.broadcasted_iota(jnp.int32, (length, flat), 1)
    row = lax.broadcasted_iota(jnp.int32, (length, flat), 0)
    same_token = lax.div(lane, nst) == lax.rem(row, GROUP)
    lane_r = lax.broadcasted_iota(jnp.int32, (nst, flat), 1)
    row_r = lax.broadcasted_iota(jnp.int32, (nst, flat), 0)
    unit = (lax.rem(lane_r, nst) == row_r).astype(f32)
    repeat = unit.astype(bf16)
    for k, block_ref in enumerate((b_block, c_block)):
        by_token = jnp.transpose(bc_ref[k]).astype(bf16)
        laid = jnp.dot(by_token, repeat, preferred_element_type=f32)
        block_ref[...] = jnp.where(same_token, laid, 0.0).astype(bf16)
    diagonal = same_token[:GROUP].astype(f32)
    ones_block = diagonal.astype(bf16)
    rate_buf[...] = -jnp.exp(alog_ref[...])

    for load in first[1:]:
        load.wait()

    def mix_tile(t, _):
        at = pl.ds(pl.multiple_of(t * 256, 256), 256)
        zfac_buf[:, :, at] = transposed(gm[...], ow[at, :]).reshape(groups, GROUP, 256)
        return 0

    lax.fori_loop(0, channels // 256, mix_tile, 0, unroll=True)
    for load in loads:
        load.start()
    xpad[8 : 8 + length, :] = x_ref[...].astype(f32)
    halo.wait_recv()
    xpad[0:8, :] = jnp.where(s > 0, xhalo[...].astype(f32)[GROUP - 8 :], 0.0)

    def prepare(t, _):
        at = pl.ds(pl.multiple_of(t * LANES, LANES), LANES)

        def put(ref, value):
            ref[:, :, at] = value.reshape(groups, GROUP, LANES)

        pre = bias_ref[:, at] + conv_ref[0:1, at] * xpad[5 : 5 + length, at]
        for tap in range(1, KW):
            pre = pre + conv_ref[tap : tap + 1, at] * xpad[5 + tap : 5 + tap + length, at]
        conv_sig = jax.nn.sigmoid(pre)
        conv_out = pre * conv_sig
        put(conv_buf, conv_out)
        put(dsilu_buf, conv_sig * (1.0 + pre * (1.0 - conv_sig)))
        raw = dt_ref[:, at] + dtb_ref[:, at]
        step = jnp.maximum(raw, 0.0) + jnp.log1p(jnp.exp(-jnp.abs(raw)))
        put(step_buf, step)
        put(drive_buf, step * conv_out)
        put(dtsig_buf, jax.nn.sigmoid(raw))
        z_val = z_ref[:, at].astype(f32)
        z_sig = jax.nn.sigmoid(z_val)
        mixed = zfac_buf[:, :, at].reshape(length, LANES)
        gate = z_val * z_sig
        put(zgate_buf, gate)
        put(grad_buf, mixed * gate)
        put(zfac_buf, mixed * z_sig * (1.0 + z_val * (1.0 - z_sig)))
        return 0

    lax.fori_loop(0, channels // LANES, prepare, 0)

    def lanes(k):
        return pl.ds(k * scan, scan)

    def totals(k, low, high, carry):
        at = lanes(k)
        rate = rate_buf[:, at]

        def advance(i, carry):
            state, passed, leaving = carry
            for j in range(GROUP):
                decay = jnp.exp(step_buf[i, j : j + 1, at] * rate)
                decays[i * GROUP + j, :, at] = decay
                state = decay * state + drive_buf[i, j : j + 1, at] * wide(
                    b_wide[i * GROUP + j], scan
                )
                passed = passed * decay
                leaving = leaving + passed * (
                    grad_buf[i, j : j + 1, at] * wide(c_wide[i * GROUP + j], scan)
                )
            return (state, passed, leaving)

        return lax.fori_loop(low, high, advance, carry)

    zero = jnp.zeros((nst, scan), f32)
    nothing = (zero, jnp.ones_like(zero), zero)

    def keep(k, carry):
        for m in range(3):
            tot[k, m] = carry[m].astype(bf16)

    beside = [to(tot.at[k], tsib.at[k], sib, z) for k in range(2)]
    xbit, ybit = lax.rem(lax.div(s, 2), 2), lax.div(s, 4)
    beyond = []
    for k in range(2):
        for m, (seq, bit) in enumerate(((ax, xbit), (ay, ybit), (diag, ybit))):
            at = pl.ds(bit, 2)
            beyond.append(to(tpair.at[k, at], trecv.at[k, m, at], seq, z))

    def join(k):
        beside[k].wait_recv()
        own = [tot[k, m].astype(f32) for m in range(3)]
        their = [tsib[k, m].astype(f32) for m in range(3)]
        one = [jnp.where(core == 0, a, b) for a, b in zip(own, their)]
        two = [jnp.where(core == 0, b, a) for a, b in zip(own, their)]
        tpair[k, 0] = (two[1] * one[0] + two[0]).astype(bf16)
        tpair[k, 1] = (one[1] * two[1]).astype(bf16)
        tpair[k, 2] = (one[2] + one[1] * two[2]).astype(bf16)
        for copy in beyond[3 * k : 3 * k + 3]:
            copy.start()

    def enter(k):
        for copy in beyond[3 * k : 3 * k + 3]:
            copy.wait_recv()
        chip = lax.div(s, 2)
        start, arriving = zero, zero

        def other_chip(c):
            relation = (c % 2 + xbit - 2 * (c % 2) * xbit) + 2 * (c // 2 + ybit - 2 * (c // 2) * ybit)
            return trecv.at[k, jnp.maximum(relation - 1, 0)]

        for c in range(4):
            at = other_chip(c)
            start = jnp.where(c < chip, at[1].astype(f32) * start + at[0].astype(f32), start)
            at = other_chip(3 - c)
            arriving = jnp.where(
                3 - c > chip, at[1].astype(f32) * arriving + at[2].astype(f32), arriving
            )
        passed = tsib[k, 1].astype(f32)
        start = jnp.where(core == 1, passed * start + tsib[k, 0].astype(f32), start)
        arriving = jnp.where(core == 0, passed * arriving + tsib[k, 2].astype(f32), arriving)
        start_buf[:, lanes(k)] = start
        arrive_buf[:, lanes(k)] = arriving

    keep(0, totals(0, 0, groups, nothing))
    beside[0].start()
    middle = totals(1, 0, groups // 2, nothing)
    join(0)
    keep(1, totals(1, groups // 2, groups, middle))
    beside[1].start()
    join(1)

    def state_rows(at, number):
        return pl.ds(pl.multiple_of(at * nst, nst), number * nst)

    def forward(k):
        at = lanes(k)
        states[0:nst, at] = start_buf[:, at].astype(bf16)

        def advance(i, state):
            for j in range(GROUP):
                t = i * GROUP + j
                state = decays[t, :, at] * state + drive_buf[i, j : j + 1, at] * wide(
                    b_wide[t], scan
                )
                states[state_rows(t + 1, 1), at] = state.astype(bf16)
            here = pl.ds(pl.multiple_of(i * GROUP, GROUP), GROUP)
            y_val = jnp.dot(
                c_block[here, :],
                states[state_rows(i * GROUP + 1, GROUP), at],
                preferred_element_type=f32,
            )
            y_val = y_val + gain_ref[:, at] * conv_buf[i, :, at]
            gz_buf[here, at] = zfac_buf[i, :, at] * y_val
            gated[here, at] = (zgate_buf[i, :, at] * y_val).astype(bf16)
            return state

        lax.fori_loop(0, groups, advance, start_buf[:, at])

    for k in range(2):
        enter(k)
        forward(k)

    written = [
        pltpu.make_async_copy(gz_buf, gz_ref, w_sem.at[3 + 2 * tiles]),
        pltpu.make_async_copy(gdt_buf, gdt_ref, w_sem.at[4 + 2 * tiles]),
        pltpu.make_async_copy(gx_buf, gx_ref, w_sem.at[5 + 2 * tiles]),
    ]
    written[0].start()

    waves = 2
    piece = rows // waves
    pack = ways * piece

    def block(seq, exp, w):
        at = (w * seqs + seq) * pack + exp * piece
        return pl.ds(pl.multiple_of(at, piece), piece)

    def within(exp, w):
        return pl.ds(pl.multiple_of(exp * rows + w * piece, piece), piece)

    def project(t, _):
        at = pl.ds(pl.multiple_of(t * 256, 256), 256)
        p_buf[:, at] = jnp.dot(gated[...], ow[:, at], preferred_element_type=f32).astype(bf16)
        return 0

    lax.fori_loop(0, width // 256, project, 0, unroll=True)

    z_out = [
        [to(p_buf.at[within(zs[d], w)], zrecv.at[w, d - 1], s, zs[d]) for d in (1, 2, 3)]
        for w in range(waves)
    ]
    for copy in z_out[0]:
        copy.start()

    gb_acc[...] = jnp.zeros_like(gb_acc)
    gc_acc[...] = jnp.zeros_like(gc_acc)

    def backward(k):
        at = lanes(k)

        def retreat(n, carry):
            flow, alog_sum = carry
            i = groups - 1 - n
            for j in reversed(range(GROUP)):
                t = i * GROUP + j
                adjoint = wide(c_wide[t], scan) * grad_buf[i, j : j + 1, at] + flow
                adj[j * nst : (j + 1) * nst, :] = adjoint.astype(bf16)
                flow = decays[t, :, at] * adjoint
                share = rate_buf[:, at] * (flow * states[state_rows(t, 1), at].astype(f32))
                alog_sum = alog_sum + step_buf[i, j : j + 1, at] * share
                quo[j * nst : (j + 1) * nst, :] = share.astype(bf16)
            here = pl.ds(pl.multiple_of(i * GROUP, GROUP), GROUP)
            into_buf[i, :, at] = jnp.dot(b_block[here, :], adj[...], preferred_element_type=f32)
            qsum_buf[i, :, at] = jnp.dot(ones_block, quo[...], preferred_element_type=f32)
            gb_acc[i] += transposed(drive_buf[i, :, at].astype(bf16), adj[...])
            gc_acc[i] += transposed(
                grad_buf[i, :, at].astype(bf16), states[state_rows(i * GROUP + 1, GROUP), at]
            )
            return (flow, alog_sum)

        _, alog_sum = lax.fori_loop(0, groups, retreat, (arrive_buf[:, at], zero))
        sums_own[0:nst, at] = alog_sum

    gather, to_x, to_y, to_b, forward = [], [], [], [], []
    for w in range(waves):
        here = rows_all.at[block(s, z, w)]
        gather.append([to(here, here, s, zs[d]) for d in (1, 2, 3)])
        blocks = [rows_all.at[block(s, zb[d], w)] for d in range(ways)]
        to_x.append([to(at, at, ax, z) for at in blocks])
        to_y.append([to(at, at, ay, z) for at in blocks])
        to_b.append([to(at, at, sib, z) for at in blocks])
        passing = []
        for d in range(ways):
            origin, target = (ay, ax) if d < 2 else (ax, ay)
            at = rows_all.at[block(origin, zb[d], w)]
            passing.append(to(at, at, target, z))
        forward.append(passing)

    def mixed_rows(w):
        for copy in z_out[w]:
            copy.wait_recv()
        own = pl.ds(w * piece, piece)
        total = resid_ref[own, :].astype(f32) + p_buf[within(z, w), :].astype(f32)
        for d in range(3):
            total = total + zrecv[w, d].astype(f32)
        own_h[own, :] = total.astype(bf16)
        rows_all[block(s, z, w), :] = total.astype(bf16)
        for copy in gather[w] + [to_x[w][0], to_y[w][0], to_b[w][0]]:
            copy.start()

    def spread_rows(w):
        for d in (1, 2, 3):
            gather[w][d - 1].wait_recv()
            to_x[w][d].start()
            to_y[w][d].start()
            to_b[w][d].start()

    backward(0)
    for copy in z_out[1]:
        copy.start()
    mixed_rows(0)
    backward(1)
    for k, held in enumerate((gb_acc, gc_acc)):
        kept = jnp.where(same_token, held[...].reshape(length, flat), 0.0)
        bc_own[k] = lax.dot_general(
            unit,
            kept,
            (((1,), (1,)), ((), ())),
            precision=lax.Precision.HIGHEST,
            preferred_element_type=f32,
        )
    bc_copies = [to(bc_own, bc_recv.at[d - 1], s, zs[d]) for d in (1, 2, 3)]
    for copy in bc_copies:
        copy.start()

    def finish(t, _):
        at = pl.ds(pl.multiple_of(t * LANES, LANES), LANES)

        def get(ref):
            return ref[:, :, at].reshape(length, LANES)

        def total(value):
            return jnp.sum(value, axis=0, keepdims=True)

        into, conv_out, grad_y = get(into_buf), get(conv_buf), get(grad_buf)
        grad_dt = (get(qsum_buf) + conv_out * into) * get(dtsig_buf)
        gdt_buf[:, at] = grad_dt
        grad_pre = (gain_ref[:, at] * grad_y + get(step_buf) * into) * get(dsilu_buf)
        gpad[0:length, at] = grad_pre
        for tap in range(KW):
            sums_own[nst + tap : nst + tap + 1, at] = total(
                grad_pre * xpad[5 + tap : 5 + tap + length, at]
            )
        sums_own[nst + KW : nst + KW + 1, at] = total(grad_pre)
        sums_own[nst + KW + 1 : nst + KW + 2, at] = total(grad_y * conv_out)
        sums_own[nst + KW + 2 : nst + KW + 3, at] = total(grad_dt)
        return 0

    lax.fori_loop(0, channels // LANES, finish, 0)
    written[1].start()
    sums_own[nst + KW + 3 :, :] = jnp.zeros_like(sums_own[nst + KW + 3 :, :])
    rim = to(gpad.at[pl.ds(0, 8)], ghalo, ahead, z)
    rim.start()
    sums_copies = [
        to(sums_own, sums_recv.at[0], sib, z),
        to(sums_acc.at[0], sums_recv.at[1], ax, z),
        to(sums_acc.at[1], sums_recv.at[2], ay, z),
    ]
    sums_copies[0].start()
    mixed_rows(1)
    sums_copies[0].wait_recv()
    sums_acc[0] = sums_own[...] + sums_recv[0]
    sums_copies[1].start()
    spread_rows(0)
    rim.wait_recv()
    gpad[length : length + 8, :] = jnp.where(s < seqs - 1, ghalo[...], 0.0)

    def spread_back(t, _):
        at = pl.ds(pl.multiple_of(t * LANES, LANES), LANES)
        grad_x = conv_ref[KW - 1 : KW, at] * gpad[0:length, at]
        for tap in range(KW - 1):
            away = KW - 1 - tap
            grad_x = grad_x + conv_ref[tap : tap + 1, at] * gpad[away : away + length, at]
        gx_buf[:, at] = grad_x
        return 0

    lax.fori_loop(0, channels // LANES, spread_back, 0)
    written[2].start()
    to_y[0][0].wait_recv()
    forward[0][0].start()

    sums_copies[1].wait_recv()
    sums_acc[1] = sums_acc[0] + sums_recv[1]
    sums_copies[2].start()

    for copy in bc_copies:
        copy.wait_recv()
    bc_out[...] = (bc_own[...] + bc_recv[0]) + (bc_recv[1] + bc_recv[2])

    def up(w, seq):
        first_row = (w * seqs + 4 * lax.div(seq, 4)) * pack
        at = pl.ds(pl.multiple_of(first_row, 4 * pack), 4 * pack)

        def tile(t, _):
            both = jnp.dot(
                rows_all[at, :],
                wgu[:, pl.ds(pl.multiple_of(t * 256, 256), 256)],
                preferred_element_type=f32,
            )
            gate, upper = both[:, :128], both[:, 128:]
            value = gate * jax.nn.sigmoid(gate) * upper
            hidden[:, pl.ds(pl.multiple_of(t * 128, 128), 128)] = value.astype(bf16)
            return 0

        lax.fori_loop(0, tiles, tile, 0, unroll=True)

    quarter = width // 4
    order = (0, 2, 1, 3)

    def cols(h):
        return pl.ds(h * quarter, quarter)

    def small(h):
        return pl.ds((h % 2) * quarter, quarter)

    def part_rows(r, of_core):
        side = xbit if r % 2 == 0 else 1 - xbit
        return pl.ds(pl.multiple_of((2 * side + of_core) * pack, pack), pack)

    pair = {}

    def down(w, r0, h):
        g = 2 * w + r0 // 2
        part[g, :, cols(h)] = jnp.dot(
            hidden[...], wd[:, cols(h)], preferred_element_type=f32
        ).astype(bf16)
        for r in (r0, r0 + 1):
            copy = to(
                part.at[g, part_rows(r, 1 - core), cols(h)], psib.at[w, r, :, cols(h)], sib, z
            )
            copy.start()
            pair[w, r, h] = copy

    def paired(w, r, h):
        pair[w, r, h].wait_recv()
        acc[w, r, :, cols(h)] = (
            part[2 * w + r // 2, part_rows(r, core), cols(h)].astype(f32)
            + psib[w, r, :, cols(h)].astype(f32)
        ).astype(bf16)

    def pack_of(seq, w):
        at = (w * seqs + seq) * pack
        return rows_all.at[pl.ds(pl.multiple_of(at, pack), pack)]

    share_out = [[to(pack_of(o, w), pack_of(o, w), sib, z) for o in (ax, ay, diag)] for w in range(waves)]
    send = {}

    def reduce_out(name, src, dst, seq):
        copy = to(src, dst, seq, z)
        copy.start()
        send[name] = copy

    def to_across_x(w, h):
        reduce_out(("x", w, h), acc.at[w, 1, :, cols(h)], rx.at[w, :, cols(h)], ax)

    def to_across_y(w, h):
        reduce_out(("y", w, h), acc.at[w, 2, :, cols(h)], ry.at[w, :, cols(h)], ay)

    def near(w):
        to_x[w][0].wait_recv()
        to_x[w][1].wait_recv()
        to_y[w][1].wait_recv()
        forward[w][1].start()
        to_x[w][2].wait_recv()
        forward[w][2].start()
        to_x[w][3].wait_recv()
        forward[w][3].start()
        share_out[w][0].start()
        to_y[w][2].wait_recv()
        to_y[w][3].wait_recv()
        share_out[w][1].start()

    def near_ready(w):
        for copy in to_b[w]:
            copy.wait_recv()
        share_out[w][0].wait_recv()

    def far(w):
        for copy in forward[w]:
            copy.wait_recv()
        share_out[w][2].start()

    def far_ready(w):
        share_out[w][1].wait_recv()
        share_out[w][2].wait_recv()

    def diagonal_out(w, h):
        paired(w, 3, h)
        if h < 2:
            reduce_out(("d", w, h), acc.at[w, 3, :, cols(h)], rdx.at[w, :, small(h)], ax)
        else:
            reduce_out(("d", w, h), acc.at[w, 3, :, cols(h)], rdy.at[w, :, small(h)], ay)

    def direct_x(w):
        for h in (0, 1):
            paired(w, 1, h)
            to_across_x(w, h)
        for h in (2, 3):
            paired(w, 1, h)

    def direct_y(w):
        for h in (2, 3):
            paired(w, 2, h)
            to_across_y(w, h)
        for h in (0, 1):
            paired(w, 2, h)
        for h in range(4):
            paired(w, 0, h)

    def joined(w):
        for h in order:
            send["d", w, h].wait_recv()
            r, got = (2, rdx) if h < 2 else (1, rdy)
            acc[w, r, :, cols(h)] = (
                acc[w, r, :, cols(h)].astype(f32) + got[w, :, small(h)].astype(f32)
            ).astype(bf16)
            if h < 2:
                to_across_y(w, h)
            else:
                to_across_x(w, h)

    back = {}

    def reduced(w, h):
        send["x", w, h].wait_recv()
        send["y", w, h].wait_recv()
        total = (
            acc[w, 0, :, cols(h)].astype(f32)
            + rx[w, :, cols(h)].astype(f32)
            + ry[w, :, cols(h)].astype(f32)
        ).astype(bf16)
        fin[w, :, cols(h)] = total
        for d in (1, 2, 3):
            at = pl.ds(pl.multiple_of(zs[d] * piece, piece), piece)
            copy = to(fin.at[w, at, cols(h)], zfin.at[w, d - 1, :, cols(h)], s, zs[d])
            copy.start()
            back[w, h, d] = copy

    eye = lax.broadcasted_iota(jnp.int32, (rows, rows), 0) == lax.broadcasted_iota(
        jnp.int32, (rows, rows), 1
    )

    def column(row):
        return jnp.sum(jnp.where(eye, row, 0.0), axis=1, keepdims=True)

    shares = []
    for d in range(ways):
        mine = [
            jnp.where(ids_ref[k : k + 1, :] == zb[d], weight_ref[k : k + 1, :], 0.0) for k in range(2)
        ]
        shares.append(column(mine[0] + mine[1]))

    def result(w, h):
        own = pl.ds(w * piece, piece)
        at = pl.ds(pl.multiple_of(z * piece, piece), piece)
        total = own_h[own, cols(h)].astype(f32)
        total = total + shares[0][w * piece : (w + 1) * piece] * fin[w, at, cols(h)].astype(f32)
        for d in (1, 2, 3):
            back[w, h, d].wait_recv()
            total = total + shares[d][w * piece : (w + 1) * piece] * zfin[
                w, d - 1, :, cols(h)
            ].astype(f32)
        out_ref[own, cols(h)] = total.astype(bf16)

    near(0)
    spread_rows(1)
    near_ready(0)
    for load in loads:
        load.wait()
    to_y[1][0].wait_recv()
    forward[1][0].start()
    up(0, s)
    far(0)
    for h in range(4):
        down(0, 0, h)
    far_ready(0)
    up(0, ay)
    near(1)
    for h in order:
        down(0, 2, h)
    direct_x(0)
    for h in order:
        diagonal_out(0, h)
    direct_y(0)
    near_ready(1)
    up(1, s)
    far(1)
    for h in range(4):
        down(1, 0, h)
    joined(0)
    direct_x(1)
    far_ready(1)
    up(1, ay)
    for h in order:
        reduced(0, h)
    down(1, 2, 0)
    down(1, 2, 2)
    diagonal_out(1, 0)
    down(1, 2, 1)
    diagonal_out(1, 2)
    down(1, 2, 3)
    diagonal_out(1, 1)
    diagonal_out(1, 3)
    direct_y(1)

    sums_copies[2].wait_recv()
    summed = sums_acc[1] + sums_recv[2]
    alog_out[...] = summed[:nst]
    taps_out[...] = summed[nst : nst + KW]
    chan_out[...] = summed[nst + KW : nst + KW + 3]

    for h in order:
        result(0, h)
    joined(1)
    for h in order:
        reduced(1, h)
    for h in order:
        result(1, h)
    for copy in written:
        copy.wait()
    for copy in everything:
        copy.wait_send()


def deliver_kernel(number, *refs):
    given, results, stops, sem = (
        refs[:number],
        refs[number : 2 * number],
        refs[2 * number : 3 * number],
        refs[3 * number],
    )
    fetch = [pltpu.make_async_copy(given[k], stops[k], sem.at[0, k]) for k in range(number)]
    store = [pltpu.make_async_copy(stops[k], results[k], sem.at[1, k]) for k in range(number)]
    for copy in fetch:
        copy.start()
    for k in range(number):
        fetch[k].wait()
        store[k].start()
    for copy in store:
        copy.wait()


def deliver(arrays):
    number = len(arrays)
    anywhere = pl.BlockSpec(memory_space=pl.ANY)
    return pl.pallas_call(
        functools.partial(deliver_kernel, number),
        out_shape=[jax.ShapeDtypeStruct(a.shape, a.dtype) for a in arrays],
        in_specs=[anywhere] * number,
        out_specs=[anywhere] * number,
        scratch_shapes=[pltpu.VMEM(a.shape, a.dtype) for a in arrays]
        + [pltpu.SemaphoreType.DMA((2, number))],
        name="deliver",
    )(*arrays)


def layer(
    x_in,
    z_in,
    dt_raw,
    bc_in,
    a_log,
    taps,
    bias,
    gain,
    dt_bias,
    resid,
    route_ids,
    route_weight,
    out_weight,
    grad_mix,
    w_gate,
    w_up,
    w_down,
):
    rows, width = resid.shape
    length, channels = x_in.shape
    states = a_log.shape[0]
    units = w_gate.shape[2]
    tiles = units // 128
    seqs = lax.axis_size("seq")
    half, scan, groups = width // 2, channels // 2, length // GROUP
    bf16, f32 = jnp.bfloat16, jnp.float32
    vmem = pl.BlockSpec(memory_space=pltpu.VMEM)
    hbm = pl.BlockSpec(memory_space=pl.ANY)
    sem = pltpu.SemaphoreType.DMA
    flat = GROUP * states

    def held(*shape, kind=f32):
        return pltpu.VMEM(shape, kind)

    def rows_of():
        return held(groups, GROUP, channels)

    summed = (states + 8, channels)
    grads = (2, states, length)
    return pl.pallas_call(
        layer_kernel,
        out_shape=[
            jax.ShapeDtypeStruct((rows, width), bf16),
            jax.ShapeDtypeStruct((length, channels), f32),
            jax.ShapeDtypeStruct((length, channels), f32),
            jax.ShapeDtypeStruct((length, channels), f32),
            jax.ShapeDtypeStruct((states, channels), f32),
            jax.ShapeDtypeStruct((KW, channels), f32),
            jax.ShapeDtypeStruct((3, channels), f32),
            jax.ShapeDtypeStruct(grads, f32),
        ],
        in_specs=[hbm] * 3 + [vmem] * 9 + [hbm] * 5,
        out_specs=[vmem] + [hbm] * 3 + [vmem] * 4,
        scratch_shapes=[
            held(length, channels),
            held(length, channels),
            held(length, channels),
            held(length, channels, kind=bf16),
            held(length, channels, kind=bf16),
            held(length, channels),
            held(seqs * length, width, kind=bf16),
            held(width, 2 * units, kind=bf16),
            held(units, width, kind=bf16),
            held(channels, width, kind=bf16),
            held(length, width, kind=bf16),
            held(2 * length, units, kind=bf16),
            held(rows, width, kind=bf16),
            held(2, 3, rows // 2, width, kind=bf16),
            held(2, 3, rows // 2, width, kind=bf16),
            held(4, 2 * length, width, kind=bf16),
            held(2, 4, length // 2, width, kind=bf16),
            held(2, 4, length // 2, width, kind=bf16),
            held(2, length // 2, width, kind=bf16),
            held(2, length // 2, width, kind=bf16),
            held(2, length // 2, half, kind=bf16),
            held(2, length // 2, half, kind=bf16),
            held(2, length // 2, width, kind=bf16),
            held(length, width, kind=bf16),
            held(*summed),
            held(3, *summed),
            held(2, *summed),
            held(*grads),
            held(3, *grads),
            held(length, states, channels),
            held((length + 1) * states, channels, kind=bf16),
            held(length, states, LANES),
            held(length, states, LANES),
            held(length, flat, kind=bf16),
            held(length, flat, kind=bf16),
        ]
        + [rows_of() for _ in range(10)]
        + [
            held(length + 8, channels),
            held(length + 8, channels),
            held(GROUP, channels, kind=bf16),
            held(8, channels),
            held(length, channels, kind=bf16),
            held(flat, scan, kind=bf16),
            held(flat, scan, kind=bf16),
            held(groups, GROUP, flat),
            held(groups, GROUP, flat),
            held(2, 3, states, scan, kind=bf16),
            held(2, 3, states, scan, kind=bf16),
            held(2, 3, states, scan, kind=bf16),
            held(2, 3, 3, states, scan, kind=bf16),
            held(states, channels),
            held(states, channels),
            held(states, channels),
            sem((2 * tiles + 9,)),
            sem((2, 192)),
        ],
        compiler_params=pltpu.CompilerParams(
            collective_id=0, has_side_effects=True, vmem_limit_bytes=60 << 20
        ),
        cost_estimate=pl.CostEstimate(
            flops=6 * seqs * length * width * units + 4 * length * width * channels,
            bytes_accessed=6 * width * units,
            transcendentals=seqs * length * units + length * channels * states,
        ),
        name="layer",
    )(
        x_in,
        z_in,
        dt_raw,
        bc_in,
        a_log,
        taps,
        bias.reshape(1, channels),
        gain.reshape(1, channels),
        dt_bias.reshape(1, channels),
        resid,
        route_ids.T,
        route_weight.T,
        out_weight,
        grad_mix,
        w_gate,
        w_up,
        w_down,
    )


def entering(everything):
    peers, here = everything.shape[0], lax.axis_index("seq")
    values = everything.astype(jnp.float32)
    start = jnp.zeros_like(values[0, 0])
    arriving = jnp.zeros_like(start)
    for k in range(peers):
        start = jnp.where(k < here, values[k, 0] * start + values[k, 1], start)
        back = peers - 1 - k
        arriving = jnp.where(back > here, values[back, 0] * arriving + values[back, 2], arriving)
    return start, arriving


def routed_experts(partial_value, resid, w_gate, w_up, w_down, route_ids, route_weight):
    rows = resid.shape[0]
    mixed = lax.psum(partial_value, "expert").astype(jnp.float32)
    own = lax.dynamic_slice_in_dim(mixed, lax.axis_index("expert") * rows, rows, 0)
    hidden_in = (resid.astype(jnp.float32) + own).astype(jnp.bfloat16)
    experts = lax.axis_size("expert")
    capacity = 4 * rows // experts
    flat_ids = route_ids.reshape(-1)
    order = jnp.arange(flat_ids.shape[0], dtype=jnp.int32)
    earlier = (flat_ids[:, None] == flat_ids[None, :]) & (order[None, :] < order[:, None])
    rank = jnp.sum(earlier.astype(jnp.int32), axis=1)
    slot = flat_ids * capacity + rank
    placing = (jnp.arange(experts * capacity, dtype=jnp.int32)[:, None] == slot[None, :]).astype(
        jnp.bfloat16
    )
    doubled = jnp.repeat(hidden_in, 2, axis=0)
    outgoing = jnp.dot(placing, doubled, preferred_element_type=jnp.float32).astype(jnp.bfloat16)
    incoming = lax.all_to_all(outgoing, "expert", split_axis=0, concat_axis=0, tiled=True)
    piece = lax.all_gather(incoming, "seq", axis=0, tiled=True)
    gate = jnp.dot(piece, w_gate[0], preferred_element_type=jnp.float32)
    upper = jnp.dot(piece, w_up[0], preferred_element_type=jnp.float32)
    hidden = (jax.nn.silu(gate) * upper).astype(jnp.bfloat16)
    expert_sum = lax.psum_scatter(
        jnp.dot(hidden, w_down[0], preferred_element_type=jnp.float32).astype(jnp.bfloat16),
        "seq",
        scatter_dimension=0,
        tiled=True,
    )
    returned = lax.all_to_all(expert_sum, "expert", split_axis=0, concat_axis=0, tiled=True)
    picked = lax.dot_general(
        placing, returned, (((0,), (0,)), ((), ())), preferred_element_type=jnp.float32
    )
    picked = picked.reshape(rows, 2, -1)
    moe = picked[:, 0] * route_weight[:, 0:1] + picked[:, 1] * route_weight[:, 1:2]
    return (hidden_in.astype(jnp.float32) + moe).astype(jnp.bfloat16)


def local(
    x_in,
    z_in,
    dt_raw,
    bc_in,
    a_log,
    conv_weight,
    conv_bias,
    skip_gain,
    dt_bias,
    out_weight,
    resid,
    w_gate,
    w_up,
    w_down,
    route_ids,
    route_weight,
    grad_mix,
):
    length, channels = x_in.shape
    states = a_log.shape[0]
    rim = KW - 1
    rows = resid.shape[0]
    experts = lax.axis_size("expert")
    if experts == 4 and lax.axis_size("seq") == 8:
        layer_out, grad_x, grad_z, grad_dt, grad_alog, grad_conv, grad_chan, grad_bc = deliver(
            layer(
                x_in,
                z_in,
                dt_raw,
                bc_in,
                a_log,
                conv_weight,
                conv_bias,
                skip_gain,
                dt_bias,
                resid,
                route_ids,
                route_weight,
                out_weight,
                grad_mix,
                w_gate,
                w_up,
                w_down,
            )
        )
        return (layer_out, grad_x, grad_z, grad_dt, grad_bc, grad_alog, grad_conv, grad_chan)
    x_val = x_in.astype(jnp.float32)
    z_val = z_in.astype(jnp.float32)
    before = shifted(x_in[length - rim :], "seq", 1)
    padded = jnp.concatenate([before.astype(jnp.float32), x_val], axis=0)
    pre = conv_bias[None, :] + conv_weight[0][None, :] * padded[0:length]
    for tap in range(1, KW):
        pre = pre + conv_weight[tap][None, :] * padded[tap : tap + length]
    conv_sig = jax.nn.sigmoid(pre)
    conv_out = pre * conv_sig
    step = jax.nn.softplus(dt_raw + dt_bias[None, :])
    rate = -jnp.exp(a_log)
    drive = step * conv_out
    z_sig = jax.nn.sigmoid(z_val)
    back_mix = lax.dot_general(
        grad_mix, out_weight, (((1,), (1,)), ((), ())), preferred_element_type=jnp.float32
    )
    grad_y = back_mix * z_val * z_sig

    def grouped(array):
        return array.reshape(length // SUB, SUB, channels)

    def flat(array):
        return array.reshape(length, channels)

    spread = jnp.broadcast_to(
        bc_in.transpose(0, 2, 1)[:, :, :, None], (2, length, states, LANES)
    ).reshape(2, length // SUB, SUB, states, LANES)
    b_wide, c_wide = spread[0], spread[1]
    totals, forward, backward = sweeps(length, channels, states)
    step_g, drive_g, grad_g, conv_g = (grouped(a) for a in (step, drive, grad_y, conv_out))
    own_totals = totals(step_g, drive_g, grad_g, b_wide, c_wide, rate)
    start, arriving = entering(lax.all_gather(own_totals, "seq"))
    y_val = flat(forward(step_g, drive_g, b_wide, c_wide, rate, start))
    y_val = y_val + skip_gain[None, :] * conv_out
    gated = (y_val * z_val * z_sig).astype(jnp.bfloat16)
    partial_value = jnp.dot(gated, out_weight, preferred_element_type=jnp.float32)
    grad_z = back_mix * y_val * z_sig * (1.0 + z_val * (1.0 - z_sig))
    grad_step, conv_part_grad, grad_b, grad_c, grad_alog_local = backward(
        step_g, drive_g, conv_g, grad_g, b_wide, c_wide, rate, start, arriving
    )
    grad_step, conv_part_grad = flat(grad_step), flat(conv_part_grad)
    grad_conv_out = skip_gain[None, :] * grad_y + conv_part_grad
    grad_skip = jnp.sum(grad_y * conv_out, axis=0)
    grad_dt = grad_step * jax.nn.sigmoid(dt_raw + dt_bias[None, :])
    grad_pre = grad_conv_out * (conv_sig * (1.0 + pre * (1.0 - conv_sig)))
    after = shifted(grad_pre[:rim], "seq", -1)
    grad_pad = jnp.concatenate([grad_pre, after], axis=0)
    grad_x = conv_weight[rim][None, :] * grad_pad[0:length]
    for tap in range(rim):
        grad_x = grad_x + conv_weight[tap][None, :] * grad_pad[rim - tap : rim - tap + length]
    grad_taps = jnp.stack(
        [jnp.sum(grad_pre * padded[tap : tap + length], axis=0) for tap in range(KW)]
    )
    channel_grads = jnp.stack([jnp.sum(grad_pre, axis=0), grad_skip, jnp.sum(grad_dt, axis=0)])
    own_sums = jnp.concatenate([grad_alog_local, grad_taps, channel_grads], axis=0)
    own_bc = jnp.stack([jnp.sum(grad_b, axis=-1), jnp.sum(grad_c, axis=-1)])
    own_bc = own_bc.reshape(2, length, states).transpose(0, 2, 1).reshape(2 * states, length)
    layer_out = routed_experts(
        partial_value.astype(jnp.bfloat16),
        resid,
        w_gate,
        w_up,
        w_down,
        route_ids,
        route_weight,
    )
    sums = lax.psum(own_sums, "seq")
    grad_bc = lax.psum(own_bc, "expert").reshape(2, states, length)
    grad_alog = sums[:states]
    grad_conv = sums[states : states + KW]
    grad_chan = sums[states + KW : states + KW + 3]
    return (layer_out, grad_x, grad_z, grad_dt, grad_bc, grad_alog, grad_conv, grad_chan)


def solution(mesh):
    in_specs = (
        P("seq", "expert"),
        P("seq", "expert"),
        P("seq", "expert"),
        P(None, None, "seq"),
        P(None, "expert"),
        P(None, "expert"),
        P("expert"),
        P("expert"),
        P("expert"),
        P("expert", None),
        P(("seq", "expert"), None),
        P("expert", None, "seq"),
        P("expert", None, "seq"),
        P("expert", "seq", None),
        P(("seq", "expert"), None),
        P(("seq", "expert"), None),
        P("seq", None),
    )
    out_specs = (
        P(("seq", "expert"), None),
        P("seq", "expert"),
        P("seq", "expert"),
        P("seq", "expert"),
        P(None, None, "seq"),
        P(None, "expert"),
        P(None, "expert"),
        P(None, "expert"),
    )
    return jax.shard_map(local, mesh=mesh, in_specs=in_specs, out_specs=out_specs, check_vma=False)
```

```python
import functools

import jax
import jax.numpy as jnp
from jax import lax
from jax.experimental import pallas as pl
from jax.experimental.pallas import tpu as pltpu
from jax.sharding import PartitionSpec as P

KW = 4
SUB = 8
LANES = 128


def shifted(x, axis, by):
    peers = lax.axis_size(axis)
    pairs = [(i, i + by) for i in range(peers) if 0 <= i + by < peers]
    return lax.ppermute(x, axis, pairs)


def wide(tile, width):
    return jnp.concatenate([tile] * (width // tile.shape[1]), axis=1)


def folded(value):
    total = value[:, :LANES]
    for at in range(LANES, value.shape[1], LANES):
        total = total + value[:, at : at + LANES]
    return total


def totals_kernel(step_ref, drive_ref, grad_ref, b_ref, c_ref, rate_ref, out_ref):
    rate = rate_ref[...]
    width = rate.shape[1]

    def advance(i, carry):
        state, passed, leaving = carry
        for j in range(SUB):
            decay = jnp.exp(step_ref[i, j : j + 1, :] * rate)
            state = decay * state + drive_ref[i, j : j + 1, :] * wide(b_ref[i, j], width)
            passed = passed * decay
            leaving = leaving + passed * (grad_ref[i, j : j + 1, :] * wide(c_ref[i, j], width))
        return (state, passed, leaving)

    zero = jnp.zeros_like(rate)
    state, passed, leaving = lax.fori_loop(
        0, step_ref.shape[0], advance, (zero, jnp.ones_like(rate), zero)
    )
    out_ref[0] = passed.astype(out_ref.dtype)
    out_ref[1] = state.astype(out_ref.dtype)
    out_ref[2] = leaving.astype(out_ref.dtype)


def forward_kernel(step_ref, drive_ref, b_ref, c_ref, rate_ref, start_ref, y_ref):
    rate = rate_ref[...]
    width = rate.shape[1]

    def advance(i, state):
        for j in range(SUB):
            decay = jnp.exp(step_ref[i, j : j + 1, :] * rate)
            state = decay * state + drive_ref[i, j : j + 1, :] * wide(b_ref[i, j], width)
            y_ref[i, j : j + 1, :] = jnp.sum(
                wide(c_ref[i, j], width) * state, axis=0, keepdims=True
            )
        return state

    lax.fori_loop(0, step_ref.shape[0], advance, start_ref[...])


def backward_kernel(
    step_ref,
    drive_ref,
    conv_ref,
    grad_ref,
    b_ref,
    c_ref,
    rate_ref,
    start_ref,
    arriving_ref,
    step_out_ref,
    conv_out_ref,
    b_out_ref,
    c_out_ref,
    alog_ref,
    states,
):
    rate = rate_ref[...]
    width = rate.shape[1]
    groups = step_ref.shape[0]

    @pl.when(pl.program_id(0) == 0)
    def _():
        b_out_ref[...] = jnp.zeros_like(b_out_ref)
        c_out_ref[...] = jnp.zeros_like(c_out_ref)

    states[0] = start_ref[...]

    def advance(i, state):
        for j in range(SUB):
            decay = jnp.exp(step_ref[i, j : j + 1, :] * rate)
            state = decay * state + drive_ref[i, j : j + 1, :] * wide(b_ref[i, j], width)
            states[i * SUB + j + 1] = state
        return state

    lax.fori_loop(0, groups, advance, start_ref[...])

    def retreat(k, carry):
        flow, alog_sum = carry
        i = groups - 1 - k
        for j in reversed(range(SUB)):
            at = i * SUB + j
            step_now = step_ref[i, j : j + 1, :]
            grad_now = grad_ref[i, j : j + 1, :]
            decay = jnp.exp(step_now * rate)
            adjoint = wide(c_ref[i, j], width) * grad_now + flow
            flow = decay * adjoint
            held = flow * states[at]
            alog_sum = alog_sum + step_now * held
            into_drive = jnp.sum(adjoint * wide(b_ref[i, j], width), axis=0, keepdims=True)
            step_out_ref[i, j : j + 1, :] = (
                jnp.sum(rate * held, axis=0, keepdims=True)
                + conv_ref[i, j : j + 1, :] * into_drive
            )
            conv_out_ref[i, j : j + 1, :] = step_now * into_drive
            b_out_ref[i, j] += folded(adjoint * drive_ref[i, j : j + 1, :])
            c_out_ref[i, j] += folded(grad_now * states[at + 1])
        return (flow, alog_sum)

    _, alog_sum = lax.fori_loop(0, groups, retreat, (arriving_ref[...], jnp.zeros_like(rate)))
    alog_ref[...] = alog_sum * rate


def sweeps(length, channels, states):
    block = min(512, channels)
    groups = length // SUB
    rows = pl.BlockSpec((groups, SUB, block), lambda k: (0, 0, k))
    spread = pl.BlockSpec((groups, SUB, states, LANES), lambda k: (0, 0, 0, 0))
    column = pl.BlockSpec((states, block), lambda k: (0, k))
    grid = (channels // block,)
    f32 = jnp.float32
    row_shape = jax.ShapeDtypeStruct((groups, SUB, channels), f32)
    spread_shape = jax.ShapeDtypeStruct((groups, SUB, states, LANES), f32)
    column_shape = jax.ShapeDtypeStruct((states, channels), f32)
    totals = pl.pallas_call(
        totals_kernel,
        grid=grid,
        in_specs=[rows, rows, rows, spread, spread, column],
        out_specs=pl.BlockSpec((3, states, block), lambda k: (0, 0, k)),
        out_shape=jax.ShapeDtypeStruct((3, states, channels), jnp.bfloat16),
        name="totals",
    )
    forward = pl.pallas_call(
        forward_kernel,
        grid=grid,
        in_specs=[rows, rows, spread, spread, column, column],
        out_specs=rows,
        out_shape=row_shape,
        name="forward",
    )
    backward = pl.pallas_call(
        backward_kernel,
        grid=grid,
        in_specs=[rows, rows, rows, rows, spread, spread, column, column, column],
        out_specs=[rows, rows, spread, spread, column],
        out_shape=[row_shape, row_shape, spread_shape, spread_shape, column_shape],
        scratch_shapes=[pltpu.VMEM((length + 1, states, block), f32)],
        name="backward",
    )
    return totals, forward, backward


MESH = pl.DeviceIdType.MESH
GROUP = 16


def places():
    s, z = lax.axis_index("seq"), lax.axis_index("expert")
    core = lax.rem(s, 2)
    sib = s + 1 - 2 * core
    across_x = s + 2 - 4 * lax.rem(lax.div(s, 2), 2)
    across_y = s + 4 - 8 * lax.div(s, 4)
    return s, z, core, sib, across_x, across_y


def transposed(a, b):
    return lax.dot_general(a, b, (((1,), (1,)), ((), ())), preferred_element_type=jnp.float32)


def layer_kernel(
    x_hbm,
    z_hbm,
    dt_hbm,
    bc_ref,
    alog_ref,
    conv_ref,
    bias_ref,
    gain_ref,
    dtb_ref,
    resid_ref,
    ids_ref,
    weight_ref,
    ow_hbm,
    gm_hbm,
    wg_hbm,
    wu_hbm,
    wd_hbm,
    out_ref,
    gx_ref,
    gz_ref,
    gdt_ref,
    alog_out,
    taps_out,
    chan_out,
    bc_out,
    gx_buf,
    gz_buf,
    gdt_buf,
    x_ref,
    z_ref,
    dt_ref,
    rows_all,
    wgu,
    wd,
    ow,
    gm,
    hidden,
    own_h,
    zrecv,
    zfin,
    part,
    psib,
    acc,
    rx,
    ry,
    rdx,
    rdy,
    fin,
    p_buf,
    sums_own,
    sums_recv,
    sums_acc,
    bc_own,
    bc_recv,
    decays,
    states,
    b_wide,
    c_wide,
    b_block,
    c_block,
    step_buf,
    drive_buf,
    conv_buf,
    grad_buf,
    dsilu_buf,
    dtsig_buf,
    zgate_buf,
    zfac_buf,
    into_buf,
    qsum_buf,
    xpad,
    gpad,
    xhalo,
    ghalo,
    gated,
    adj,
    quo,
    gb_acc,
    gc_acc,
    tot,
    tsib,
    tpair,
    trecv,
    rate_buf,
    start_buf,
    arrive_buf,
    w_sem,
    sems,
):
    s, z, core, sib, ax, ay = places()
    diag = ax + ay - s
    f32, bf16 = jnp.float32, jnp.bfloat16
    ways, seqs = 4, 8
    rows = resid_ref.shape[0]
    length, channels = x_ref.shape
    width = resid_ref.shape[1]
    half = width // 2
    scan = channels // 2
    groups = length // GROUP
    nst = alog_ref.shape[0]
    flat = GROUP * nst
    tiles = wgu.shape[1] // 256
    after = lax.rem(s + 1, seqs)
    ahead = lax.rem(s + seqs - 1, seqs)
    count = [0]
    everything = []

    def to(src, dst, seq, exp):
        index = count[0]
        count[0] += 1
        copy = pltpu.make_async_remote_copy(
            src_ref=src,
            dst_ref=dst,
            send_sem=sems.at[0, index],
            recv_sem=sems.at[1, index],
            device_id=(seq, exp),
            device_id_type=MESH,
        )
        everything.append(copy)
        return copy

    first = [
        pltpu.make_async_copy(x_hbm, x_ref, w_sem.at[6 + 2 * tiles]),
        pltpu.make_async_copy(z_hbm, z_ref, w_sem.at[7 + 2 * tiles]),
        pltpu.make_async_copy(dt_hbm, dt_ref, w_sem.at[8 + 2 * tiles]),
        pltpu.make_async_copy(ow_hbm, ow, w_sem.at[0]),
        pltpu.make_async_copy(gm_hbm, gm, w_sem.at[1]),
    ]
    for load in first:
        load.start()
    loads = []
    for t in range(tiles):
        for k, w_hbm in enumerate((wg_hbm, wu_hbm)):
            loads.append(
                pltpu.make_async_copy(
                    w_hbm.at[0, :, pl.ds(t * 128, 128)],
                    wgu.at[:, pl.ds(t * 256 + k * 128, 128)],
                    w_sem.at[2 + 2 * t + k],
                )
            )
    loads.append(pltpu.make_async_copy(wd_hbm.at[0], wd, w_sem.at[2 + 2 * tiles]))

    zs = [lax.rem(z + d, ways) for d in range(ways)]
    zb = [lax.rem(z + ways - d, ways) for d in range(ways)]

    barrier = pltpu.get_barrier_semaphore()
    partners = [(sib, z), (ax, z), (ay, z), (diag, z), (after, z), (ahead, z)]
    partners += [(s, zs[1]), (s, zs[2]), (s, zs[3])]
    for seq, exp in partners:
        pl.semaphore_signal(barrier, inc=1, device_id=(seq, exp), device_id_type=MESH)
    pl.semaphore_wait(barrier, len(partners))

    first[0].wait()
    halo = to(x_ref.at[pl.ds(length - GROUP, GROUP), :], xhalo, after, z)
    halo.start()

    for k, spread in enumerate((b_wide, c_wide)):
        value = bc_ref[k]
        for t in range(length):
            spread[t] = jnp.broadcast_to(value[:, t : t + 1], (nst, LANES))
    lane = lax.broadcasted_iota(jnp.int32, (length, flat), 1)
    row = lax.broadcasted_iota(jnp.int32, (length, flat), 0)
    same_token = lax.div(lane, nst) == lax.rem(row, GROUP)
    lane_r = lax.broadcasted_iota(jnp.int32, (nst, flat), 1)
    row_r = lax.broadcasted_iota(jnp.int32, (nst, flat), 0)
    unit = (lax.rem(lane_r, nst) == row_r).astype(f32)
    repeat = unit.astype(bf16)
    for k, block_ref in enumerate((b_block, c_block)):
        by_token = jnp.transpose(bc_ref[k]).astype(bf16)
        laid = jnp.dot(by_token, repeat, preferred_element_type=f32)
        block_ref[...] = jnp.where(same_token, laid, 0.0).astype(bf16)
    diagonal = same_token[:GROUP].astype(f32)
    ones_block = diagonal.astype(bf16)
    rate_buf[...] = -jnp.exp(alog_ref[...])

    for load in first[1:]:
        load.wait()

    def mix_tile(t, _):
        at = pl.ds(pl.multiple_of(t * 256, 256), 256)
        zfac_buf[:, :, at] = transposed(gm[...], ow[at, :]).reshape(groups, GROUP, 256)
        return 0

    lax.fori_loop(0, channels // 256, mix_tile, 0, unroll=True)
    for load in loads:
        load.start()
    xpad[8 : 8 + length, :] = x_ref[...].astype(f32)
    halo.wait_recv()
    xpad[0:8, :] = jnp.where(s > 0, xhalo[...].astype(f32)[GROUP - 8 :], 0.0)

    def prepare(t, _):
        at = pl.ds(pl.multiple_of(t * LANES, LANES), LANES)

        def put(ref, value):
            ref[:, :, at] = value.reshape(groups, GROUP, LANES)

        pre = bias_ref[:, at] + conv_ref[0:1, at] * xpad[5 : 5 + length, at]
        for tap in range(1, KW):
            pre = pre + conv_ref[tap : tap + 1, at] * xpad[5 + tap : 5 + tap + length, at]
        conv_sig = jax.nn.sigmoid(pre)
        conv_out = pre * conv_sig
        put(conv_buf, conv_out)
        put(dsilu_buf, conv_sig * (1.0 + pre * (1.0 - conv_sig)))
        raw = dt_ref[:, at] + dtb_ref[:, at]
        step = jnp.maximum(raw, 0.0) + jnp.log1p(jnp.exp(-jnp.abs(raw)))
        put(step_buf, step)
        put(drive_buf, step * conv_out)
        put(dtsig_buf, jax.nn.sigmoid(raw))
        z_val = z_ref[:, at].astype(f32)
        z_sig = jax.nn.sigmoid(z_val)
        mixed = zfac_buf[:, :, at].reshape(length, LANES)
        gate = z_val * z_sig
        put(zgate_buf, gate)
        put(grad_buf, mixed * gate)
        put(zfac_buf, mixed * z_sig * (1.0 + z_val * (1.0 - z_sig)))
        return 0

    lax.fori_loop(0, channels // LANES, prepare, 0)

    def lanes(k):
        return pl.ds(k * scan, scan)

    def totals(k, low, high, carry):
        at = lanes(k)
        rate = rate_buf[:, at]

        def advance(i, carry):
            state, passed, leaving = carry
            for j in range(GROUP):
                decay = jnp.exp(step_buf[i, j : j + 1, at] * rate)
                decays[i * GROUP + j, :, at] = decay
                state = decay * state + drive_buf[i, j : j + 1, at] * wide(
                    b_wide[i * GROUP + j], scan
                )
                passed = passed * decay
                leaving = leaving + passed * (
                    grad_buf[i, j : j + 1, at] * wide(c_wide[i * GROUP + j], scan)
                )
            return (state, passed, leaving)

        return lax.fori_loop(low, high, advance, carry)

    zero = jnp.zeros((nst, scan), f32)
    nothing = (zero, jnp.ones_like(zero), zero)

    def keep(k, carry):
        for m in range(3):
            tot[k, m] = carry[m].astype(bf16)

    beside = [to(tot.at[k], tsib.at[k], sib, z) for k in range(2)]
    xbit, ybit = lax.rem(lax.div(s, 2), 2), lax.div(s, 4)
    beyond = []
    for k in range(2):
        for m, (seq, bit) in enumerate(((ax, xbit), (ay, ybit), (diag, ybit))):
            at = pl.ds(bit, 2)
            beyond.append(to(tpair.at[k, at], trecv.at[k, m, at], seq, z))

    def join(k):
        beside[k].wait_recv()
        own = [tot[k, m].astype(f32) for m in range(3)]
        their = [tsib[k, m].astype(f32) for m in range(3)]
        one = [jnp.where(core == 0, a, b) for a, b in zip(own, their)]
        two = [jnp.where(core == 0, b, a) for a, b in zip(own, their)]
        tpair[k, 0] = (two[1] * one[0] + two[0]).astype(bf16)
        tpair[k, 1] = (one[1] * two[1]).astype(bf16)
        tpair[k, 2] = (one[2] + one[1] * two[2]).astype(bf16)
        for copy in beyond[3 * k : 3 * k + 3]:
            copy.start()

    def enter(k):
        for copy in beyond[3 * k : 3 * k + 3]:
            copy.wait_recv()
        chip = lax.div(s, 2)
        start, arriving = zero, zero

        def other_chip(c):
            relation = (c % 2 + xbit - 2 * (c % 2) * xbit) + 2 * (c // 2 + ybit - 2 * (c // 2) * ybit)
            return trecv.at[k, jnp.maximum(relation - 1, 0)]

        for c in range(4):
            at = other_chip(c)
            start = jnp.where(c < chip, at[1].astype(f32) * start + at[0].astype(f32), start)
            at = other_chip(3 - c)
            arriving = jnp.where(
                3 - c > chip, at[1].astype(f32) * arriving + at[2].astype(f32), arriving
            )
        passed = tsib[k, 1].astype(f32)
        start = jnp.where(core == 1, passed * start + tsib[k, 0].astype(f32), start)
        arriving = jnp.where(core == 0, passed * arriving + tsib[k, 2].astype(f32), arriving)
        start_buf[:, lanes(k)] = start
        arrive_buf[:, lanes(k)] = arriving

    keep(0, totals(0, 0, groups, nothing))
    beside[0].start()
    middle = totals(1, 0, groups // 2, nothing)
    join(0)
    keep(1, totals(1, groups // 2, groups, middle))
    beside[1].start()
    join(1)

    def state_rows(at, number):
        return pl.ds(pl.multiple_of(at * nst, nst), number * nst)

    def forward(k):
        at = lanes(k)
        states[0:nst, at] = start_buf[:, at].astype(bf16)

        def advance(i, state):
            for j in range(GROUP):
                t = i * GROUP + j
                state = decays[t, :, at] * state + drive_buf[i, j : j + 1, at] * wide(
                    b_wide[t], scan
                )
                states[state_rows(t + 1, 1), at] = state.astype(bf16)
            here = pl.ds(pl.multiple_of(i * GROUP, GROUP), GROUP)
            y_val = jnp.dot(
                c_block[here, :],
                states[state_rows(i * GROUP + 1, GROUP), at],
                preferred_element_type=f32,
            )
            y_val = y_val + gain_ref[:, at] * conv_buf[i, :, at]
            gz_buf[here, at] = zfac_buf[i, :, at] * y_val
            gated[here, at] = (zgate_buf[i, :, at] * y_val).astype(bf16)
            return state

        lax.fori_loop(0, groups, advance, start_buf[:, at])

    for k in range(2):
        enter(k)
        forward(k)

    written = [
        pltpu.make_async_copy(gz_buf, gz_ref, w_sem.at[3 + 2 * tiles]),
        pltpu.make_async_copy(gdt_buf, gdt_ref, w_sem.at[4 + 2 * tiles]),
        pltpu.make_async_copy(gx_buf, gx_ref, w_sem.at[5 + 2 * tiles]),
    ]
    written[0].start()

    waves = 2
    piece = rows // waves
    pack = ways * piece

    def block(seq, exp, w):
        at = (w * seqs + seq) * pack + exp * piece
        return pl.ds(pl.multiple_of(at, piece), piece)

    def within(exp, w):
        return pl.ds(pl.multiple_of(exp * rows + w * piece, piece), piece)

    def project(t, _):
        at = pl.ds(pl.multiple_of(t * 256, 256), 256)
        p_buf[:, at] = jnp.dot(gated[...], ow[:, at], preferred_element_type=f32).astype(bf16)
        return 0

    lax.fori_loop(0, width // 256, project, 0, unroll=True)

    z_out = [
        [to(p_buf.at[within(zs[d], w)], zrecv.at[w, d - 1], s, zs[d]) for d in (1, 2, 3)]
        for w in range(waves)
    ]
    for copy in z_out[0]:
        copy.start()

    gb_acc[...] = jnp.zeros_like(gb_acc)
    gc_acc[...] = jnp.zeros_like(gc_acc)

    def backward(k):
        at = lanes(k)

        def retreat(n, carry):
            flow, alog_sum = carry
            i = groups - 1 - n
            for j in reversed(range(GROUP)):
                t = i * GROUP + j
                adjoint = wide(c_wide[t], scan) * grad_buf[i, j : j + 1, at] + flow
                adj[j * nst : (j + 1) * nst, :] = adjoint.astype(bf16)
                flow = decays[t, :, at] * adjoint
                share = rate_buf[:, at] * (flow * states[state_rows(t, 1), at].astype(f32))
                alog_sum = alog_sum + step_buf[i, j : j + 1, at] * share
                quo[j * nst : (j + 1) * nst, :] = share.astype(bf16)
            here = pl.ds(pl.multiple_of(i * GROUP, GROUP), GROUP)
            into_buf[i, :, at] = jnp.dot(b_block[here, :], adj[...], preferred_element_type=f32)
            qsum_buf[i, :, at] = jnp.dot(ones_block, quo[...], preferred_element_type=f32)
            gb_acc[i] += transposed(drive_buf[i, :, at].astype(bf16), adj[...])
            gc_acc[i] += transposed(
                grad_buf[i, :, at].astype(bf16), states[state_rows(i * GROUP + 1, GROUP), at]
            )
            return (flow, alog_sum)

        _, alog_sum = lax.fori_loop(0, groups, retreat, (arrive_buf[:, at], zero))
        sums_own[0:nst, at] = alog_sum

    gather, to_x, to_y, to_b, forward = [], [], [], [], []
    for w in range(waves):
        here = rows_all.at[block(s, z, w)]
        gather.append([to(here, here, s, zs[d]) for d in (1, 2, 3)])
        blocks = [rows_all.at[block(s, zb[d], w)] for d in range(ways)]
        to_x.append([to(at, at, ax, z) for at in blocks])
        to_y.append([to(at, at, ay, z) for at in blocks])
        to_b.append([to(at, at, sib, z) for at in blocks])
        passing = []
        for d in range(ways):
            origin, target = (ay, ax) if d < 2 else (ax, ay)
            at = rows_all.at[block(origin, zb[d], w)]
            passing.append(to(at, at, target, z))
        forward.append(passing)

    def mixed_rows(w):
        for copy in z_out[w]:
            copy.wait_recv()
        own = pl.ds(w * piece, piece)
        total = resid_ref[own, :].astype(f32) + p_buf[within(z, w), :].astype(f32)
        for d in range(3):
            total = total + zrecv[w, d].astype(f32)
        own_h[own, :] = total.astype(bf16)
        rows_all[block(s, z, w), :] = total.astype(bf16)
        for copy in gather[w] + [to_x[w][0], to_y[w][0], to_b[w][0]]:
            copy.start()

    def spread_rows(w):
        for d in (1, 2, 3):
            gather[w][d - 1].wait_recv()
            to_x[w][d].start()
            to_y[w][d].start()
            to_b[w][d].start()

    backward(0)
    for copy in z_out[1]:
        copy.start()
    mixed_rows(0)
    backward(1)
    for k, held in enumerate((gb_acc, gc_acc)):
        kept = jnp.where(same_token, held[...].reshape(length, flat), 0.0)
        bc_own[k] = lax.dot_general(
            unit,
            kept,
            (((1,), (1,)), ((), ())),
            precision=lax.Precision.HIGHEST,
            preferred_element_type=f32,
        )
    bc_copies = [to(bc_own, bc_recv.at[d - 1], s, zs[d]) for d in (1, 2, 3)]
    for copy in bc_copies:
        copy.start()

    def finish(t, _):
        at = pl.ds(pl.multiple_of(t * LANES, LANES), LANES)

        def get(ref):
            return ref[:, :, at].reshape(length, LANES)

        def total(value):
            return jnp.sum(value, axis=0, keepdims=True)

        into, conv_out, grad_y = get(into_buf), get(conv_buf), get(grad_buf)
        grad_dt = (get(qsum_buf) + conv_out * into) * get(dtsig_buf)
        gdt_buf[:, at] = grad_dt
        grad_pre = (gain_ref[:, at] * grad_y + get(step_buf) * into) * get(dsilu_buf)
        gpad[0:length, at] = grad_pre
        for tap in range(KW):
            sums_own[nst + tap : nst + tap + 1, at] = total(
                grad_pre * xpad[5 + tap : 5 + tap + length, at]
            )
        sums_own[nst + KW : nst + KW + 1, at] = total(grad_pre)
        sums_own[nst + KW + 1 : nst + KW + 2, at] = total(grad_y * conv_out)
        sums_own[nst + KW + 2 : nst + KW + 3, at] = total(grad_dt)
        return 0

    lax.fori_loop(0, channels // LANES, finish, 0)
    written[1].start()
    sums_own[nst + KW + 3 :, :] = jnp.zeros_like(sums_own[nst + KW + 3 :, :])
    rim = to(gpad.at[pl.ds(0, 8)], ghalo, ahead, z)
    rim.start()
    sums_copies = [
        to(sums_own, sums_recv.at[0], sib, z),
        to(sums_acc.at[0], sums_recv.at[1], ax, z),
        to(sums_acc.at[1], sums_recv.at[2], ay, z),
    ]
    sums_copies[0].start()
    mixed_rows(1)
    sums_copies[0].wait_recv()
    sums_acc[0] = sums_own[...] + sums_recv[0]
    sums_copies[1].start()
    spread_rows(0)
    rim.wait_recv()
    gpad[length : length + 8, :] = jnp.where(s < seqs - 1, ghalo[...], 0.0)

    def spread_back(t, _):
        at = pl.ds(pl.multiple_of(t * LANES, LANES), LANES)
        grad_x = conv_ref[KW - 1 : KW, at] * gpad[0:length, at]
        for tap in range(KW - 1):
            away = KW - 1 - tap
            grad_x = grad_x + conv_ref[tap : tap + 1, at] * gpad[away : away + length, at]
        gx_buf[:, at] = grad_x
        return 0

    lax.fori_loop(0, channels // LANES, spread_back, 0)
    written[2].start()
    to_y[0][0].wait_recv()
    forward[0][0].start()

    sums_copies[1].wait_recv()
    sums_acc[1] = sums_acc[0] + sums_recv[1]
    sums_copies[2].start()

    for copy in bc_copies:
        copy.wait_recv()
    bc_out[...] = (bc_own[...] + bc_recv[0]) + (bc_recv[1] + bc_recv[2])

    def up(w, seq):
        first_row = (w * seqs + 4 * lax.div(seq, 4)) * pack
        at = pl.ds(pl.multiple_of(first_row, 4 * pack), 4 * pack)

        def tile(t, _):
            both = jnp.dot(
                rows_all[at, :],
                wgu[:, pl.ds(pl.multiple_of(t * 256, 256), 256)],
                preferred_element_type=f32,
            )
            gate, upper = both[:, :128], both[:, 128:]
            value = gate * jax.nn.sigmoid(gate) * upper
            hidden[:, pl.ds(pl.multiple_of(t * 128, 128), 128)] = value.astype(bf16)
            return 0

        lax.fori_loop(0, tiles, tile, 0, unroll=True)

    quarter = width // 4
    order = (0, 2, 1, 3)

    def cols(h):
        return pl.ds(h * quarter, quarter)

    def small(h):
        return pl.ds((h % 2) * quarter, quarter)

    def part_rows(r, of_core):
        side = xbit if r % 2 == 0 else 1 - xbit
        return pl.ds(pl.multiple_of((2 * side + of_core) * pack, pack), pack)

    pair = {}

    def down(w, r0, h):
        g = 2 * w + r0 // 2
        part[g, :, cols(h)] = jnp.dot(
            hidden[...], wd[:, cols(h)], preferred_element_type=f32
        ).astype(bf16)
        for r in (r0, r0 + 1):
            copy = to(
                part.at[g, part_rows(r, 1 - core), cols(h)], psib.at[w, r, :, cols(h)], sib, z
            )
            copy.start()
            pair[w, r, h] = copy

    def paired(w, r, h):
        pair[w, r, h].wait_recv()
        acc[w, r, :, cols(h)] = (
            part[2 * w + r // 2, part_rows(r, core), cols(h)].astype(f32)
            + psib[w, r, :, cols(h)].astype(f32)
        ).astype(bf16)

    def pack_of(seq, w):
        at = (w * seqs + seq) * pack
        return rows_all.at[pl.ds(pl.multiple_of(at, pack), pack)]

    share_out = [[to(pack_of(o, w), pack_of(o, w), sib, z) for o in (ax, ay, diag)] for w in range(waves)]
    send = {}

    def reduce_out(name, src, dst, seq):
        copy = to(src, dst, seq, z)
        copy.start()
        send[name] = copy

    def to_across_x(w, h):
        reduce_out(("x", w, h), acc.at[w, 1, :, cols(h)], rx.at[w, :, cols(h)], ax)

    def to_across_y(w, h):
        reduce_out(("y", w, h), acc.at[w, 2, :, cols(h)], ry.at[w, :, cols(h)], ay)

    def near(w):
        to_x[w][0].wait_recv()
        to_x[w][1].wait_recv()
        to_y[w][1].wait_recv()
        forward[w][1].start()
        to_x[w][2].wait_recv()
        forward[w][2].start()
        to_x[w][3].wait_recv()
        forward[w][3].start()
        share_out[w][0].start()
        to_y[w][2].wait_recv()
        to_y[w][3].wait_recv()
        share_out[w][1].start()

    def near_ready(w):
        for copy in to_b[w]:
            copy.wait_recv()
        share_out[w][0].wait_recv()

    def far(w):
        for copy in forward[w]:
            copy.wait_recv()
        share_out[w][2].start()

    def far_ready(w):
        share_out[w][1].wait_recv()
        share_out[w][2].wait_recv()

    def diagonal_out(w, h):
        paired(w, 3, h)
        if h < 2:
            reduce_out(("d", w, h), acc.at[w, 3, :, cols(h)], rdx.at[w, :, small(h)], ax)
        else:
            reduce_out(("d", w, h), acc.at[w, 3, :, cols(h)], rdy.at[w, :, small(h)], ay)

    def direct_x(w):
        for h in (0, 1):
            paired(w, 1, h)
            to_across_x(w, h)
        for h in (2, 3):
            paired(w, 1, h)

    def direct_y(w):
        for h in (2, 3):
            paired(w, 2, h)
            to_across_y(w, h)
        for h in (0, 1):
            paired(w, 2, h)
        for h in range(4):
            paired(w, 0, h)

    def joined(w):
        for h in order:
            send["d", w, h].wait_recv()
            r, got = (2, rdx) if h < 2 else (1, rdy)
            acc[w, r, :, cols(h)] = (
                acc[w, r, :, cols(h)].astype(f32) + got[w, :, small(h)].astype(f32)
            ).astype(bf16)
            if h < 2:
                to_across_y(w, h)
            else:
                to_across_x(w, h)

    back = {}

    def reduced(w, h):
        send["x", w, h].wait_recv()
        send["y", w, h].wait_recv()
        total = (
            acc[w, 0, :, cols(h)].astype(f32)
            + rx[w, :, cols(h)].astype(f32)
            + ry[w, :, cols(h)].astype(f32)
        ).astype(bf16)
        fin[w, :, cols(h)] = total
        for d in (1, 2, 3):
            at = pl.ds(pl.multiple_of(zs[d] * piece, piece), piece)
            copy = to(fin.at[w, at, cols(h)], zfin.at[w, d - 1, :, cols(h)], s, zs[d])
            copy.start()
            back[w, h, d] = copy

    eye = lax.broadcasted_iota(jnp.int32, (rows, rows), 0) == lax.broadcasted_iota(
        jnp.int32, (rows, rows), 1
    )

    def column(row):
        return jnp.sum(jnp.where(eye, row, 0.0), axis=1, keepdims=True)

    shares = []
    for d in range(ways):
        mine = [
            jnp.where(ids_ref[k : k + 1, :] == zb[d], weight_ref[k : k + 1, :], 0.0) for k in range(2)
        ]
        shares.append(column(mine[0] + mine[1]))

    def result(w, h):
        own = pl.ds(w * piece, piece)
        at = pl.ds(pl.multiple_of(z * piece, piece), piece)
        total = own_h[own, cols(h)].astype(f32)
        total = total + shares[0][w * piece : (w + 1) * piece] * fin[w, at, cols(h)].astype(f32)
        for d in (1, 2, 3):
            back[w, h, d].wait_recv()
            total = total + shares[d][w * piece : (w + 1) * piece] * zfin[
                w, d - 1, :, cols(h)
            ].astype(f32)
        out_ref[own, cols(h)] = total.astype(bf16)

    near(0)
    spread_rows(1)
    near_ready(0)
    for load in loads:
        load.wait()
    to_y[1][0].wait_recv()
    forward[1][0].start()
    up(0, s)
    far(0)
    for h in range(4):
        down(0, 0, h)
    far_ready(0)
    up(0, ay)
    near(1)
    for h in order:
        down(0, 2, h)
    for h in order:
        diagonal_out(0, h)
    near_ready(1)
    direct_x(0)
    direct_y(0)
    up(1, s)
    far(1)
    for h in range(4):
        down(1, 0, h)
    joined(0)
    direct_x(1)
    far_ready(1)
    up(1, ay)
    for h in order:
        reduced(0, h)
    down(1, 2, 0)
    down(1, 2, 2)
    diagonal_out(1, 0)
    down(1, 2, 1)
    diagonal_out(1, 2)
    down(1, 2, 3)
    diagonal_out(1, 1)
    diagonal_out(1, 3)
    direct_y(1)

    sums_copies[2].wait_recv()
    summed = sums_acc[1] + sums_recv[2]
    alog_out[...] = summed[:nst]
    taps_out[...] = summed[nst : nst + KW]
    chan_out[...] = summed[nst + KW : nst + KW + 3]

    for h in order:
        result(0, h)
    joined(1)
    for h in order:
        reduced(1, h)
    for h in order:
        result(1, h)
    for copy in written:
        copy.wait()
    for copy in everything:
        copy.wait_send()


def deliver_kernel(number, *refs):
    given, results, stops, sem = (
        refs[:number],
        refs[number : 2 * number],
        refs[2 * number : 3 * number],
        refs[3 * number],
    )
    fetch = [pltpu.make_async_copy(given[k], stops[k], sem.at[0, k]) for k in range(number)]
    store = [pltpu.make_async_copy(stops[k], results[k], sem.at[1, k]) for k in range(number)]
    for copy in fetch:
        copy.start()
    for k in range(number):
        fetch[k].wait()
        store[k].start()
    for copy in store:
        copy.wait()


def deliver(arrays):
    number = len(arrays)
    anywhere = pl.BlockSpec(memory_space=pl.ANY)
    return pl.pallas_call(
        functools.partial(deliver_kernel, number),
        out_shape=[jax.ShapeDtypeStruct(a.shape, a.dtype) for a in arrays],
        in_specs=[anywhere] * number,
        out_specs=[anywhere] * number,
        scratch_shapes=[pltpu.VMEM(a.shape, a.dtype) for a in arrays]
        + [pltpu.SemaphoreType.DMA((2, number))],
        name="deliver",
    )(*arrays)


def layer(
    x_in,
    z_in,
    dt_raw,
    bc_in,
    a_log,
    taps,
    bias,
    gain,
    dt_bias,
    resid,
    route_ids,
    route_weight,
    out_weight,
    grad_mix,
    w_gate,
    w_up,
    w_down,
):
    rows, width = resid.shape
    length, channels = x_in.shape
    states = a_log.shape[0]
    units = w_gate.shape[2]
    tiles = units // 128
    seqs = lax.axis_size("seq")
    half, scan, groups = width // 2, channels // 2, length // GROUP
    bf16, f32 = jnp.bfloat16, jnp.float32
    vmem = pl.BlockSpec(memory_space=pltpu.VMEM)
    hbm = pl.BlockSpec(memory_space=pl.ANY)
    sem = pltpu.SemaphoreType.DMA
    flat = GROUP * states

    def held(*shape, kind=f32):
        return pltpu.VMEM(shape, kind)

    def rows_of():
        return held(groups, GROUP, channels)

    summed = (states + 8, channels)
    grads = (2, states, length)
    return pl.pallas_call(
        layer_kernel,
        out_shape=[
            jax.ShapeDtypeStruct((rows, width), bf16),
            jax.ShapeDtypeStruct((length, channels), f32),
            jax.ShapeDtypeStruct((length, channels), f32),
            jax.ShapeDtypeStruct((length, channels), f32),
            jax.ShapeDtypeStruct((states, channels), f32),
            jax.ShapeDtypeStruct((KW, channels), f32),
            jax.ShapeDtypeStruct((3, channels), f32),
            jax.ShapeDtypeStruct(grads, f32),
        ],
        in_specs=[hbm] * 3 + [vmem] * 9 + [hbm] * 5,
        out_specs=[vmem] + [hbm] * 3 + [vmem] * 4,
        scratch_shapes=[
            held(length, channels),
            held(length, channels),
            held(length, channels),
            held(length, channels, kind=bf16),
            held(length, channels, kind=bf16),
            held(length, channels),
            held(seqs * length, width, kind=bf16),
            held(width, 2 * units, kind=bf16),
            held(units, width, kind=bf16),
            held(channels, width, kind=bf16),
            held(length, width, kind=bf16),
            held(2 * length, units, kind=bf16),
            held(rows, width, kind=bf16),
            held(2, 3, rows // 2, width, kind=bf16),
            held(2, 3, rows // 2, width, kind=bf16),
            held(4, 2 * length, width, kind=bf16),
            held(2, 4, length // 2, width, kind=bf16),
            held(2, 4, length // 2, width, kind=bf16),
            held(2, length // 2, width, kind=bf16),
            held(2, length // 2, width, kind=bf16),
            held(2, length // 2, half, kind=bf16),
            held(2, length // 2, half, kind=bf16),
            held(2, length // 2, width, kind=bf16),
            held(length, width, kind=bf16),
            held(*summed),
            held(3, *summed),
            held(2, *summed),
            held(*grads),
            held(3, *grads),
            held(length, states, channels),
            held((length + 1) * states, channels, kind=bf16),
            held(length, states, LANES),
            held(length, states, LANES),
            held(length, flat, kind=bf16),
            held(length, flat, kind=bf16),
        ]
        + [rows_of() for _ in range(10)]
        + [
            held(length + 8, channels),
            held(length + 8, channels),
            held(GROUP, channels, kind=bf16),
            held(8, channels),
            held(length, channels, kind=bf16),
            held(flat, scan, kind=bf16),
            held(flat, scan, kind=bf16),
            held(groups, GROUP, flat),
            held(groups, GROUP, flat),
            held(2, 3, states, scan, kind=bf16),
            held(2, 3, states, scan, kind=bf16),
            held(2, 3, states, scan, kind=bf16),
            held(2, 3, 3, states, scan, kind=bf16),
            held(states, channels),
            held(states, channels),
            held(states, channels),
            sem((2 * tiles + 9,)),
            sem((2, 192)),
        ],
        compiler_params=pltpu.CompilerParams(
            collective_id=0, has_side_effects=True, vmem_limit_bytes=60 << 20
        ),
        cost_estimate=pl.CostEstimate(
            flops=6 * seqs * length * width * units + 4 * length * width * channels,
            bytes_accessed=6 * width * units,
            transcendentals=seqs * length * units + length * channels * states,
        ),
        name="layer",
    )(
        x_in,
        z_in,
        dt_raw,
        bc_in,
        a_log,
        taps,
        bias.reshape(1, channels),
        gain.reshape(1, channels),
        dt_bias.reshape(1, channels),
        resid,
        route_ids.T,
        route_weight.T,
        out_weight,
        grad_mix,
        w_gate,
        w_up,
        w_down,
    )


def entering(everything):
    peers, here = everything.shape[0], lax.axis_index("seq")
    values = everything.astype(jnp.float32)
    start = jnp.zeros_like(values[0, 0])
    arriving = jnp.zeros_like(start)
    for k in range(peers):
        start = jnp.where(k < here, values[k, 0] * start + values[k, 1], start)
        back = peers - 1 - k
        arriving = jnp.where(back > here, values[back, 0] * arriving + values[back, 2], arriving)
    return start, arriving


def routed_experts(partial_value, resid, w_gate, w_up, w_down, route_ids, route_weight):
    rows = resid.shape[0]
    mixed = lax.psum(partial_value, "expert").astype(jnp.float32)
    own = lax.dynamic_slice_in_dim(mixed, lax.axis_index("expert") * rows, rows, 0)
    hidden_in = (resid.astype(jnp.float32) + own).astype(jnp.bfloat16)
    experts = lax.axis_size("expert")
    capacity = 4 * rows // experts
    flat_ids = route_ids.reshape(-1)
    order = jnp.arange(flat_ids.shape[0], dtype=jnp.int32)
    earlier = (flat_ids[:, None] == flat_ids[None, :]) & (order[None, :] < order[:, None])
    rank = jnp.sum(earlier.astype(jnp.int32), axis=1)
    slot = flat_ids * capacity + rank
    placing = (jnp.arange(experts * capacity, dtype=jnp.int32)[:, None] == slot[None, :]).astype(
        jnp.bfloat16
    )
    doubled = jnp.repeat(hidden_in, 2, axis=0)
    outgoing = jnp.dot(placing, doubled, preferred_element_type=jnp.float32).astype(jnp.bfloat16)
    incoming = lax.all_to_all(outgoing, "expert", split_axis=0, concat_axis=0, tiled=True)
    piece = lax.all_gather(incoming, "seq", axis=0, tiled=True)
    gate = jnp.dot(piece, w_gate[0], preferred_element_type=jnp.float32)
    upper = jnp.dot(piece, w_up[0], preferred_element_type=jnp.float32)
    hidden = (jax.nn.silu(gate) * upper).astype(jnp.bfloat16)
    expert_sum = lax.psum_scatter(
        jnp.dot(hidden, w_down[0], preferred_element_type=jnp.float32).astype(jnp.bfloat16),
        "seq",
        scatter_dimension=0,
        tiled=True,
    )
    returned = lax.all_to_all(expert_sum, "expert", split_axis=0, concat_axis=0, tiled=True)
    picked = lax.dot_general(
        placing, returned, (((0,), (0,)), ((), ())), preferred_element_type=jnp.float32
    )
    picked = picked.reshape(rows, 2, -1)
    moe = picked[:, 0] * route_weight[:, 0:1] + picked[:, 1] * route_weight[:, 1:2]
    return (hidden_in.astype(jnp.float32) + moe).astype(jnp.bfloat16)


def local(
    x_in,
    z_in,
    dt_raw,
    bc_in,
    a_log,
    conv_weight,
    conv_bias,
    skip_gain,
    dt_bias,
    out_weight,
    resid,
    w_gate,
    w_up,
    w_down,
    route_ids,
    route_weight,
    grad_mix,
):
    length, channels = x_in.shape
    states = a_log.shape[0]
    rim = KW - 1
    rows = resid.shape[0]
    experts = lax.axis_size("expert")
    if experts == 4 and lax.axis_size("seq") == 8:
        layer_out, grad_x, grad_z, grad_dt, grad_alog, grad_conv, grad_chan, grad_bc = deliver(
            layer(
                x_in,
                z_in,
                dt_raw,
                bc_in,
                a_log,
                conv_weight,
                conv_bias,
                skip_gain,
                dt_bias,
                resid,
                route_ids,
                route_weight,
                out_weight,
                grad_mix,
                w_gate,
                w_up,
                w_down,
            )
        )
        return (layer_out, grad_x, grad_z, grad_dt, grad_bc, grad_alog, grad_conv, grad_chan)
    x_val = x_in.astype(jnp.float32)
    z_val = z_in.astype(jnp.float32)
    before = shifted(x_in[length - rim :], "seq", 1)
    padded = jnp.concatenate([before.astype(jnp.float32), x_val], axis=0)
    pre = conv_bias[None, :] + conv_weight[0][None, :] * padded[0:length]
    for tap in range(1, KW):
        pre = pre + conv_weight[tap][None, :] * padded[tap : tap + length]
    conv_sig = jax.nn.sigmoid(pre)
    conv_out = pre * conv_sig
    step = jax.nn.softplus(dt_raw + dt_bias[None, :])
    rate = -jnp.exp(a_log)
    drive = step * conv_out
    z_sig = jax.nn.sigmoid(z_val)
    back_mix = lax.dot_general(
        grad_mix, out_weight, (((1,), (1,)), ((), ())), preferred_element_type=jnp.float32
    )
    grad_y = back_mix * z_val * z_sig

    def grouped(array):
        return array.reshape(length // SUB, SUB, channels)

    def flat(array):
        return array.reshape(length, channels)

    spread = jnp.broadcast_to(
        bc_in.transpose(0, 2, 1)[:, :, :, None], (2, length, states, LANES)
    ).reshape(2, length // SUB, SUB, states, LANES)
    b_wide, c_wide = spread[0], spread[1]
    totals, forward, backward = sweeps(length, channels, states)
    step_g, drive_g, grad_g, conv_g = (grouped(a) for a in (step, drive, grad_y, conv_out))
    own_totals = totals(step_g, drive_g, grad_g, b_wide, c_wide, rate)
    start, arriving = entering(lax.all_gather(own_totals, "seq"))
    y_val = flat(forward(step_g, drive_g, b_wide, c_wide, rate, start))
    y_val = y_val + skip_gain[None, :] * conv_out
    gated = (y_val * z_val * z_sig).astype(jnp.bfloat16)
    partial_value = jnp.dot(gated, out_weight, preferred_element_type=jnp.float32)
    grad_z = back_mix * y_val * z_sig * (1.0 + z_val * (1.0 - z_sig))
    grad_step, conv_part_grad, grad_b, grad_c, grad_alog_local = backward(
        step_g, drive_g, conv_g, grad_g, b_wide, c_wide, rate, start, arriving
    )
    grad_step, conv_part_grad = flat(grad_step), flat(conv_part_grad)
    grad_conv_out = skip_gain[None, :] * grad_y + conv_part_grad
    grad_skip = jnp.sum(grad_y * conv_out, axis=0)
    grad_dt = grad_step * jax.nn.sigmoid(dt_raw + dt_bias[None, :])
    grad_pre = grad_conv_out * (conv_sig * (1.0 + pre * (1.0 - conv_sig)))
    after = shifted(grad_pre[:rim], "seq", -1)
    grad_pad = jnp.concatenate([grad_pre, after], axis=0)
    grad_x = conv_weight[rim][None, :] * grad_pad[0:length]
    for tap in range(rim):
        grad_x = grad_x + conv_weight[tap][None, :] * grad_pad[rim - tap : rim - tap + length]
    grad_taps = jnp.stack(
        [jnp.sum(grad_pre * padded[tap : tap + length], axis=0) for tap in range(KW)]
    )
    channel_grads = jnp.stack([jnp.sum(grad_pre, axis=0), grad_skip, jnp.sum(grad_dt, axis=0)])
    own_sums = jnp.concatenate([grad_alog_local, grad_taps, channel_grads], axis=0)
    own_bc = jnp.stack([jnp.sum(grad_b, axis=-1), jnp.sum(grad_c, axis=-1)])
    own_bc = own_bc.reshape(2, length, states).transpose(0, 2, 1).reshape(2 * states, length)
    layer_out = routed_experts(
        partial_value.astype(jnp.bfloat16),
        resid,
        w_gate,
        w_up,
        w_down,
        route_ids,
        route_weight,
    )
    sums = lax.psum(own_sums, "seq")
    grad_bc = lax.psum(own_bc, "expert").reshape(2, states, length)
    grad_alog = sums[:states]
    grad_conv = sums[states : states + KW]
    grad_chan = sums[states + KW : states + KW + 3]
    return (layer_out, grad_x, grad_z, grad_dt, grad_bc, grad_alog, grad_conv, grad_chan)


def solution(mesh):
    in_specs = (
        P("seq", "expert"),
        P("seq", "expert"),
        P("seq", "expert"),
        P(None, None, "seq"),
        P(None, "expert"),
        P(None, "expert"),
        P("expert"),
        P("expert"),
        P("expert"),
        P("expert", None),
        P(("seq", "expert"), None),
        P("expert", None, "seq"),
        P("expert", None, "seq"),
        P("expert", "seq", None),
        P(("seq", "expert"), None),
        P(("seq", "expert"), None),
        P("seq", None),
    )
    out_specs = (
        P(("seq", "expert"), None),
        P("seq", "expert"),
        P("seq", "expert"),
        P("seq", "expert"),
        P(None, None, "seq"),
        P(None, "expert"),
        P(None, "expert"),
        P(None, "expert"),
    )
    return jax.shard_map(local, mesh=mesh, in_specs=in_specs, out_specs=out_specs, check_vma=False)
```
